128 devices in a mesh: slab: 32 (over y, x_hi, z), patch: 4 (over x_lo, core).
Axes of the slice: x: 4 (x_hi: 2, x_lo: 2; x = x_hi * 2 + x_lo), y: 4, z: 4, core: 2. Of those that a mesh axis runs over, the one named last changes fastest.
Arguments:
- fluid_state: float32 [64, 256, 256], P('slab', 'patch'), may hold values from -6 to 6
- fluid_rhs: float32 [64, 256, 256], P('slab', 'patch'), may hold values from -24 to 24
- element_scale: float32 [64, 256], P('slab', 'patch'), may hold values from 1 to 4
- element_matrix: bfloat16 [256, 256], replicated
- couple_x: bfloat16 [256, 256], replicated, may hold values from -0.09375 to 0.09375
- couple_y: bfloat16 [256, 256], replicated, may hold values from -0.09375 to 0.09375
- block_inverse: bfloat16 [256, 256], replicated
- traction_map: bfloat16 [3, 256], replicated, may hold values from -0.375 to 0.375
- slot_elem: int32 [32, 4, 1024], P('slab', 'patch'), may hold values from 0 to 127
- slot_point: int32 [32, 4, 1024], P('slab', 'patch'), may hold values from 0 to 8191
- slot_count: int32 [32, 4, 4], P('slab', 'patch'), may hold values from 0 to 256, as said below
- displacement: float32 [3, 256, 128], P(None, 'patch'), may hold values from -6 to 6
- stiffness: float32 [256, 128], P('patch'), may hold values from 0.03 to 0.3
Outputs:
- fluid_out: float32 [64, 256, 256], P('slab', 'patch')
- displacement_new: float32 [3, 256, 128], P(None, 'patch')
- wall_motion: float32 [3, 32, 4, 1024], P(None, 'slab', 'patch')
The draws below stay inside these ranges and needn't reach their ends.
Inputs may be any that keep to these rules, and one draw needn't show every extreme that they name: For every block and owner only the first slot_count slots of that owner's 256 slots are live; the count 256 is reached for some block and owner in every draw.
All inputs are finite; a program needn't handle non-finite values.
Results may differ from the reference program's by a relative error of at most 0.0049.
Values may be sent and summed in bfloat16 or wider, within the bound.
No kernel may reach another device: no remote copies, remote signals or barrier semaphores. Data moves between devices by JAX's collectives and lax.ppermute only.
A program may use at most 128 MiB of HBM per device.

```python
import math
import jax
import jax.numpy as jnp

DOF = 256
EX_DEV = 2
EY_DEV = 64
SWEEPS = 3
NU = 64
NV = 128
CAP = 256
QDEV = 1024
NX = 64
NY = 256
NU_ALL = 256
N_SLAB = 32
N_PATCH = 4


def draw_element_matrix(key, part):
    noise = jax.random.normal(jax.random.fold_in(key, 3), (DOF, DOF), jnp.float32)
    return (4.0 * jnp.eye(DOF, dtype=jnp.float32) + noise / jnp.sqrt(DOF * 1.0)).astype(jnp.bfloat16)


def draw_block_inverse(key, part):
    noise = jax.random.normal(jax.random.fold_in(key, 5), (DOF, DOF), jnp.float32)
    return (0.25 * jnp.eye(DOF, dtype=jnp.float32) + 0.1 * noise / jnp.sqrt(DOF * 1.0)).astype(jnp.bfloat16)


def draw_slot_count(key, part):
    first, second = jax.random.split(jax.random.fold_in(key, 11), 2)
    base = jax.random.randint(first, (N_SLAB, N_PATCH, N_PATCH), CAP // 2, CAP + 1)
    slab_rank = jnp.arange(N_SLAB, dtype=jnp.int32)[:, None, None]
    counts = (base * (slab_rank + 1) // N_SLAB).reshape(-1)
    chosen = jax.random.randint(second, (), 0, N_SLAB * N_PATCH * N_PATCH)
    counts = counts.at[chosen].set(CAP)
    return counts.reshape(N_SLAB, N_PATCH, N_PATCH).astype(jnp.int32)


def plant(values, stream_key, least, largest):
    extent = values.shape
    place = [jax.random.randint(jax.random.fold_in(stream_key, axis), (), 0, extent[axis]) for axis in range(len(extent))]
    values = values.at[tuple(place)].set(least)
    longest = extent.index(max(extent))
    place[longest] = (place[longest] + 1) % extent[longest]
    return values.at[tuple(place)].set(largest)


def steps_of(key, extent, pieces, low, largest):
    loudness = 1.0
    for position, shards_of in pieces:
        steps = jax.random.uniform(jax.random.fold_in(jax.random.fold_in(key, 6), position), (shards_of,), jnp.float32, low / len(pieces), largest / len(pieces))
        loudness = loudness * jnp.repeat(jnp.exp(steps), extent[position] // shards_of).reshape((-1,) + (1,) * (len(extent) - 1 - position))
    return loudness


def centred(rng, dims, scale, reach, cuts=(), kind=jnp.bfloat16):
    array = jax.random.normal(rng, dims, jnp.float32) * scale
    if len(cuts) > 0:
        array = steps_of(rng, dims, cuts, -0.22, 0.18) * array
    return jnp.clip(array, min=-reach, max=reach).astype(kind)


def setup_inputs(seed: int = 0) -> dict:
    streams_of = jax.random.split(jax.random.key(seed), 14)
    fluid_state = centred(streams_of[0], (NX, NY, DOF), 1.0, 6.0, ((0, 32), (1, 4)), jnp.float32)
    fluid_rhs = centred(streams_of[1], (NX, NY, DOF), 4.0, 24.0, ((0, 32), (1, 4)), jnp.float32)
    element_scale = jnp.clip(jnp.exp(math.log(4.0) - 1.3862944 * jax.random.uniform(streams_of[2], (NX, NY), jnp.float32) ** steps_of(streams_of[2], (NX, NY), ((0, 32), (1, 4)), -0.2, 0.2)), 1.0, 4.0)
    element_matrix = draw_element_matrix(jax.random.fold_in(streams_of[13], 71), 0)
    couple_x = centred(streams_of[4], (DOF, DOF), (16 * DOF) ** -0.5, 0.09375)
    couple_y = centred(streams_of[5], (DOF, DOF), (16 * DOF) ** -0.5, 0.09375)
    block_inverse = draw_block_inverse(jax.random.fold_in(streams_of[13], 71), 0)
    traction_map = centred(streams_of[7], (3, DOF), DOF ** -0.5, 0.375)
    slot_elem = plant(jax.random.randint(streams_of[8], (N_SLAB, N_PATCH, QDEV), 0, EX_DEV * EY_DEV), jax.random.fold_in(streams_of[8], 1), 0, (EX_DEV * EY_DEV) - 1).astype(jnp.int32)
    slot_point = plant(jax.random.randint(streams_of[9], (N_SLAB, N_PATCH, QDEV), 0, NU * NV), jax.random.fold_in(streams_of[9], 1), 0, (NU * NV) - 1).astype(jnp.int32)
    slot_count = draw_slot_count(jax.random.fold_in(streams_of[13], 71), 0)
    displacement = centred(streams_of[11], (3, NU_ALL, NV), 1.0, 6.0, ((1, 4),), jnp.float32)
    stiffness = jnp.clip(jnp.exp(math.log(0.3) - 2.3025852 * jax.random.uniform(streams_of[12], (NU_ALL, NV), jnp.float32) ** steps_of(streams_of[12], (NU_ALL, NV), ((0, 4),), -0.2, 0.2)), 0.03, 0.3)
    return {"fluid_state": fluid_state, "fluid_rhs": fluid_rhs, "element_scale": element_scale, "element_matrix": element_matrix, "couple_x": couple_x, "couple_y": couple_y, "block_inverse": block_inverse, "traction_map": traction_map, "slot_elem": slot_elem, "slot_point": slot_point, "slot_count": slot_count, "displacement": displacement, "stiffness": stiffness}


def element_apply(rounded, scale, element_matrix, couple_x, couple_y):
    padded = jnp.pad(rounded, ((1, 1), (1, 1), (0, 0)))
    along_x = (padded[:-2, 1:-1].astype(jnp.float32) + padded[2:, 1:-1].astype(jnp.float32)).astype(jnp.bfloat16)
    along_y = (padded[1:-1, :-2].astype(jnp.float32) + padded[1:-1, 2:].astype(jnp.float32)).astype(jnp.bfloat16)
    width = rounded.shape[2]
    own = jnp.dot(rounded.reshape(-1, width), element_matrix, preferred_element_type=jnp.float32)
    side_x = jnp.dot(along_x.reshape(-1, width), couple_x, preferred_element_type=jnp.float32)
    side_y = jnp.dot(along_y.reshape(-1, width), couple_y, preferred_element_type=jnp.float32)
    return scale[:, :, None] * own.reshape(rounded.shape) - side_x.reshape(rounded.shape) - side_y.reshape(rounded.shape)


def laplace_net(field):
    edged = jnp.pad(field, ((0, 0), (1, 1), (1, 1)))
    return 4.0 * field - (edged[:, 2:, 1:-1] + edged[:, :-2, 1:-1] + edged[:, 1:-1, 2:] + edged[:, 1:-1, :-2])


def pick_rows(block, picks):
    return block[picks]


def reference(fluid_state, fluid_rhs, element_scale, element_matrix, couple_x, couple_y, block_inverse, traction_map, slot_elem, slot_point, slot_count, displacement, stiffness):
    state = fluid_state
    for sweep in range(SWEEPS):
        rounded = state.astype(jnp.bfloat16)
        applied = element_apply(rounded, element_scale, element_matrix, couple_x, couple_y)
        residue = (fluid_rhs - applied).astype(jnp.bfloat16)
        update = jnp.dot(residue.reshape(-1, DOF), block_inverse, preferred_element_type=jnp.float32).reshape(state.shape)
        state = state + update / element_scale[:, :, None]
    fluid_out = state
    final = fluid_out.astype(jnp.bfloat16)
    blocks = final.reshape(N_SLAB, EX_DEV, N_PATCH, EY_DEV, DOF).transpose(0, 2, 1, 3, 4).reshape(N_SLAB, N_PATCH, EX_DEV * EY_DEV, DOF)
    rows = jax.vmap(jax.vmap(pick_rows))(blocks, slot_elem)
    pull = jnp.einsum("cd,snqd->csnq", traction_map.astype(jnp.float32), rows.astype(jnp.float32))
    slot_ids = jnp.arange(QDEV, dtype=jnp.int32)
    owner = slot_ids // CAP
    limit = jnp.take(slot_count, owner, axis=2)
    live = ((slot_ids % CAP)[None, None, :] < limit).astype(jnp.float32)
    target = owner[None, None, :] * (NU * NV) + slot_point
    loads = jnp.zeros((3, N_PATCH * NU * NV), jnp.float32).at[:, target.reshape(-1)].add((pull * live[None]).reshape(3, -1))
    loads = loads.reshape(3, NU_ALL, NV)
    bend = laplace_net(displacement)
    stiff_term = stiffness[None] * (laplace_net(bend) + 4.0 * bend)
    displacement_new = displacement + (loads - stiff_term) / (36.0 * stiffness[None])
    wall_motion = displacement_new.reshape(3, -1)[:, target.reshape(-1)].reshape(3, N_SLAB, N_PATCH, QDEV) * live[None]
    return fluid_out, displacement_new, wall_motion
```

```python
import jax
import jax.numpy as jnp
from jax import lax
from jax.experimental import pallas as pl
from jax.experimental.pallas import tpu as pltpu
from jax.sharding import PartitionSpec as P

SWEEPS = 3
BF = jnp.bfloat16
F32 = jnp.float32
I32 = jnp.int32
LIMIT = 48 << 20


def vmem(n):
    return [pl.BlockSpec(memory_space=pltpu.VMEM)] * n


def iota(shape, dim):
    return lax.broadcasted_iota(I32, shape, dim)


def nt(a, b):
    return lax.dot_general(a, b, (((1,), (1,)), ((), ())), preferred_element_type=F32)


def slot_rows(final, tmap, elem, point, count_ref, rows_ref):
    owners = rows_ref.shape[0]
    slots = elem.shape[1]
    cap = slots // owners
    traction = nt(tmap, final).astype(BF)
    hot = (iota((final.shape[0], slots), 0) == elem).astype(F32).astype(BF)
    pull = jnp.dot(traction, hot, preferred_element_type=F32)
    slot = iota((1, slots), 1)
    owner = slot // cap
    limit = jnp.zeros((1, slots), I32)
    for k in range(owners):
        limit = jnp.where(owner == k, count_ref[0, k], limit)
    live = (slot - owner * cap) < limit
    row = point // 128
    code = (128 + (point - row * 128)).astype(F32)
    for b in range(6):
        code = code * jnp.where((row >> b) & 1 == 1, F32(2.0 ** (2**b)), F32(1.0))
    code = jnp.where(live, code, 0.0)
    pull = jnp.where(live, pull, 0.0)
    for k in range(owners):
        for j in range(4):
            source = code if j == 3 else pull[j : j + 1]
            for h in range(2):
                start = k * cap + h * 128
                rows_ref[k, 2 * j + h : 2 * j + h + 1, :] = source[:, start : start + 128]


def pack_kernel(state_ref, tmap_ref, elem_ref, point_ref, count_ref, out_ref, rows_ref):
    width = state_ref.shape[2]
    final = state_ref[...].astype(BF).reshape(-1, width)
    slot_rows(final, tmap_ref[...], elem_ref[...], point_ref[...], count_ref, rows_ref)
    out_ref[...] = jnp.broadcast_to(rows_ref[...].astype(BF)[None], out_ref.shape)


def decode(code):
    row = jnp.zeros(code.shape, F32)
    for b in (5, 4, 3, 2, 1, 0):
        big = code >= F32(128.0 * 2.0 ** (2**b))
        row = row + jnp.where(big, F32(2**b), 0.0)
        code = code * jnp.where(big, F32(2.0 ** -(2**b)), 1.0)
    return row, code - 128.0


def owner_kernel(src_ref, got_ref, disp_ref, stiff_ref, kd_ref, new_ref, *rest):
    replies = rest[:4]
    row_ref, lane_ref, acc_ref = rest[4:]
    sources = got_ref.shape[0]
    rows = disp_ref.shape[1]
    for h in range(2):
        row, lane = decode(got_ref[:, 6 + h, :].astype(F32))
        row_ref[h] = row
        lane_ref[h] = lane
    row_ids = iota((rows, 128), 0).astype(F32)
    lane_ids = iota((128, 128), 0).astype(F32)
    acc_ref[...] = jnp.zeros_like(acc_ref)
    group = 8

    def body(i, carry):
        base = pl.multiple_of(i * group, group)
        row8 = [row_ref[h, pl.ds(base, group), :] for h in range(2)]
        lane8 = [lane_ref[h, pl.ds(base, group), :] for h in range(2)]
        total = jnp.zeros((3 * rows, 128), F32)
        for g in range(group):
            vals = got_ref[base + g].astype(F32)
            left = []
            right = []
            for h in range(2):
                mask = row_ids == row8[h][g : g + 1]
                left.append(
                    jnp.concatenate(
                        [
                            jnp.where(mask, vals[2 * c + h : 2 * c + h + 1], 0.0).astype(BF)
                            for c in range(3)
                        ],
                        axis=0,
                    )
                )
                right.append((lane_ids == lane8[h][g : g + 1]).astype(F32).astype(BF))
            total += nt(jnp.concatenate(left, axis=1), jnp.concatenate(right, axis=1))
        acc_ref[...] += total
        return carry

    lax.fori_loop(0, sources // group, body, 0)
    loads = acc_ref[...].reshape(3, rows, 128)
    new = disp_ref[...] + (loads - kd_ref[...]) / (36.0 * stiff_ref[...])[None]
    new_ref[...] = new
    flat = new.reshape(3 * rows, 128)
    high = flat.astype(BF)
    rest1 = flat - high.astype(F32)
    mid = rest1.astype(BF)
    low = (rest1 - mid.astype(F32)).astype(BF)
    for d in range(4):
        src = src_ref[d]
        for h in range(2):
            row = row_ref[h, pl.ds(src, 1), :]
            lane = lane_ref[h, pl.ds(src, 1), :]
            hot = (lane_ids == lane).astype(F32).astype(BF)
            picked = jnp.dot(high, hot, preferred_element_type=F32)
            picked += jnp.dot(mid, hot, preferred_element_type=F32)
            picked += jnp.dot(low, hot, preferred_element_type=F32)
            mask = row_ids == row
            for c in range(3):
                part = jnp.where(mask, picked[c * rows : (c + 1) * rows], 0.0)
                replies[d][c : c + 1, h * 128 : (h + 1) * 128] = part.sum(axis=0, keepdims=True)


def finish_kernel(src_ref, r0, r1, r2, r3, out_ref):
    cap = r0.shape[1]
    for d, reply in enumerate((r0, r1, r2, r3)):
        start = pl.multiple_of(src_ref[4 + d] * cap, cap)
        out_ref[:, pl.ds(start, cap)] = reply[0:3, :]


def shell_kernel(side_ref, disp_ref, stiff_ref, high_ref, low_ref, kd_ref, field_ref, bend_ref):
    rows = disp_ref.shape[1]
    top = side_ref[0] > 0
    bottom = side_ref[1] > 0
    halo = high_ref[...].astype(F32) + low_ref[...].astype(F32)
    field_ref[...] = jnp.zeros_like(field_ref)
    bend_ref[...] = jnp.zeros_like(bend_ref)
    field_ref[:, 8 : 8 + rows, :] = disp_ref[...]
    lane = iota((1, 1, 128), 2)

    def sides(x):
        left = jnp.where(lane == 0, 0.0, pltpu.roll(x, 1, 2))
        right = jnp.where(lane == 127, 0.0, pltpu.roll(x, 127, 2))
        return left + right

    for c in range(3):
        field_ref[c, 6:8, :] = jnp.where(top, halo[0, 2 * c : 2 * c + 2], 0.0)
        field_ref[c, 8 + rows : 10 + rows, :] = jnp.where(bottom, halo[1, 2 * c : 2 * c + 2], 0.0)
    mid = field_ref[:, 7 : 9 + rows, :]
    bend = 4.0 * mid - (
        field_ref[:, 6 : 8 + rows, :] + field_ref[:, 8 : 10 + rows, :] + sides(mid)
    )
    bend_ref[:, 7 : 9 + rows, :] = bend
    for c in range(3):
        bend_ref[c, 7:8, :] = jnp.where(top, bend_ref[c, 7:8, :], 0.0)
        bend_ref[c, 8 + rows : 9 + rows, :] = jnp.where(
            bottom, bend_ref[c, 8 + rows : 9 + rows, :], 0.0
        )
    mid = bend_ref[:, 8 : 8 + rows, :]
    again = 4.0 * mid - (
        bend_ref[:, 7 : 7 + rows, :] + bend_ref[:, 9 : 9 + rows, :] + sides(mid)
    )
    kd_ref[...] = stiff_ref[...][None] * (again + 4.0 * mid)


def smem():
    return pl.BlockSpec(memory_space=pltpu.SMEM)


def params():
    return pltpu.CompilerParams(vmem_limit_bytes=LIMIT)


def patch_pairs(d):
    return [(p, p ^ d) for p in range(4)]


def exchange_and_relax(message, displacement, stiffness, kd):
    slabs, owners = lax.axis_size("slab"), lax.axis_size("patch")
    rows = displacement.shape[1]
    sources = slabs * owners
    got = lax.all_to_all(
        message.reshape(sources, 8, 128), ("slab", "patch"), 0, 0, tiled=True
    )
    slab, patch = lax.axis_index("slab"), lax.axis_index("patch")
    peer = patch ^ jnp.arange(4, dtype=I32)
    where = jnp.concatenate([slab * owners + peer, peer])
    reply = jax.ShapeDtypeStruct((8, 256), F32)
    new, *replies = pl.pallas_call(
        owner_kernel,
        out_shape=(jax.ShapeDtypeStruct(displacement.shape, F32),) + (reply,) * 4,
        in_specs=[smem()] + vmem(4),
        out_specs=vmem(5),
        scratch_shapes=[
            pltpu.VMEM((2, sources, 128), F32),
            pltpu.VMEM((2, sources, 128), F32),
            pltpu.VMEM((3 * rows, 128), F32),
        ],
        compiler_params=params(),
        name="owner",
    )(where, got, displacement, stiffness, kd)
    back = [replies[0]] + [
        lax.ppermute(replies[d], "patch", patch_pairs(d)) for d in (1, 2, 3)
    ]
    wall = pl.pallas_call(
        finish_kernel,
        out_shape=jax.ShapeDtypeStruct((3, owners * 256), F32),
        in_specs=[smem()] + vmem(4),
        out_specs=pl.BlockSpec(memory_space=pltpu.VMEM),
        compiler_params=params(),
        name="finish",
    )(where, *back)
    return new, wall


def split(value):
    high = value.astype(BF)
    return high, (value - high.astype(F32)).astype(BF)


def shell_force(displacement, stiffness):
    patch = lax.axis_index("patch")
    rows = displacement.shape[1]
    last = lax.axis_size("patch") - 1
    even = patch % 2 == 0
    first_rows = displacement[:, :2].reshape(6, 128)
    last_rows = displacement[:, rows - 2 :].reshape(6, 128)
    to_one = jnp.concatenate(split(jnp.where(even, last_rows, first_rows)))
    to_three = jnp.concatenate(split(jnp.where(even, first_rows, last_rows)))
    from_one = lax.ppermute(to_one, "patch", patch_pairs(1))
    from_three = lax.ppermute(to_three, "patch", patch_pairs(3))
    above = jnp.where(even, from_three, from_one)
    below = jnp.where(even, from_one, from_three)
    halo = jnp.stack([above, below])
    side = jnp.stack([(patch > 0).astype(I32), (patch < last).astype(I32)])
    shape = displacement.shape
    return pl.pallas_call(
        shell_kernel,
        out_shape=jax.ShapeDtypeStruct(shape, F32),
        in_specs=[smem()] + vmem(4),
        out_specs=pl.BlockSpec(memory_space=pltpu.VMEM),
        scratch_shapes=[pltpu.VMEM((3, rows + 16, 128), F32)] * 2,
        compiler_params=params(),
        name="shell",
    )(side, displacement, stiffness, halo[:, :6], halo[:, 6:])


def extended(value, sides, width):
    edges = {}
    for axis, dim in sides:
        count, length = (lax.axis_size(axis), value.shape[dim])
        up = [(i, (i + 1) % count) for i in range(count - 1)]
        last = lax.slice_in_dim(value, length - width, length, axis=dim)
        leading = lax.slice_in_dim(value, 0, width, axis=dim)
        edges[dim] = (
            lax.ppermute(last, axis, up),
            lax.ppermute(leading, axis, [(b, a) for a, b in up]),
        )
    done = []
    for _, dim in sides:
        low, high = edges[dim]
        around = [(width, width) if d in done else (0, 0) for d in range(value.ndim)]
        value = jnp.concatenate([jnp.pad(low, around), value, jnp.pad(high, around)], axis=dim)
        done.append(dim)
    return value


def element_apply(rounded, scale, element_matrix, couple_x, couple_y):
    padded = extended(rounded, (("slab", 0), ("patch", 1)), 1)
    along_x = (padded[:-2, 1:-1].astype(F32) + padded[2:, 1:-1].astype(F32)).astype(BF)
    along_y = (padded[1:-1, :-2].astype(F32) + padded[1:-1, 2:].astype(F32)).astype(BF)
    width = rounded.shape[2]
    own = jnp.dot(rounded.reshape(-1, width), element_matrix, preferred_element_type=F32)
    side_x = jnp.dot(along_x.reshape(-1, width), couple_x, preferred_element_type=F32)
    side_y = jnp.dot(along_y.reshape(-1, width), couple_y, preferred_element_type=F32)
    return (
        scale[:, :, None] * own.reshape(rounded.shape)
        - side_x.reshape(rounded.shape)
        - side_y.reshape(rounded.shape)
    )


def shards(
    fluid_state,
    fluid_rhs,
    element_scale,
    element_matrix,
    couple_x,
    couple_y,
    block_inverse,
    traction_map,
    slot_elem,
    slot_point,
    slot_count,
    displacement,
    stiffness,
):
    width = fluid_state.shape[2]
    slots = slot_elem.shape[2]
    slabs, owners = lax.axis_size("slab"), lax.axis_size("patch")
    kd = shell_force(displacement, stiffness)
    state = fluid_state
    for sweep in range(SWEEPS):
        rounded = state.astype(BF)
        applied = element_apply(rounded, element_scale, element_matrix, couple_x, couple_y)
        residue = (fluid_rhs - applied).astype(BF)
        update = jnp.dot(
            residue.reshape(-1, width), block_inverse, preferred_element_type=F32
        ).reshape(state.shape)
        state = state + update / element_scale[:, :, None]
    tmap = jnp.pad(traction_map, ((0, 5), (0, 0)))
    message = pl.pallas_call(
        pack_kernel,
        out_shape=jax.ShapeDtypeStruct((slabs, owners, 8, 128), BF),
        in_specs=vmem(4) + [smem()],
        out_specs=pl.BlockSpec(memory_space=pltpu.VMEM),
        scratch_shapes=[pltpu.VMEM((owners, 8, 128), F32)],
        compiler_params=params(),
        name="pack",
    )(
        state,
        tmap,
        slot_elem.reshape(1, slots),
        slot_point.reshape(1, slots),
        slot_count.reshape(1, owners),
    )
    new, wall = exchange_and_relax(message, displacement, stiffness, kd)
    return state, new, wall.reshape(3, 1, 1, slots)


def solution(mesh):
    return jax.shard_map(
        shards,
        mesh=mesh,
        in_specs=(
            P("slab", "patch", None),
            P("slab", "patch", None),
            P("slab", "patch"),
            P(),
            P(),
            P(),
            P(),
            P(),
            P("slab", "patch", None),
            P("slab", "patch", None),
            P("slab", "patch", None),
            P(None, "patch", None),
            P("patch", None),
        ),
        out_specs=(
            P("slab", "patch", None),
            P(None, "patch", None),
            P(None, "slab", "patch", None),
        ),
        check_vma=False,
    )
```

```python
import jax
import jax.numpy as jnp
from jax import lax
from jax.experimental import pallas as pl
from jax.experimental.pallas import tpu as pltpu
from jax.sharding import PartitionSpec as P

SWEEPS = 3
BF = jnp.bfloat16
F32 = jnp.float32
I32 = jnp.int32
LIMIT = 48 << 20
STRIPS = 112


def vmem(n):
    return [pl.BlockSpec(memory_space=pltpu.VMEM)] * n


def iota(shape, dim):
    return lax.broadcasted_iota(I32, shape, dim)


def nt(a, b):
    return lax.dot_general(a, b, (((1,), (1,)), ((), ())), preferred_element_type=F32)


def slot_rows(final, tmap, elem, point, count_ref, rows_ref):
    owners = rows_ref.shape[0]
    slots = elem.shape[1]
    cap = slots // owners
    traction = nt(tmap, final).astype(BF)
    hot = (iota((final.shape[0], slots), 0) == elem).astype(F32).astype(BF)
    pull = jnp.dot(traction, hot, preferred_element_type=F32)
    slot = iota((1, slots), 1)
    owner = slot // cap
    limit = jnp.zeros((1, slots), I32)
    for k in range(owners):
        limit = jnp.where(owner == k, count_ref[0:1, k : k + 1], limit)
    live = (slot - owner * cap) < limit
    row = point // 128
    code = (128 + (point - row * 128)).astype(F32)
    for b in range(6):
        code = code * jnp.where((row >> b) & 1 == 1, F32(2.0 ** (2**b)), F32(1.0))
    code = jnp.where(live, code, 0.0)
    pull = jnp.where(live, pull, 0.0)
    for k in range(owners):
        for j in range(4):
            source = code if j == 3 else pull[j : j + 1]
            for h in range(2):
                start = k * cap + h * 128
                rows_ref[k, 2 * j + h : 2 * j + h + 1, :] = source[:, start : start + 128]


def decode(code):
    row = jnp.zeros(code.shape, F32)
    for b in (5, 4, 3, 2, 1, 0):
        big = code >= F32(128.0 * 2.0 ** (2**b))
        row = row + jnp.where(big, F32(2**b), 0.0)
        code = code * jnp.where(big, F32(2.0 ** -(2**b)), 1.0)
    return row, code - 128.0


def owner_kernel(got_ref, disp_ref, stiff_ref, kd_ref, new_ref, *rest):
    replies = rest[:4]
    row_ref, lane_ref, acc_ref = rest[4:]
    sources = got_ref.shape[0]
    rows = disp_ref.shape[1]
    patch = lax.axis_index("patch")
    first = lax.axis_index("slab") * 4
    for h in range(2):
        row, lane = decode(got_ref[:, 6 + h, :].astype(F32))
        row_ref[h] = row
        lane_ref[h] = lane
    row_ids = iota((rows, 128), 0).astype(F32)
    lane_ids = iota((128, 128), 0).astype(F32)
    acc_ref[...] = jnp.zeros_like(acc_ref)
    group = 8

    def body(i, carry):
        base = pl.multiple_of(i * group, group)
        row8 = [row_ref[h, pl.ds(base, group), :] for h in range(2)]
        lane8 = [lane_ref[h, pl.ds(base, group), :] for h in range(2)]
        total = jnp.zeros((3 * rows, 128), F32)
        for g in range(group):
            vals = got_ref[base + g].astype(F32)
            left = []
            right = []
            for h in range(2):
                mask = row_ids == row8[h][g : g + 1]
                left.append(
                    jnp.concatenate(
                        [
                            jnp.where(mask, vals[2 * c + h : 2 * c + h + 1], 0.0).astype(BF)
                            for c in range(3)
                        ],
                        axis=0,
                    )
                )
                right.append((lane_ids == lane8[h][g : g + 1]).astype(F32).astype(BF))
            total += nt(jnp.concatenate(left, axis=1), jnp.concatenate(right, axis=1))
        acc_ref[...] += total
        return carry

    lax.fori_loop(0, sources // group, body, 0)
    loads = acc_ref[...].reshape(3, rows, 128)
    new = disp_ref[...] + (loads - kd_ref[...]) / (36.0 * stiff_ref[...])[None]
    new_ref[...] = new
    flat = new.reshape(3 * rows, 128)
    high = flat.astype(BF)
    rest1 = flat - high.astype(F32)
    mid = rest1.astype(BF)
    low = (rest1 - mid.astype(F32)).astype(BF)
    for d in range(4):
        src = first + (patch ^ d)
        for h in range(2):
            row = row_ref[h, pl.ds(src, 1), :]
            lane = lane_ref[h, pl.ds(src, 1), :]
            hot = (lane_ids == lane).astype(F32).astype(BF)
            picked = jnp.dot(high, hot, preferred_element_type=F32)
            picked += jnp.dot(mid, hot, preferred_element_type=F32)
            picked += jnp.dot(low, hot, preferred_element_type=F32)
            mask = row_ids == row
            for c in range(3):
                part = jnp.where(mask, picked[c * rows : (c + 1) * rows], 0.0)
                replies[d][c : c + 1, h * 128 : (h + 1) * 128] = part.sum(axis=0, keepdims=True)


def finish_kernel(r0, r1, r2, r3, out_ref):
    cap = r0.shape[1]
    patch = lax.axis_index("patch")
    for d, reply in enumerate((r0, r1, r2, r3)):
        start = pl.multiple_of((patch ^ d) * cap, cap)
        for c in range(3):
            out_ref[c, 0, :, pl.ds(start, cap)] = reply[c : c + 1, :]


def shell_kernel(one_ref, three_ref, disp_ref, stiff_ref, kd_ref, field_ref, bend_ref):
    rows = disp_ref.shape[1]
    patch = lax.axis_index("patch")
    top = patch > 0
    bottom = patch < 3
    even = patch % 2 == 0
    one, three = (
        ref[STRIPS - 8 :, :128].astype(F32) + ref[STRIPS - 8 :, 128:].astype(F32)
        for ref in (one_ref, three_ref)
    )
    above = jnp.where(even, three, one)
    below = jnp.where(even, one, three)
    field_ref[...] = jnp.zeros_like(field_ref)
    bend_ref[...] = jnp.zeros_like(bend_ref)
    field_ref[:, 8 : 8 + rows, :] = disp_ref[...]
    lane = iota((1, 1, 128), 2)

    def sides(x):
        left = jnp.where(lane == 0, 0.0, pltpu.roll(x, 1, 2))
        right = jnp.where(lane == 127, 0.0, pltpu.roll(x, 127, 2))
        return left + right

    for c in range(3):
        field_ref[c, 6:8, :] = jnp.where(top, above[2 * c : 2 * c + 2], 0.0)
        field_ref[c, 8 + rows : 10 + rows, :] = jnp.where(bottom, below[2 * c : 2 * c + 2], 0.0)
    mid = field_ref[:, 7 : 9 + rows, :]
    bend = 4.0 * mid - (
        field_ref[:, 6 : 8 + rows, :] + field_ref[:, 8 : 10 + rows, :] + sides(mid)
    )
    bend_ref[:, 7 : 9 + rows, :] = bend
    for c in range(3):
        bend_ref[c, 7:8, :] = jnp.where(top, bend_ref[c, 7:8, :], 0.0)
        bend_ref[c, 8 + rows : 9 + rows, :] = jnp.where(
            bottom, bend_ref[c, 8 + rows : 9 + rows, :], 0.0
        )
    mid = bend_ref[:, 8 : 8 + rows, :]
    again = 4.0 * mid - (
        bend_ref[:, 7 : 7 + rows, :] + bend_ref[:, 9 : 9 + rows, :] + sides(mid)
    )
    kd_ref[...] = stiff_ref[...][None] * (again + 4.0 * mid)


def params():
    return pltpu.CompilerParams(vmem_limit_bytes=LIMIT)


def patch_pairs(d):
    return [(p, p ^ d) for p in range(4)]


def exchange_and_relax(message, displacement, stiffness, kd):
    slabs, owners = lax.axis_size("slab"), lax.axis_size("patch")
    rows = displacement.shape[1]
    sources = slabs * owners
    got = lax.all_to_all(
        message.reshape(sources, 8, 128), ("slab", "patch"), 0, 0, tiled=True
    )
    reply = jax.ShapeDtypeStruct((8, 256), F32)
    new, *replies = pl.pallas_call(
        owner_kernel,
        out_shape=(jax.ShapeDtypeStruct(displacement.shape, F32),) + (reply,) * 4,
        in_specs=vmem(4),
        out_specs=vmem(5),
        scratch_shapes=[
            pltpu.VMEM((2, sources, 128), F32),
            pltpu.VMEM((2, sources, 128), F32),
            pltpu.VMEM((3 * rows, 128), F32),
        ],
        compiler_params=params(),
        name="owner",
    )(got, displacement, stiffness, kd)
    back = [replies[0]] + [
        lax.ppermute(replies[d], "patch", patch_pairs(d)) for d in (1, 2, 3)
    ]
    wall = pl.pallas_call(
        finish_kernel,
        out_shape=jax.ShapeDtypeStruct((3, 1, 1, owners * 256), F32),
        in_specs=vmem(4),
        out_specs=pl.BlockSpec(memory_space=pltpu.VMEM),
        compiler_params=params(),
        name="finish",
    )(*back)
    return new, wall


def halves(value):
    high = value.astype(BF)
    low = (value - high.astype(F32)).astype(BF)
    return jnp.concatenate([high.astype(F32), low.astype(F32)], axis=1)


def near_kernel(state_ref, rhs_ref, scale_ref, out_ref):
    odd = lax.axis_index("slab") % 2
    cols = state_ref.shape[1]
    for i, row in enumerate((odd, 1 - odd)):
        out_ref[i * cols : (i + 1) * cols, :] = state_ref[row].astype(BF)
        out_ref[(i + 2) * cols : (i + 3) * cols, :] = rhs_ref[row].astype(BF)
    flip = odd == 1
    first = jnp.where(flip, scale_ref[1:2], scale_ref[0:1])
    second = jnp.where(flip, scale_ref[0:1], scale_ref[1:2])
    pair = jnp.concatenate([halves(first), halves(second), jnp.zeros((14, 256), F32)], axis=0)
    out_ref[4 * cols :, :] = pair.astype(BF)


def row_table(own, inner, outer):
    return (
        (outer, 1, 3, 1),
        (outer, 0, 2, 0),
        (own, 0, 2, 0),
        (own, 1, 3, 1),
        (inner, 1, 3, 1),
        (inner, 0, 2, 0),
    )


def strip_kernel(own_ref, inner_ref, outer_ref, disp_ref, one_ref, three_ref, relay_ref, build_ref):
    patch = lax.axis_index("patch")
    even = patch % 2 == 0
    cols = relay_ref.shape[0]
    relay_ref[...] = outer_ref[0:cols, :]
    table = row_table(own_ref, inner_ref, outer_ref)
    build_ref[:, 96:, :] = jnp.zeros((2, STRIPS - 96, 256), F32)
    for r, (ref, state, rhs, scale) in enumerate(table):
        for part, block in enumerate((state, rhs)):
            at = (part * 6 + r) * 8
            low = ref[block * cols : block * cols + 16, :].astype(F32)[0:8]
            high = ref[(block + 1) * cols - 16 : (block + 1) * cols, :].astype(F32)[8:16]
            build_ref[0, at : at + 8, :] = jnp.where(even, high, low)
            build_ref[1, at : at + 8, :] = jnp.where(even, low, high)
        line = ref[4 * cols : 4 * cols + 16, :].astype(F32)[scale : scale + 1]
        build_ref[0, 97 + r : 98 + r, :] = line
        build_ref[1, 97 + r : 98 + r, :] = line
    rows = disp_ref.shape[1]
    for c in range(3):
        top = halves(disp_ref[c, 0:2, :])
        bottom = halves(disp_ref[c, rows - 2 : rows, :])
        at = STRIPS - 8 + 2 * c
        build_ref[0, at : at + 2, :] = jnp.where(even, bottom, top)
        build_ref[1, at : at + 2, :] = jnp.where(even, top, bottom)
    one_ref[...] = build_ref[0].astype(BF)
    three_ref[...] = build_ref[1].astype(BF)


def sweep_kernel(
    state_ref,
    rhs_ref,
    scale_ref,
    inner_ref,
    outer_ref,
    one_ref,
    three_ref,
    relay_ref,
    matrix_ref,
    x_ref,
    y_ref,
    inverse_ref,
    tmap_ref,
    elem_ref,
    point_ref,
    count_ref,
    out_ref,
    message_ref,
    v_ref,
    r_ref,
    s_ref,
    i_ref,
    line_ref,
    side_ref,
    rows_ref,
):
    slab, patch = lax.axis_index("slab"), lax.axis_index("patch")
    last_slab, last_patch = lax.axis_size("slab") - 1, lax.axis_size("patch") - 1
    odd = slab % 2
    even = patch % 2 == 0
    cols, width = state_ref.shape[1], state_ref.shape[2]
    wide = cols + 16
    inside = (slab > 0) & (slab < last_slab)
    one = one_ref[...].astype(F32)
    three = three_ref[...].astype(F32)
    side_ref[0] = jnp.where(even, three, one)
    side_ref[1] = jnp.where(even, one, three)
    col = iota((wide, width), 0)
    valid = (col >= 8) & (col < 8 + cols)
    valid = valid | ((col < 8) & (patch > 0)) | ((col >= 8 + cols) & (patch < last_patch))
    edge = valid.astype(F32)
    keep = edge * inside.astype(F32)
    table = row_table(None, inner_ref, outer_ref)
    lane = iota((1, 128), 1)
    line_ref[...] = jnp.ones_like(line_ref)
    for r, (ref, state, rhs, scale) in enumerate(table):
        if ref is None:
            row = odd if r == 2 else 1 - odd
            v_ref[r + 1, 8 : 8 + cols, :] = state_ref[row]
            r_ref[r, 8 : 8 + cols, :] = rhs_ref[row]
            line = jnp.where(row == 1, scale_ref[1:2], scale_ref[0:1])
        else:
            v_ref[r + 1, 8 : 8 + cols, :] = ref[state * cols : (state + 1) * cols, :].astype(F32)
            r_ref[r, 8 : 8 + cols, :] = ref[rhs * cols : (rhs + 1) * cols, :].astype(F32)
            both = ref[4 * cols : 4 * cols + 16, :].astype(F32)[scale : scale + 1]
            line = both[:, :128] + both[:, 128:]
        for e, start in ((0, 0), (1, 8 + cols)):
            v_ref[r + 1, start : start + 8, :] = side_ref[e, 8 * r : 8 * r + 8, :]
            r_ref[r, start : start + 8, :] = side_ref[e, 48 + 8 * r : 56 + 8 * r, :]
            both = side_ref[e, 97 + r : 98 + r, :]
            far = pltpu.roll(both[:, :128] + both[:, 128:], 64, 1)
            here = (lane >= start) & (lane < start + 8)
            line = jnp.where(here, far, line)
        line_ref[r : r + 1, :] = jnp.where(line > 0.0, line, 1.0)
    v_ref[0] = jnp.zeros((wide, width), F32)
    v_ref[7] = jnp.zeros((wide, width), F32)
    v_ref[0, 8 : 8 + cols, :] = outer_ref[4 * cols + 16 : 5 * cols + 16, :].astype(F32)
    v_ref[7, 8 : 8 + cols, :] = relay_ref[...].astype(F32)
    for r in range(8):
        v_ref[r] = v_ref[r] * (keep if r < 3 else edge)
    lines = line_ref[...]
    columns = jnp.transpose(lines)
    inverses = jnp.transpose(1.0 / lines)
    for r in range(6):
        s_ref[r] = jnp.broadcast_to(columns[:wide, r : r + 1], (wide, width))
        i_ref[r] = jnp.broadcast_to(inverses[:wide, r : r + 1], (wide, width))
    for sweep in range(SWEEPS):
        a, b = 1 + sweep, 7 - sweep
        n = b - a
        near = v_ref[a - 1 : b + 1].astype(BF).astype(F32)
        mid = near[1 : n + 1]
        nx = (near[0:n] + near[2 : n + 2]).astype(BF)
        ny = (pltpu.roll(mid, 1, 1) + pltpu.roll(mid, wide - 1, 1)).astype(BF)
        flat = (n * wide, width)
        own = jnp.dot(mid.astype(BF).reshape(flat), matrix_ref[...], preferred_element_type=F32)
        side = jnp.dot(nx.reshape(flat), x_ref[...], preferred_element_type=F32)
        side += jnp.dot(ny.reshape(flat), y_ref[...], preferred_element_type=F32)
        scale = s_ref[a - 1 : b - 1].reshape(flat)
        rhs = r_ref[a - 1 : b - 1].reshape(flat)
        residue = (rhs - (scale * own - side)).astype(BF)
        update = jnp.dot(residue, inverse_ref[...], preferred_element_type=F32)
        update = update * i_ref[a - 1 : b - 1].reshape(flat)
        value = v_ref[a:b] + update.reshape(n, wide, width)
        for j in range(n):
            v_ref[a + j] = value[j] * (keep if a + j < 3 else edge)
    out_ref[odd] = v_ref[3, 8 : 8 + cols, :]
    out_ref[1 - odd] = v_ref[4, 8 : 8 + cols, :]
    final = out_ref[...].astype(BF).reshape(2 * cols, width)
    slot_rows(final, tmap_ref[...], elem_ref[...], point_ref[...], count_ref, rows_ref)
    message_ref[...] = jnp.broadcast_to(rows_ref[...].astype(BF)[None], message_ref.shape)


def call(kernel, name, out_shape, operands, scratch=()):
    return pl.pallas_call(
        kernel,
        out_shape=out_shape,
        in_specs=vmem(len(operands)),
        out_specs=jax.tree.map(lambda _: vmem(1)[0], out_shape),
        scratch_shapes=list(scratch),
        compiler_params=params(),
        name=name,
    )(*operands)


def shards(
    fluid_state,
    fluid_rhs,
    element_scale,
    element_matrix,
    couple_x,
    couple_y,
    block_inverse,
    traction_map,
    slot_elem,
    slot_point,
    slot_count,
    displacement,
    stiffness,
):
    cols, width = fluid_state.shape[1:]
    slots = slot_elem.shape[2]
    slabs, owners = lax.axis_size("slab"), lax.axis_size("patch")
    shape = jax.ShapeDtypeStruct
    inner_pairs = [(s, s ^ 1) for s in range(slabs)]
    outer_pairs = [(s, s + 1) for s in range(1, slabs - 1, 2)]
    outer_pairs = outer_pairs + [(b, a) for a, b in outer_pairs]
    scale = jnp.pad(element_scale, ((0, 0), (8, 120 - cols)))
    own = call(
        near_kernel, "near", shape((4 * cols + 16, width), BF), (fluid_state, fluid_rhs, scale)
    )
    inner = lax.ppermute(own, "slab", inner_pairs)
    outer = lax.ppermute(
        jnp.concatenate([own, inner[cols : 2 * cols]]), "slab", outer_pairs
    )
    strip = shape((STRIPS, width), BF)
    to_one, to_three, relay = call(
        strip_kernel,
        "strip",
        (strip, strip, shape((cols, width), BF)),
        (own, inner, outer, displacement),
        [pltpu.VMEM((2, STRIPS, width), F32)],
    )
    relayed = lax.ppermute(relay, "slab", inner_pairs)
    from_one = lax.ppermute(to_one, "patch", patch_pairs(1))
    from_three = lax.ppermute(to_three, "patch", [(1, 2), (2, 1)])
    wide = cols + 16
    state, message = call(
        sweep_kernel,
        "sweep",
        (shape(fluid_state.shape, F32), shape((slabs, owners, 8, 128), BF)),
        (
            fluid_state,
            fluid_rhs,
            scale,
            inner,
            outer,
            from_one,
            from_three,
            relayed,
            element_matrix,
            couple_x,
            couple_y,
            block_inverse,
            traction_map,
            slot_elem.reshape(1, slots),
            slot_point.reshape(1, slots),
            slot_count.reshape(1, owners),
        ),
        [
            pltpu.VMEM((8, wide, width), F32),
            pltpu.VMEM((6, wide, width), F32),
            pltpu.VMEM((6, wide, width), F32),
            pltpu.VMEM((6, wide, width), F32),
            pltpu.VMEM((8, 128), F32),
            pltpu.VMEM((2, STRIPS, width), F32),
            pltpu.VMEM((owners, 8, 128), F32),
        ],
    )
    kd = call(
        shell_kernel,
        "shell",
        shape(displacement.shape, F32),
        (from_one, from_three, displacement, stiffness),
        [pltpu.VMEM((3, displacement.shape[1] + 16, 128), F32)] * 2,
    )
    new, wall = exchange_and_relax(message, displacement, stiffness, kd)
    return state, new, wall


def solution(mesh):
    return jax.shard_map(
        shards,
        mesh=mesh,
        in_specs=(
            P("slab", "patch", None),
            P("slab", "patch", None),
            P("slab", "patch"),
            P(),
            P(),
            P(),
            P(),
            P(),
            P("slab", "patch", None),
            P("slab", "patch", None),
            P("slab", "patch", None),
            P(None, "patch", None),
            P("patch", None),
        ),
        out_specs=(
            P("slab", "patch", None),
            P(None, "patch", None),
            P(None, "slab", "patch", None),
        ),
        check_vma=False,
    )
```

```python
import jax
import jax.numpy as jnp
from jax import lax
from jax.experimental import pallas as pl
from jax.experimental.pallas import tpu as pltpu
from jax.sharding import PartitionSpec as P

SWEEPS = 3
BF = jnp.bfloat16
F32 = jnp.float32
I32 = jnp.int32
LIMIT = 48 << 20
EDGE = 40


def vmem(n):
    return [pl.BlockSpec(memory_space=pltpu.VMEM)] * n


def hbm(n):
    return [pl.BlockSpec(memory_space=pltpu.HBM)] * n


def iota(shape, dim):
    return lax.broadcasted_iota(I32, shape, dim)


def nt(a, b):
    return lax.dot_general(a, b, (((1,), (1,)), ((), ())), preferred_element_type=F32)


def slot_rows(final, tmap, elem, point, count_ref, rows_ref):
    owners = rows_ref.shape[0]
    slots = elem.shape[1]
    cap = slots // owners
    traction = nt(tmap, final).astype(BF)
    hot = (iota((final.shape[0], slots), 0) == elem).astype(F32).astype(BF)
    pull = jnp.dot(traction, hot, preferred_element_type=F32)
    slot = iota((1, slots), 1)
    owner = slot // cap
    limit = jnp.zeros((1, slots), I32)
    for k in range(owners):
        limit = jnp.where(owner == k, count_ref[0:1, k : k + 1], limit)
    live = (slot - owner * cap) < limit
    row = point // 128
    code = (128 + (point - row * 128)).astype(F32)
    for b in range(6):
        code = code * jnp.where((row >> b) & 1 == 1, F32(2.0 ** (2**b)), F32(1.0))
    code = jnp.where(live, code, 0.0)
    pull = jnp.where(live, pull, 0.0)
    for k in range(owners):
        for j in range(4):
            source = code if j == 3 else pull[j : j + 1]
            for h in range(2):
                start = k * cap + h * 128
                rows_ref[k, 2 * j + h : 2 * j + h + 1, :] = source[:, start : start + 128]


def decode(code):
    row = jnp.zeros(code.shape, F32)
    for b in (5, 4, 3, 2, 1, 0):
        big = code >= F32(128.0 * 2.0 ** (2**b))
        row = row + jnp.where(big, F32(2**b), 0.0)
        code = code * jnp.where(big, F32(2.0 ** -(2**b)), 1.0)
    return row, code - 128.0


def owner_kernel(
    got_ref, disp_ref, stiff_ref, kd_ref, new_ref, r0, r1, r2, r3, row_ref, lane_ref, hold_ref, sem
):
    replies = (r0, r1, r2, r3)
    sources = got_ref.shape[0]
    rows = disp_ref.shape[1]
    patch = lax.axis_index("patch")
    first = lax.axis_index("slab") * 4
    for h in range(2):
        row, lane = decode(got_ref[:, 6 + h, :].astype(F32))
        row_ref[h] = row
        lane_ref[h] = lane
    row_ids = iota((rows, 128), 0).astype(F32).astype(BF)
    lane_ids = iota((128, 128), 0).astype(F32).astype(BF)
    none = jnp.zeros((rows, 128), BF)
    ones, zeros = jnp.ones((128, 128), BF), jnp.zeros((128, 128), BF)
    total = jnp.zeros((3 * rows, 128), F32)
    group = 8
    for base in range(0, sources, group):
        row8 = [row_ref[h, base : base + group, :].astype(BF) for h in range(2)]
        lane8 = [lane_ref[h, base : base + group, :].astype(BF) for h in range(2)]
        for g in range(group):
            vals = got_ref[base + g]
            left, right = [], []
            for h in range(2):
                mask = row_ids == row8[h][g : g + 1]
                left.append(
                    jnp.concatenate(
                        [jnp.where(mask, vals[2 * c + h : 2 * c + h + 1], none) for c in range(3)],
                        axis=0,
                    )
                )
                right.append(jnp.where(lane_ids == lane8[h][g : g + 1], ones, zeros))
            total += nt(jnp.concatenate(left, axis=1), jnp.concatenate(right, axis=1))
    loads = total.reshape(3, rows, 128)
    new = disp_ref[...] + (loads - kd_ref[...]) / (36.0 * stiff_ref[...])[None]
    hold_ref[...] = new
    out = pltpu.make_async_copy(hold_ref, new_ref, sem)
    out.start()
    flat = new.reshape(3 * rows, 128)
    high = flat.astype(BF)
    rest1 = flat - high.astype(F32)
    mid = rest1.astype(BF)
    low = (rest1 - mid.astype(F32)).astype(BF)
    row_ids = iota((rows, 128), 0).astype(F32)
    for d in range(4):
        src = first + (patch ^ d)
        for h in range(2):
            row = row_ref[h, pl.ds(src, 1), :]
            lane = lane_ref[h, pl.ds(src, 1), :]
            hot = jnp.where(lane_ids == lane.astype(BF), ones, zeros)
            picked = jnp.dot(high, hot, preferred_element_type=F32)
            picked += jnp.dot(mid, hot, preferred_element_type=F32)
            picked += jnp.dot(low, hot, preferred_element_type=F32)
            mask = row_ids == row
            for c in range(3):
                part = jnp.where(mask, picked[c * rows : (c + 1) * rows], 0.0)
                replies[d][c : c + 1, h * 128 : (h + 1) * 128] = part.sum(axis=0, keepdims=True)
    out.wait()


def finish_kernel(r0, r1, r2, r3, out_ref):
    cap = r0.shape[1]
    patch = lax.axis_index("patch")
    for d, reply in enumerate((r0, r1, r2, r3)):
        start = pl.multiple_of((patch ^ d) * cap, cap)
        for c in range(3):
            out_ref[c, 0, :, pl.ds(start, cap)] = reply[c : c + 1, :]


def shell_kernel(one_ref, three_ref, disp_ref, stiff_ref, kd_ref, field_ref, bend_ref):
    rows = disp_ref.shape[1]
    patch = lax.axis_index("patch")
    top = patch > 0
    bottom = patch < 3
    even = patch % 2 == 0
    one, three = (
        ref[EDGE:, :128].astype(F32) + ref[EDGE:, 128:].astype(F32)
        for ref in (one_ref, three_ref)
    )
    above = jnp.where(even, three, one)
    below = jnp.where(even, one, three)
    field_ref[...] = jnp.zeros_like(field_ref)
    bend_ref[...] = jnp.zeros_like(bend_ref)
    field_ref[:, 8 : 8 + rows, :] = disp_ref[...]
    lane = iota((1, 1, 128), 2)

    def sides(x):
        left = jnp.where(lane == 0, 0.0, pltpu.roll(x, 1, 2))
        right = jnp.where(lane == 127, 0.0, pltpu.roll(x, 127, 2))
        return left + right

    for c in range(3):
        field_ref[c, 6:8, :] = jnp.where(top, above[2 * c : 2 * c + 2], 0.0)
        field_ref[c, 8 + rows : 10 + rows, :] = jnp.where(bottom, below[2 * c : 2 * c + 2], 0.0)
    mid = field_ref[:, 7 : 9 + rows, :]
    bend = 4.0 * mid - (
        field_ref[:, 6 : 8 + rows, :] + field_ref[:, 8 : 10 + rows, :] + sides(mid)
    )
    bend_ref[:, 7 : 9 + rows, :] = bend
    for c in range(3):
        bend_ref[c, 7:8, :] = jnp.where(top, bend_ref[c, 7:8, :], 0.0)
        bend_ref[c, 8 + rows : 9 + rows, :] = jnp.where(
            bottom, bend_ref[c, 8 + rows : 9 + rows, :], 0.0
        )
    mid = bend_ref[:, 8 : 8 + rows, :]
    again = 4.0 * mid - (
        bend_ref[:, 7 : 7 + rows, :] + bend_ref[:, 9 : 9 + rows, :] + sides(mid)
    )
    kd_ref[...] = stiff_ref[...][None] * (again + 4.0 * mid)


def params():
    return pltpu.CompilerParams(vmem_limit_bytes=LIMIT)


def patch_pairs(d):
    return [(p, p ^ d) for p in range(4)]


def exchange_and_relax(message, displacement, stiffness, kd):
    slabs, owners = lax.axis_size("slab"), lax.axis_size("patch")
    rows = displacement.shape[1]
    sources = slabs * owners
    got = lax.all_to_all(
        message.reshape(sources, 8, 128), ("slab", "patch"), 0, 0, tiled=True
    )
    reply = jax.ShapeDtypeStruct((8, 256), F32)
    new, *replies = pl.pallas_call(
        owner_kernel,
        out_shape=(jax.ShapeDtypeStruct(displacement.shape, F32),) + (reply,) * 4,
        in_specs=vmem(4),
        out_specs=hbm(1) + vmem(4),
        scratch_shapes=[
            pltpu.VMEM((2, sources, 128), F32),
            pltpu.VMEM((2, sources, 128), F32),
            pltpu.VMEM((3, rows, 128), F32),
            pltpu.SemaphoreType.DMA,
        ],
        compiler_params=params(),
        name="owner",
    )(got, displacement, stiffness, kd)
    back = [replies[0]] + [
        lax.ppermute(replies[d], "patch", patch_pairs(d)) for d in (1, 2, 3)
    ]
    wall = pl.pallas_call(
        finish_kernel,
        out_shape=jax.ShapeDtypeStruct((3, 1, 1, owners * 256), F32),
        in_specs=vmem(4),
        out_specs=pl.BlockSpec(memory_space=pltpu.VMEM),
        compiler_params=params(),
        name="finish",
    )(*back)
    return new, wall


def halves(value):
    high = value.astype(BF)
    low = (value - high.astype(F32)).astype(BF)
    return jnp.concatenate([high.astype(F32), low.astype(F32)], axis=1)


def lines_of(scale_ref, pad_ref):
    pad_ref[...] = jnp.zeros_like(pad_ref)
    pad_ref[0:2, 0 : scale_ref.shape[1]] = scale_ref[...]
    return pltpu.roll(pad_ref[...], 8, 1)


def near_kernel(
    state_hbm, rhs_hbm, scale_hbm, disp_hbm, own_ref, one_ref, three_ref,
    state_ref, rhs_ref, scale_ref, disp_ref, pad_ref, build_ref, sems,
):
    copies = [
        pltpu.make_async_copy(a, b, sems.at[i])
        for i, (a, b) in enumerate(
            (
                (scale_hbm, scale_ref),
                (state_hbm, state_ref),
                (rhs_hbm, rhs_ref),
                (disp_hbm, disp_ref),
            )
        )
    ]
    for copy in copies:
        copy.start()
    odd = lax.axis_index("slab") % 2
    even = lax.axis_index("patch") % 2 == 0
    cols = state_ref.shape[1]
    for copy in copies:
        copy.wait()
    for i, row in enumerate((odd, 1 - odd)):
        for part, ref in ((0, state_ref), (2, rhs_ref)):
            value = ref[row]
            at = part + i
            own_ref[at * cols : (at + 1) * cols, :] = value.astype(BF)
            low, high = value[0:8], value[cols - 8 : cols]
            build_ref[0, 8 * at : 8 * at + 8, :] = jnp.where(even, high, low)
            build_ref[1, 8 * at : 8 * at + 8, :] = jnp.where(even, low, high)
    lines = lines_of(scale_ref, pad_ref)
    flip = odd == 1
    first = jnp.where(flip, lines[1:2], lines[0:1])
    second = jnp.where(flip, lines[0:1], lines[1:2])
    pair = jnp.concatenate([halves(first), halves(second), jnp.zeros((6, 256), F32)], axis=0)
    own_ref[4 * cols : 4 * cols + 8, :] = pair.astype(BF)
    own_ref[4 * cols + 8 :, :] = jnp.zeros((8, 256), BF)
    for e in range(2):
        build_ref[e, 32:40, :] = pair
        build_ref[e, EDGE:, :] = jnp.zeros((8, 256), F32)
    rows = disp_ref.shape[1]
    for c in range(3):
        top = halves(disp_ref[c, 0:2, :])
        bottom = halves(disp_ref[c, rows - 2 : rows, :])
        at = EDGE + 2 * c
        build_ref[0, at : at + 2, :] = jnp.where(even, bottom, top)
        build_ref[1, at : at + 2, :] = jnp.where(even, top, bottom)
    one_ref[...] = build_ref[0].astype(BF)
    three_ref[...] = build_ref[1].astype(BF)


def sweep_kernel(
    state_ref,
    rhs_ref,
    scale_ref,
    inner_ref,
    outer_ref,
    one_ref,
    three_ref,
    relay_ref,
    matrix_ref,
    x_ref,
    y_ref,
    inverse_ref,
    tmap_ref,
    elem_hbm,
    point_hbm,
    count_hbm,
    out_hbm,
    message_ref,
    v_ref,
    r_ref,
    s_ref,
    i_ref,
    line_ref,
    rows_ref,
    elem_ref,
    point_ref,
    count_ref,
    out_ref,
    sems,
):
    copies = [
        pltpu.make_async_copy(a, b, sems.at[i])
        for i, (a, b) in enumerate(
            ((elem_hbm, elem_ref), (point_hbm, point_ref), (count_hbm, count_ref))
        )
    ]
    for copy in copies:
        copy.start()
    slab, patch = lax.axis_index("slab"), lax.axis_index("patch")
    last_slab, last_patch = lax.axis_size("slab") - 1, lax.axis_size("patch") - 1
    odd = slab % 2
    even = patch % 2 == 0
    cols, width = state_ref.shape[1], state_ref.shape[2]
    wide = cols + 16
    inside = (slab > 0) & (slab < last_slab)
    col = iota((wide, width), 0)
    valid = (col >= 8) & (col < 8 + cols)
    valid = valid | ((col < 8) & (patch > 0)) | ((col >= 8 + cols) & (patch < last_patch))
    edge = valid.astype(F32)
    keep = edge * inside.astype(F32)
    head = 5 * cols + 16
    strips = {
        0: (one_ref[0:EDGE], three_ref[0:EDGE]),
        1: (relay_ref[cols : cols + EDGE], relay_ref[cols + EDGE : cols + 2 * EDGE]),
        2: (outer_ref[head : head + EDGE], outer_ref[head + EDGE : head + 2 * EDGE]),
    }
    sides = {}
    for kind, pair in strips.items():
        one, three = (x.astype(F32) for x in pair)
        sides[kind] = (jnp.where(even, three, one), jnp.where(even, one, three))
    lane = iota((1, 128), 1)
    line_ref[...] = jnp.zeros_like(line_ref)
    line_ref[0:2, 0:cols] = scale_ref[...]
    exact = pltpu.roll(line_ref[...], 8, 1)
    table = ((2, 1), (2, 0), (0, 0), (0, 1), (1, 1), (1, 0))
    for r, (kind, i) in enumerate(table):
        if kind == 0:
            row = odd if i == 0 else 1 - odd
            v_ref[r + 1, 8 : 8 + cols, :] = state_ref[row]
            r_ref[r, 8 : 8 + cols, :] = rhs_ref[row]
            line = jnp.where(row == 1, exact[1:2], exact[0:1])
        else:
            ref = inner_ref if kind == 1 else outer_ref
            v_ref[r + 1, 8 : 8 + cols, :] = ref[i * cols : (i + 1) * cols, :].astype(F32)
            r_ref[r, 8 : 8 + cols, :] = ref[(i + 2) * cols : (i + 3) * cols, :].astype(F32)
            both = ref[4 * cols : 4 * cols + 16, :].astype(F32)[i : i + 1]
            line = both[:, :128] + both[:, 128:]
        for side, start in zip(sides[kind], (0, 8 + cols)):
            v_ref[r + 1, start : start + 8, :] = side[8 * i : 8 * i + 8]
            r_ref[r, start : start + 8, :] = side[16 + 8 * i : 24 + 8 * i]
            both = side[32 + i : 33 + i]
            far = pltpu.roll(both[:, :128] + both[:, 128:], 64, 1)
            here = (lane >= start) & (lane < start + 8)
            line = jnp.where(here, far, line)
        line_ref[r : r + 1, :] = jnp.where(line > 0.0, line, 1.0)
    line_ref[6:8, :] = jnp.ones((2, 128), F32)
    v_ref[0] = jnp.zeros((wide, width), F32)
    v_ref[7] = jnp.zeros((wide, width), F32)
    v_ref[0, 8 : 8 + cols, :] = outer_ref[4 * cols + 16 : head, :].astype(F32)
    v_ref[7, 8 : 8 + cols, :] = relay_ref[0:cols, :].astype(F32)
    for r in range(8):
        v_ref[r] = v_ref[r] * (keep if r < 3 else edge)
    lines = line_ref[...]
    columns = jnp.transpose(lines)
    inverses = jnp.transpose(1.0 / lines)
    for r in range(6):
        s_ref[r] = jnp.broadcast_to(columns[:wide, r : r + 1], (wide, width))
        i_ref[r] = jnp.broadcast_to(inverses[:wide, r : r + 1], (wide, width))
    for sweep in range(SWEEPS):
        a, b = 1 + sweep, 7 - sweep
        n = b - a
        near = v_ref[a - 1 : b + 1].astype(BF).astype(F32)
        mid = near[1 : n + 1]
        nx = (near[0:n] + near[2 : n + 2]).astype(BF)
        ny = (pltpu.roll(mid, 1, 1) + pltpu.roll(mid, wide - 1, 1)).astype(BF)
        flat = (n * wide, width)
        own = jnp.dot(mid.astype(BF).reshape(flat), matrix_ref[...], preferred_element_type=F32)
        side = jnp.dot(nx.reshape(flat), x_ref[...], preferred_element_type=F32)
        side += jnp.dot(ny.reshape(flat), y_ref[...], preferred_element_type=F32)
        scale = s_ref[a - 1 : b - 1].reshape(flat)
        rhs = r_ref[a - 1 : b - 1].reshape(flat)
        residue = (rhs - (scale * own - side)).astype(BF)
        update = jnp.dot(residue, inverse_ref[...], preferred_element_type=F32)
        update = update * i_ref[a - 1 : b - 1].reshape(flat)
        value = v_ref[a:b] + update.reshape(n, wide, width)
        for j in range(n):
            v_ref[a + j] = value[j] * (keep if a + j < 3 else edge)
    out_ref[odd] = v_ref[3, 8 : 8 + cols, :]
    out_ref[1 - odd] = v_ref[4, 8 : 8 + cols, :]
    out = pltpu.make_async_copy(out_ref, out_hbm, sems.at[3])
    out.start()
    final = out_ref[...].astype(BF).reshape(2 * cols, width)
    for copy in copies:
        copy.wait()
    slot_rows(final, tmap_ref[...], elem_ref[0], point_ref[0], count_ref.at[0], rows_ref)
    message_ref[...] = jnp.broadcast_to(rows_ref[...].astype(BF)[None], message_ref.shape)
    out.wait()


def call(kernel, name, out_shape, operands, scratch=(), in_specs=None, out_specs=None):
    return pl.pallas_call(
        kernel,
        out_shape=out_shape,
        in_specs=in_specs or vmem(len(operands)),
        out_specs=out_specs or jax.tree.map(lambda _: vmem(1)[0], out_shape),
        scratch_shapes=list(scratch),
        compiler_params=params(),
        name=name,
    )(*operands)


def shards(
    fluid_state,
    fluid_rhs,
    element_scale,
    element_matrix,
    couple_x,
    couple_y,
    block_inverse,
    traction_map,
    slot_elem,
    slot_point,
    slot_count,
    displacement,
    stiffness,
):
    cols, width = fluid_state.shape[1:]
    slots = slot_elem.shape[2]
    slabs, owners = lax.axis_size("slab"), lax.axis_size("patch")
    shape = jax.ShapeDtypeStruct
    inner_pairs = [(s, s ^ 1) for s in range(slabs)]
    outer_pairs = [(s, s + 1) for s in range(1, slabs - 1, 2)]
    outer_pairs = outer_pairs + [(b, a) for a, b in outer_pairs]
    strip = shape((EDGE + 8, width), BF)
    own, to_one, to_three = call(
        near_kernel,
        "near",
        (shape((4 * cols + 16, width), BF), strip, strip),
        (fluid_state, fluid_rhs, element_scale, displacement),
        [
            pltpu.VMEM(fluid_state.shape, F32),
            pltpu.VMEM(fluid_rhs.shape, F32),
            pltpu.VMEM(element_scale.shape, F32),
            pltpu.VMEM(displacement.shape, F32),
            pltpu.VMEM((8, 128), F32),
            pltpu.VMEM((2, EDGE + 8, width), F32),
            pltpu.SemaphoreType.DMA((4,)),
        ],
        in_specs=hbm(4),
    )
    inner = lax.ppermute(own, "slab", inner_pairs)
    from_three = lax.ppermute(to_three, "patch", [(1, 2), (2, 1)])
    from_one = lax.ppermute(to_one, "patch", patch_pairs(1))
    strips = [from_one[:EDGE], from_three[:EDGE]]
    outer = lax.ppermute(
        jnp.concatenate([own, inner[cols : 2 * cols]] + strips), "slab", outer_pairs
    )
    relay = lax.ppermute(jnp.concatenate([outer[:cols]] + strips), "slab", inner_pairs)
    wide = cols + 16
    state, message = call(
        sweep_kernel,
        "sweep",
        (shape(fluid_state.shape, F32), shape((slabs, owners, 8, 128), BF)),
        (
            fluid_state,
            fluid_rhs,
            element_scale,
            inner,
            outer,
            from_one,
            from_three,
            relay,
            element_matrix,
            couple_x,
            couple_y,
            block_inverse,
            traction_map,
            slot_elem,
            slot_point,
            slot_count,
        ),
        [
            pltpu.VMEM((8, wide, width), F32),
            pltpu.VMEM((6, wide, width), F32),
            pltpu.VMEM((6, wide, width), F32),
            pltpu.VMEM((6, wide, width), F32),
            pltpu.VMEM((8, 128), F32),
            pltpu.VMEM((owners, 8, 128), F32),
            pltpu.VMEM((1, 1, slots), I32),
            pltpu.VMEM((1, 1, slots), I32),
            pltpu.VMEM((1, 1, owners), I32),
            pltpu.VMEM(fluid_state.shape, F32),
            pltpu.SemaphoreType.DMA((4,)),
        ],
        in_specs=vmem(13) + hbm(3),
        out_specs=tuple(hbm(1) + vmem(1)),
    )
    kd = call(
        shell_kernel,
        "shell",
        shape(displacement.shape, F32),
        (from_one, from_three, displacement, stiffness),
        [pltpu.VMEM((3, displacement.shape[1] + 16, 128), F32)] * 2,
    )
    new, wall = exchange_and_relax(message, displacement, stiffness, kd)
    return state, new, wall


def solution(mesh):
    return jax.shard_map(
        shards,
        mesh=mesh,
        in_specs=(
            P("slab", "patch", None),
            P("slab", "patch", None),
            P("slab", "patch"),
            P(),
            P(),
            P(),
            P(),
            P(),
            P("slab", "patch", None),
            P("slab", "patch", None),
            P("slab", "patch", None),
            P(None, "patch", None),
            P("patch", None),
        ),
        out_specs=(
            P("slab", "patch", None),
            P(None, "patch", None),
            P(None, "slab", "patch", None),
        ),
        check_vma=False,
    )
```

```python
import jax
import jax.numpy as jnp
from jax import lax
from jax.experimental import pallas as pl
from jax.experimental.pallas import tpu as pltpu
from jax.sharding import PartitionSpec as P

SWEEPS = 3
BF = jnp.bfloat16
F32 = jnp.float32
I32 = jnp.int32
LIMIT = 48 << 20
EDGE = 24


def vmem(n):
    return [pl.BlockSpec(memory_space=pltpu.VMEM)] * n


def hbm(n):
    return [pl.BlockSpec(memory_space=pltpu.HBM)] * n


def iota(shape, dim):
    return lax.broadcasted_iota(I32, shape, dim)


def nt(a, b):
    return lax.dot_general(a, b, (((1,), (1,)), ((), ())), preferred_element_type=F32)


def slot_rows(final, tmap, elem, point, count_ref, rows_ref):
    owners = rows_ref.shape[0]
    slots = elem.shape[1]
    cap = slots // owners
    traction = nt(tmap, final).astype(BF)
    hot = (iota((final.shape[0], slots), 0) == elem).astype(F32).astype(BF)
    pull = jnp.dot(traction, hot, preferred_element_type=F32)
    slot = iota((1, slots), 1)
    owner = slot // cap
    limit = jnp.zeros((1, slots), I32)
    for k in range(owners):
        limit = jnp.where(owner == k, count_ref[0:1, k : k + 1], limit)
    live = (slot - owner * cap) < limit
    row = point // 128
    code = (128 + (point - row * 128)).astype(F32)
    for b in range(6):
        code = code * jnp.where((row >> b) & 1 == 1, F32(2.0 ** (2**b)), F32(1.0))
    code = jnp.where(live, code, 0.0)
    pull = jnp.where(live, pull, 0.0)
    for k in range(owners):
        for j in range(4):
            source = code if j == 3 else pull[j : j + 1]
            for h in range(2):
                start = k * cap + h * 128
                rows_ref[k, 2 * j + h : 2 * j + h + 1, :] = source[:, start : start + 128]


def decode(code):
    row = jnp.zeros(code.shape, F32)
    for b in (5, 4, 3, 2, 1, 0):
        big = code >= F32(128.0 * 2.0 ** (2**b))
        row = row + jnp.where(big, F32(2**b), 0.0)
        code = code * jnp.where(big, F32(2.0 ** -(2**b)), 1.0)
    return row, code - 128.0


def owner_kernel(
    got_ref, disp_ref, stiff_ref, kd_ref, new_ref, r0, r1, r2, r3, row_ref, lane_ref, hold_ref, sem
):
    replies = (r0, r1, r2, r3)
    sources = got_ref.shape[0]
    rows = disp_ref.shape[1]
    patch = lax.axis_index("patch")
    first = lax.axis_index("slab") * 4
    for h in range(2):
        row, lane = decode(got_ref[:, 6 + h, :].astype(F32))
        row_ref[h] = row
        lane_ref[h] = lane
    row_ids = iota((rows, 128), 0).astype(F32).astype(BF)
    lane_ids = iota((128, 128), 0).astype(F32).astype(BF)
    none = jnp.zeros((rows, 128), BF)
    ones, zeros = jnp.ones((128, 128), BF), jnp.zeros((128, 128), BF)
    total = jnp.zeros((3 * rows, 128), F32)
    group = 8
    for base in range(0, sources, group):
        row8 = [row_ref[h, base : base + group, :].astype(BF) for h in range(2)]
        lane8 = [lane_ref[h, base : base + group, :].astype(BF) for h in range(2)]
        for g in range(group):
            vals = got_ref[base + g]
            left, right = [], []
            for h in range(2):
                mask = row_ids == row8[h][g : g + 1]
                left.append(
                    jnp.concatenate(
                        [jnp.where(mask, vals[2 * c + h : 2 * c + h + 1], none) for c in range(3)],
                        axis=0,
                    )
                )
                right.append(jnp.where(lane_ids == lane8[h][g : g + 1], ones, zeros))
            total += nt(jnp.concatenate(left, axis=1), jnp.concatenate(right, axis=1))
    loads = total.reshape(3, rows, 128)
    new = disp_ref[...] + (loads - kd_ref[...]) / (36.0 * stiff_ref[...])[None]
    hold_ref[...] = new
    out = pltpu.make_async_copy(hold_ref, new_ref, sem)
    out.start()
    flat = new.reshape(3 * rows, 128)
    high = flat.astype(BF)
    low = (flat - high.astype(F32)).astype(BF)
    row_ids = iota((rows, 128), 0).astype(F32)
    for d in range(4):
        src = first + (patch ^ d)
        for h in range(2):
            row = row_ref[h, pl.ds(src, 1), :]
            lane = lane_ref[h, pl.ds(src, 1), :]
            hot = jnp.where(lane_ids == lane.astype(BF), ones, zeros)
            picked = jnp.dot(high, hot, preferred_element_type=F32)
            picked += jnp.dot(low, hot, preferred_element_type=F32)
            mask = row_ids == row
            for c in range(3):
                part = jnp.where(mask, picked[c * rows : (c + 1) * rows], 0.0)
                replies[d][c : c + 1, h * 128 : (h + 1) * 128] = part.sum(axis=0, keepdims=True)
    out.wait()


def finish_kernel(r0, r1, r2, r3, out_ref):
    cap = r0.shape[1]
    patch = lax.axis_index("patch")
    for d, reply in enumerate((r0, r1, r2, r3)):
        start = pl.multiple_of((patch ^ d) * cap, cap)
        for c in range(3):
            out_ref[c, 0, :, pl.ds(start, cap)] = reply[c : c + 1, :]


def shell_kernel(one_ref, three_ref, disp_ref, stiff_ref, kd_ref, field_ref, bend_ref):
    rows = disp_ref.shape[1]
    patch = lax.axis_index("patch")
    top = patch > 0
    bottom = patch < 3
    even = patch % 2 == 0
    one, three = (
        ref[EDGE:, :128].astype(F32) + ref[EDGE:, 128:].astype(F32)
        for ref in (one_ref, three_ref)
    )
    above = jnp.where(even, three, one)
    below = jnp.where(even, one, three)
    field_ref[...] = jnp.zeros_like(field_ref)
    bend_ref[...] = jnp.zeros_like(bend_ref)
    field_ref[:, 8 : 8 + rows, :] = disp_ref[...]
    lane = iota((1, 1, 128), 2)

    def sides(x):
        left = jnp.where(lane == 0, 0.0, pltpu.roll(x, 1, 2))
        right = jnp.where(lane == 127, 0.0, pltpu.roll(x, 127, 2))
        return left + right

    for c in range(3):
        field_ref[c, 6:8, :] = jnp.where(top, above[2 * c : 2 * c + 2], 0.0)
        field_ref[c, 8 + rows : 10 + rows, :] = jnp.where(bottom, below[2 * c : 2 * c + 2], 0.0)
    mid = field_ref[:, 7 : 9 + rows, :]
    bend = 4.0 * mid - (
        field_ref[:, 6 : 8 + rows, :] + field_ref[:, 8 : 10 + rows, :] + sides(mid)
    )
    bend_ref[:, 7 : 9 + rows, :] = bend
    for c in range(3):
        bend_ref[c, 7:8, :] = jnp.where(top, bend_ref[c, 7:8, :], 0.0)
        bend_ref[c, 8 + rows : 9 + rows, :] = jnp.where(
            bottom, bend_ref[c, 8 + rows : 9 + rows, :], 0.0
        )
    mid = bend_ref[:, 8 : 8 + rows, :]
    again = 4.0 * mid - (
        bend_ref[:, 7 : 7 + rows, :] + bend_ref[:, 9 : 9 + rows, :] + sides(mid)
    )
    kd_ref[...] = stiff_ref[...][None] * (again + 4.0 * mid)


def params():
    return pltpu.CompilerParams(vmem_limit_bytes=LIMIT)


def patch_pairs(d):
    return [(p, p ^ d) for p in range(4)]


def exchange_and_relax(message, displacement, stiffness, kd):
    slabs, owners = lax.axis_size("slab"), lax.axis_size("patch")
    rows = displacement.shape[1]
    sources = slabs * owners
    got = lax.all_to_all(
        message.reshape(sources, 8, 128), ("slab", "patch"), 0, 0, tiled=True
    )
    reply = jax.ShapeDtypeStruct((8, 256), F32)
    new, *replies = pl.pallas_call(
        owner_kernel,
        out_shape=(jax.ShapeDtypeStruct(displacement.shape, F32),) + (reply,) * 4,
        in_specs=vmem(4),
        out_specs=hbm(1) + vmem(4),
        scratch_shapes=[
            pltpu.VMEM((2, sources, 128), F32),
            pltpu.VMEM((2, sources, 128), F32),
            pltpu.VMEM((3, rows, 128), F32),
            pltpu.SemaphoreType.DMA,
        ],
        compiler_params=params(),
        name="owner",
    )(got, displacement, stiffness, kd)
    back = [replies[0]] + [
        lax.ppermute(replies[d], "patch", patch_pairs(d)) for d in (1, 2, 3)
    ]
    wall = pl.pallas_call(
        finish_kernel,
        out_shape=jax.ShapeDtypeStruct((3, 1, 1, owners * 256), F32),
        in_specs=vmem(4),
        out_specs=pl.BlockSpec(memory_space=pltpu.VMEM),
        compiler_params=params(),
        name="finish",
    )(*back)
    return new, wall


def halves(value):
    high = value.astype(BF)
    low = (value - high.astype(F32)).astype(BF)
    return jnp.concatenate([high.astype(F32), low.astype(F32)], axis=1)


def lines_of(scale_ref, pad_ref):
    pad_ref[...] = jnp.zeros_like(pad_ref)
    pad_ref[0:2, 0 : scale_ref.shape[1]] = scale_ref[...]
    return pltpu.roll(pad_ref[...], 8, 1)


def near_kernel(
    state_hbm, rhs_hbm, scale_hbm, disp_hbm, near_ref, own_ref, one_ref, three_ref,
    state_ref, rhs_ref, scale_ref, disp_ref, pad_ref, build_ref, sems,
):
    copies = [
        pltpu.make_async_copy(a, b, sems.at[i])
        for i, (a, b) in enumerate(
            (
                (scale_hbm, scale_ref),
                (state_hbm, state_ref),
                (rhs_hbm, rhs_ref),
                (disp_hbm, disp_ref),
            )
        )
    ]
    for copy in copies:
        copy.start()
    odd = lax.axis_index("slab") % 2
    even = lax.axis_index("patch") % 2 == 0
    cols = state_ref.shape[1]
    for copy in copies:
        copy.wait()
    for i, row in enumerate((odd, 1 - odd)):
        for part, ref in ((0, state_ref), (2, rhs_ref)):
            value = ref[row]
            at = part + i
            own_ref[at * cols : (at + 1) * cols, :] = value.astype(BF)
            low, high = value[0:4], value[cols - 4 : cols]
            build_ref[0, 4 * at : 4 * at + 4, :] = jnp.where(even, high, low)
            build_ref[1, 4 * at : 4 * at + 4, :] = jnp.where(even, low, high)
    near_ref[...] = state_ref[1 - odd].astype(BF)
    lines = lines_of(scale_ref, pad_ref)
    flip = odd == 1
    first = jnp.where(flip, lines[1:2], lines[0:1])
    second = jnp.where(flip, lines[0:1], lines[1:2])
    pair = jnp.concatenate([halves(first), halves(second), jnp.zeros((6, 256), F32)], axis=0)
    own_ref[4 * cols :, :] = pair.astype(BF)
    for e in range(2):
        build_ref[e, 16:24, :] = pair
        build_ref[e, EDGE:, :] = jnp.zeros((8, 256), F32)
    rows = disp_ref.shape[1]
    for c in range(3):
        top = halves(disp_ref[c, 0:2, :])
        bottom = halves(disp_ref[c, rows - 2 : rows, :])
        at = EDGE + 2 * c
        build_ref[0, at : at + 2, :] = jnp.where(even, bottom, top)
        build_ref[1, at : at + 2, :] = jnp.where(even, top, bottom)
    one_ref[...] = build_ref[0].astype(BF)
    three_ref[...] = build_ref[1].astype(BF)


def sweep_kernel(
    state_ref,
    rhs_ref,
    scale_ref,
    near_ref,
    inner_ref,
    outer_ref,
    one_ref,
    three_ref,
    relay_ref,
    matrix_ref,
    x_ref,
    y_ref,
    inverse_ref,
    tmap_ref,
    elem_hbm,
    point_hbm,
    count_hbm,
    out_hbm,
    message_ref,
    v_ref,
    r_ref,
    s_ref,
    i_ref,
    line_ref,
    rows_ref,
    elem_ref,
    point_ref,
    count_ref,
    out_ref,
    sems,
):
    copies = [
        pltpu.make_async_copy(a, b, sems.at[i])
        for i, (a, b) in enumerate(
            ((elem_hbm, elem_ref), (point_hbm, point_ref), (count_hbm, count_ref))
        )
    ]
    for copy in copies:
        copy.start()
    slab, patch = lax.axis_index("slab"), lax.axis_index("patch")
    last_slab, last_patch = lax.axis_size("slab") - 1, lax.axis_size("patch") - 1
    odd = slab % 2
    even = patch % 2 == 0
    cols, width = state_ref.shape[1], state_ref.shape[2]
    wide = cols + 16
    inside = (slab > 0) & (slab < last_slab)
    col = iota((wide, width), 0)
    valid = (col >= 8) & (col < 8 + cols)
    valid = valid | ((col < 8) & (patch > 0)) | ((col >= 8 + cols) & (patch < last_patch))
    edge = valid.astype(F32)
    keep = edge * inside.astype(F32)
    v_ref[:, 0:8, :] = jnp.zeros((8, 8, width), F32)
    v_ref[:, 8 + cols :, :] = jnp.zeros((8, 8, width), F32)
    r_ref[:, 0:8, :] = jnp.zeros((6, 8, width), F32)
    r_ref[:, 8 + cols :, :] = jnp.zeros((6, 8, width), F32)
    head = 5 * cols + 8
    tail = 3 * cols + 8
    strips = {
        0: (one_ref[0:EDGE], three_ref[0:EDGE]),
        1: (inner_ref[tail : tail + EDGE], inner_ref[tail + EDGE : tail + 2 * EDGE]),
        2: (outer_ref[head : head + EDGE], outer_ref[head + EDGE : head + 2 * EDGE]),
    }
    sides = {}
    for kind, pair in strips.items():
        one, three = (x.astype(F32) for x in pair)
        sides[kind] = (jnp.where(even, three, one), jnp.where(even, one, three))
    lane = iota((1, 128), 1)
    line_ref[...] = jnp.zeros_like(line_ref)
    line_ref[0:2, 0:cols] = scale_ref[...]
    exact = pltpu.roll(line_ref[...], 8, 1)
    table = ((2, 1), (2, 0), (0, 0), (0, 1), (1, 1), (1, 0))
    for r, (kind, i) in enumerate(table):
        if kind == 0:
            row = odd if i == 0 else 1 - odd
            v_ref[r + 1, 8 : 8 + cols, :] = state_ref[row]
            r_ref[r, 8 : 8 + cols, :] = rhs_ref[row]
            line = jnp.where(row == 1, exact[1:2], exact[0:1])
        else:
            if kind == 1:
                value = near_ref[...] if i == 1 else inner_ref[0:cols]
                ref, at = inner_ref, (i + 1) * cols
            else:
                value = outer_ref[i * cols : (i + 1) * cols]
                ref, at = outer_ref, (i + 2) * cols
            v_ref[r + 1, 8 : 8 + cols, :] = value.astype(F32)
            r_ref[r, 8 : 8 + cols, :] = ref[at : at + cols, :].astype(F32)
            below = (3 if kind == 1 else 4) * cols
            both = ref[below : below + 8, :].astype(F32)[i : i + 1]
            line = both[:, :128] + both[:, 128:]
        for side, start in zip(sides[kind], (4, 8 + cols)):
            v_ref[r + 1, start : start + 4, :] = side[4 * i : 4 * i + 4]
            r_ref[r, start : start + 4, :] = side[8 + 4 * i : 12 + 4 * i]
            both = side[16 + i : 17 + i]
            far = pltpu.roll(both[:, :128] + both[:, 128:], 64, 1)
            here = (lane >= start) & (lane < start + 4)
            line = jnp.where(here, far, line)
        line_ref[r : r + 1, :] = jnp.where(line > 0.0, line, 1.0)
    line_ref[6:8, :] = jnp.ones((2, 128), F32)
    v_ref[0, 8 : 8 + cols, :] = outer_ref[4 * cols + 8 : head, :].astype(F32)
    v_ref[7, 8 : 8 + cols, :] = relay_ref[...].astype(F32)
    for r in range(8):
        v_ref[r] = v_ref[r] * (keep if r < 3 else edge)
    lines = line_ref[...]
    columns = jnp.transpose(lines)
    inverses = jnp.transpose(1.0 / lines)
    for r in range(6):
        s_ref[r] = jnp.broadcast_to(columns[:wide, r : r + 1], (wide, width))
        i_ref[r] = jnp.broadcast_to(inverses[:wide, r : r + 1], (wide, width))
    for sweep in range(SWEEPS):
        a, b = 1 + sweep, 7 - sweep
        n = b - a
        near = v_ref[a - 1 : b + 1].astype(BF).astype(F32)
        mid = near[1 : n + 1]
        nx = (near[0:n] + near[2 : n + 2]).astype(BF)
        ny = (pltpu.roll(mid, 1, 1) + pltpu.roll(mid, wide - 1, 1)).astype(BF)
        flat = (n * wide, width)
        own = jnp.dot(mid.astype(BF).reshape(flat), matrix_ref[...], preferred_element_type=F32)
        side = jnp.dot(nx.reshape(flat), x_ref[...], preferred_element_type=F32)
        side += jnp.dot(ny.reshape(flat), y_ref[...], preferred_element_type=F32)
        scale = s_ref[a - 1 : b - 1].reshape(flat)
        rhs = r_ref[a - 1 : b - 1].reshape(flat)
        residue = (rhs - (scale * own - side)).astype(BF)
        update = jnp.dot(residue, inverse_ref[...], preferred_element_type=F32)
        update = update * i_ref[a - 1 : b - 1].reshape(flat)
        value = v_ref[a:b] + update.reshape(n, wide, width)
        for j in range(n):
            v_ref[a + j] = value[j] * (keep if a + j < 3 else edge)
    out_ref[odd] = v_ref[3, 8 : 8 + cols, :]
    out_ref[1 - odd] = v_ref[4, 8 : 8 + cols, :]
    out = pltpu.make_async_copy(out_ref, out_hbm, sems.at[3])
    out.start()
    final = out_ref[...].astype(BF).reshape(2 * cols, width)
    for copy in copies:
        copy.wait()
    slot_rows(final, tmap_ref[...], elem_ref[0], point_ref[0], count_ref.at[0], rows_ref)
    message_ref[...] = jnp.broadcast_to(rows_ref[...].astype(BF)[None], message_ref.shape)
    out.wait()


def call(kernel, name, out_shape, operands, scratch=(), in_specs=None, out_specs=None):
    return pl.pallas_call(
        kernel,
        out_shape=out_shape,
        in_specs=in_specs or vmem(len(operands)),
        out_specs=out_specs or jax.tree.map(lambda _: vmem(1)[0], out_shape),
        scratch_shapes=list(scratch),
        compiler_params=params(),
        name=name,
    )(*operands)


def shards(
    fluid_state,
    fluid_rhs,
    element_scale,
    element_matrix,
    couple_x,
    couple_y,
    block_inverse,
    traction_map,
    slot_elem,
    slot_point,
    slot_count,
    displacement,
    stiffness,
):
    cols, width = fluid_state.shape[1:]
    slots = slot_elem.shape[2]
    slabs, owners = lax.axis_size("slab"), lax.axis_size("patch")
    shape = jax.ShapeDtypeStruct
    inner_pairs = [(s, s ^ 1) for s in range(slabs)]
    outer_pairs = [(s, s + 1) for s in range(1, slabs - 1, 2)]
    outer_pairs = outer_pairs + [(b, a) for a, b in outer_pairs]
    strip = shape((EDGE + 8, width), BF)
    near, own, to_one, to_three = call(
        near_kernel,
        "near",
        (shape((cols, width), BF), shape((4 * cols + 8, width), BF), strip, strip),
        tuple(
            pltpu.with_memory_space_constraint(x, pltpu.HBM)
            for x in (fluid_state, fluid_rhs, element_scale, displacement)
        ),
        [
            pltpu.VMEM(fluid_state.shape, F32),
            pltpu.VMEM(fluid_rhs.shape, F32),
            pltpu.VMEM(element_scale.shape, F32),
            pltpu.VMEM(displacement.shape, F32),
            pltpu.VMEM((8, 128), F32),
            pltpu.VMEM((2, EDGE + 8, width), F32),
            pltpu.SemaphoreType.DMA((4,)),
        ],
        in_specs=hbm(4),
    )
    inner_near = lax.ppermute(near, "slab", inner_pairs)
    from_three = lax.ppermute(to_three, "patch", [(1, 2), (2, 1)])
    from_one = lax.ppermute(to_one, "patch", patch_pairs(1))
    strips = [from_one[:EDGE], from_three[:EDGE]]
    outer = lax.ppermute(jnp.concatenate([own, inner_near] + strips), "slab", outer_pairs)
    inner = lax.ppermute(
        jnp.concatenate([own[:cols], own[2 * cols :]] + strips), "slab", inner_pairs
    )
    relay = lax.ppermute(outer[:cols], "slab", inner_pairs)
    wide = cols + 16
    state, message = call(
        sweep_kernel,
        "sweep",
        (shape(fluid_state.shape, F32), shape((slabs, owners, 8, 128), BF)),
        (
            fluid_state,
            fluid_rhs,
            element_scale,
            inner_near,
            inner,
            outer,
            from_one,
            from_three,
            relay,
            element_matrix,
            couple_x,
            couple_y,
            block_inverse,
            traction_map,
            slot_elem,
            slot_point,
            slot_count,
        ),
        [
            pltpu.VMEM((8, wide, width), F32),
            pltpu.VMEM((6, wide, width), F32),
            pltpu.VMEM((6, wide, width), F32),
            pltpu.VMEM((6, wide, width), F32),
            pltpu.VMEM((8, 128), F32),
            pltpu.VMEM((owners, 8, 128), F32),
            pltpu.VMEM((1, 1, slots), I32),
            pltpu.VMEM((1, 1, slots), I32),
            pltpu.VMEM((1, 1, owners), I32),
            pltpu.VMEM(fluid_state.shape, F32),
            pltpu.SemaphoreType.DMA((4,)),
        ],
        in_specs=vmem(14) + hbm(3),
        out_specs=tuple(hbm(1) + vmem(1)),
    )
    kd = call(
        shell_kernel,
        "shell",
        shape(displacement.shape, F32),
        (from_one, from_three, displacement, stiffness),
        [pltpu.VMEM((3, displacement.shape[1] + 16, 128), F32)] * 2,
    )
    new, wall = exchange_and_relax(message, displacement, stiffness, kd)
    return state, new, wall


def solution(mesh):
    return jax.shard_map(
        shards,
        mesh=mesh,
        in_specs=(
            P("slab", "patch", None),
            P("slab", "patch", None),
            P("slab", "patch"),
            P(),
            P(),
            P(),
            P(),
            P(),
            P("slab", "patch", None),
            P("slab", "patch", None),
            P("slab", "patch", None),
            P(None, "patch", None),
            P("patch", None),
        ),
        out_specs=(
            P("slab", "patch", None),
            P(None, "patch", None),
            P(None, "slab", "patch", None),
        ),
        check_vma=False,
    )
```

```python
import jax
import jax.numpy as jnp
from jax import lax
from jax.experimental import pallas as pl
from jax.experimental.pallas import tpu as pltpu
from jax.sharding import PartitionSpec as P

SWEEPS = 3
BF = jnp.bfloat16
F32 = jnp.float32
I32 = jnp.int32
LIMIT = 48 << 20
EDGE = 24


def vmem(n):
    return [pl.BlockSpec(memory_space=pltpu.VMEM)] * n


def hbm(n):
    return [pl.BlockSpec(memory_space=pltpu.HBM)] * n


def iota(shape, dim):
    return lax.broadcasted_iota(I32, shape, dim)


def nt(a, b):
    return lax.dot_general(a, b, (((1,), (1,)), ((), ())), preferred_element_type=F32)


def slot_rows(final, tmap, elem, point, count_ref, rows_ref):
    owners = rows_ref.shape[0]
    slots = elem.shape[1]
    cap = slots // owners
    traction = nt(tmap, final).astype(BF)
    hot = (iota((final.shape[0], slots), 0) == elem).astype(F32).astype(BF)
    pull = jnp.dot(traction, hot, preferred_element_type=F32)
    slot = iota((1, slots), 1)
    owner = slot // cap
    limit = jnp.zeros((1, slots), I32)
    for k in range(owners):
        limit = jnp.where(owner == k, count_ref[0:1, k : k + 1], limit)
    live = (slot - owner * cap) < limit
    row = point // 128
    code = (128 + (point - row * 128)).astype(F32)
    for b in range(6):
        code = code * jnp.where((row >> b) & 1 == 1, F32(2.0 ** (2**b)), F32(1.0))
    code = jnp.where(live, code, 0.0)
    pull = jnp.where(live, pull, 0.0)
    for k in range(owners):
        for j in range(4):
            source = code if j == 3 else pull[j : j + 1]
            for h in range(2):
                start = k * cap + h * 128
                rows_ref[k, 2 * j + h : 2 * j + h + 1, :] = source[:, start : start + 128]


def decode(code):
    row = jnp.zeros(code.shape, F32)
    for b in (5, 4, 3, 2, 1, 0):
        big = code >= F32(128.0 * 2.0 ** (2**b))
        row = row + jnp.where(big, F32(2**b), 0.0)
        code = code * jnp.where(big, F32(2.0 ** -(2**b)), 1.0)
    return row, code - 128.0


def owner_kernel(
    got_ref, disp_ref, stiff_ref, kd_ref, new_ref, r0, r1, r2, r3, row_ref, lane_ref, hold_ref, sem
):
    replies = (r0, r1, r2, r3)
    sources = got_ref.shape[0]
    rows = disp_ref.shape[1]
    patch = lax.axis_index("patch")
    first = lax.axis_index("slab") * 4
    for h in range(2):
        row, lane = decode(got_ref[:, 6 + h, :].astype(F32))
        row_ref[h] = row
        lane_ref[h] = lane
    row_ids = iota((rows, 128), 0).astype(F32).astype(BF)
    lane_ids = iota((128, 128), 0).astype(F32).astype(BF)
    none = jnp.zeros((rows, 128), BF)
    ones, zeros = jnp.ones((128, 128), BF), jnp.zeros((128, 128), BF)
    total = jnp.zeros((3 * rows, 128), F32)
    group = 8
    for base in range(0, sources, group):
        row8 = [row_ref[h, base : base + group, :].astype(BF) for h in range(2)]
        lane8 = [lane_ref[h, base : base + group, :].astype(BF) for h in range(2)]
        for g in range(group):
            vals = got_ref[base + g]
            left, right = [], []
            for h in range(2):
                mask = row_ids == row8[h][g : g + 1]
                left.append(
                    jnp.concatenate(
                        [jnp.where(mask, vals[2 * c + h : 2 * c + h + 1], none) for c in range(3)],
                        axis=0,
                    )
                )
                right.append(jnp.where(lane_ids == lane8[h][g : g + 1], ones, zeros))
            total += nt(jnp.concatenate(left, axis=1), jnp.concatenate(right, axis=1))
    loads = total.reshape(3, rows, 128)
    new = disp_ref[...] + (loads - kd_ref[...]) / (36.0 * stiff_ref[...])[None]
    hold_ref[...] = new
    out = pltpu.make_async_copy(hold_ref, new_ref, sem)
    out.start()
    flat = new.reshape(3 * rows, 128)
    high = flat.astype(BF)
    low = (flat - high.astype(F32)).astype(BF)
    row_ids = iota((rows, 128), 0).astype(F32)
    for d in range(4):
        src = first + (patch ^ d)
        for h in range(2):
            row = row_ref[h, pl.ds(src, 1), :]
            lane = lane_ref[h, pl.ds(src, 1), :]
            hot = jnp.where(lane_ids == lane.astype(BF), ones, zeros)
            picked = jnp.dot(high, hot, preferred_element_type=F32)
            picked += jnp.dot(low, hot, preferred_element_type=F32)
            mask = row_ids == row
            for c in range(3):
                part = jnp.where(mask, picked[c * rows : (c + 1) * rows], 0.0)
                replies[d][c : c + 1, h * 128 : (h + 1) * 128] = part.sum(axis=0, keepdims=True)
    out.wait()


def finish_kernel(r0, r1, r2, r3, out_ref):
    cap = r0.shape[1]
    patch = lax.axis_index("patch")
    for d, reply in enumerate((r0, r1, r2, r3)):
        start = pl.multiple_of((patch ^ d) * cap, cap)
        for c in range(3):
            out_ref[c, 0, :, pl.ds(start, cap)] = reply[c : c + 1, :]


def shell_kernel(one_ref, three_ref, disp_ref, stiff_ref, kd_ref, field_ref, bend_ref):
    rows = disp_ref.shape[1]
    patch = lax.axis_index("patch")
    top = patch > 0
    bottom = patch < 3
    even = patch % 2 == 0
    one, three = (
        ref[EDGE:, :128].astype(F32) + ref[EDGE:, 128:].astype(F32)
        for ref in (one_ref, three_ref)
    )
    above = jnp.where(even, three, one)
    below = jnp.where(even, one, three)
    field_ref[...] = jnp.zeros_like(field_ref)
    bend_ref[...] = jnp.zeros_like(bend_ref)
    field_ref[:, 8 : 8 + rows, :] = disp_ref[...]
    lane = iota((1, 1, 128), 2)

    def sides(x):
        left = jnp.where(lane == 0, 0.0, pltpu.roll(x, 1, 2))
        right = jnp.where(lane == 127, 0.0, pltpu.roll(x, 127, 2))
        return left + right

    for c in range(3):
        field_ref[c, 6:8, :] = jnp.where(top, above[2 * c : 2 * c + 2], 0.0)
        field_ref[c, 8 + rows : 10 + rows, :] = jnp.where(bottom, below[2 * c : 2 * c + 2], 0.0)
    mid = field_ref[:, 7 : 9 + rows, :]
    bend = 4.0 * mid - (
        field_ref[:, 6 : 8 + rows, :] + field_ref[:, 8 : 10 + rows, :] + sides(mid)
    )
    bend_ref[:, 7 : 9 + rows, :] = bend
    for c in range(3):
        bend_ref[c, 7:8, :] = jnp.where(top, bend_ref[c, 7:8, :], 0.0)
        bend_ref[c, 8 + rows : 9 + rows, :] = jnp.where(
            bottom, bend_ref[c, 8 + rows : 9 + rows, :], 0.0
        )
    mid = bend_ref[:, 8 : 8 + rows, :]
    again = 4.0 * mid - (
        bend_ref[:, 7 : 7 + rows, :] + bend_ref[:, 9 : 9 + rows, :] + sides(mid)
    )
    kd_ref[...] = stiff_ref[...][None] * (again + 4.0 * mid)


def params():
    return pltpu.CompilerParams(vmem_limit_bytes=LIMIT)


def patch_pairs(d):
    return [(p, p ^ d) for p in range(4)]


def exchange_and_relax(message, displacement, stiffness, kd):
    slabs, owners = lax.axis_size("slab"), lax.axis_size("patch")
    rows = displacement.shape[1]
    sources = slabs * owners
    got = lax.all_to_all(
        message.reshape(sources, 8, 128), ("slab", "patch"), 0, 0, tiled=True
    )
    reply = jax.ShapeDtypeStruct((8, 256), F32)
    new, *replies = pl.pallas_call(
        owner_kernel,
        out_shape=(jax.ShapeDtypeStruct(displacement.shape, F32),) + (reply,) * 4,
        in_specs=vmem(4),
        out_specs=hbm(1) + vmem(4),
        scratch_shapes=[
            pltpu.VMEM((2, sources, 128), F32),
            pltpu.VMEM((2, sources, 128), F32),
            pltpu.VMEM((3, rows, 128), F32),
            pltpu.SemaphoreType.DMA,
        ],
        compiler_params=params(),
        name="owner",
    )(got, displacement, stiffness, kd)
    back = [replies[0]] + [
        lax.ppermute(replies[d], "patch", patch_pairs(d)) for d in (1, 2, 3)
    ]
    wall = pl.pallas_call(
        finish_kernel,
        out_shape=jax.ShapeDtypeStruct((3, 1, 1, owners * 256), F32),
        in_specs=vmem(4),
        out_specs=pl.BlockSpec(memory_space=pltpu.VMEM),
        compiler_params=params(),
        name="finish",
    )(*back)
    return new, wall


def halves(value):
    high = value.astype(BF)
    low = (value - high.astype(F32)).astype(BF)
    return jnp.concatenate([high.astype(F32), low.astype(F32)], axis=1)


def lines_of(scale_ref, pad_ref):
    pad_ref[...] = jnp.zeros_like(pad_ref)
    pad_ref[0:2, 0 : scale_ref.shape[1]] = scale_ref[...]
    return pltpu.roll(pad_ref[...], 8, 1)


def near_kernel(
    state_hbm, rhs_hbm, scale_hbm, disp_hbm, near_ref, own_ref, one_ref, three_ref,
    state_ref, rhs_ref, scale_ref, disp_ref, pad_ref, build_ref, sems,
):
    copies = [
        pltpu.make_async_copy(a, b, sems.at[i])
        for i, (a, b) in enumerate(
            (
                (scale_hbm, scale_ref),
                (state_hbm, state_ref),
                (rhs_hbm, rhs_ref),
                (disp_hbm, disp_ref),
            )
        )
    ]
    for copy in copies:
        copy.start()
    odd = lax.axis_index("slab") % 2
    even = lax.axis_index("patch") % 2 == 0
    cols = state_ref.shape[1]
    for copy in copies:
        copy.wait()
    for i, row in enumerate((odd, 1 - odd)):
        for part, ref in ((0, state_ref), (2, rhs_ref)):
            value = ref[row]
            at = part + i
            own_ref[at * cols : (at + 1) * cols, :] = value.astype(BF)
            low, high = value[0:4], value[cols - 4 : cols]
            build_ref[0, 4 * at : 4 * at + 4, :] = jnp.where(even, high, low)
            build_ref[1, 4 * at : 4 * at + 4, :] = jnp.where(even, low, high)
    near_ref[...] = state_ref[1 - odd].astype(BF)
    lines = lines_of(scale_ref, pad_ref)
    flip = odd == 1
    first = jnp.where(flip, lines[1:2], lines[0:1])
    second = jnp.where(flip, lines[0:1], lines[1:2])
    pair = jnp.concatenate([halves(first), halves(second), jnp.zeros((6, 256), F32)], axis=0)
    own_ref[4 * cols :, :] = pair.astype(BF)
    for e in range(2):
        build_ref[e, 16:24, :] = pair
        build_ref[e, EDGE:, :] = jnp.zeros((8, 256), F32)
    rows = disp_ref.shape[1]
    for c in range(3):
        top = halves(disp_ref[c, 0:2, :])
        bottom = halves(disp_ref[c, rows - 2 : rows, :])
        at = EDGE + 2 * c
        build_ref[0, at : at + 2, :] = jnp.where(even, bottom, top)
        build_ref[1, at : at + 2, :] = jnp.where(even, top, bottom)
    one_ref[...] = build_ref[0].astype(BF)
    three_ref[...] = build_ref[1].astype(BF)


def sweep_kernel(
    state_ref,
    rhs_ref,
    scale_ref,
    near_ref,
    inner_ref,
    outer_ref,
    one_ref,
    three_ref,
    relay_ref,
    matrix_ref,
    x_ref,
    y_ref,
    inverse_ref,
    tmap_ref,
    elem_hbm,
    point_hbm,
    count_hbm,
    out_hbm,
    message_ref,
    v_ref,
    r_ref,
    s_ref,
    i_ref,
    line_ref,
    rows_ref,
    elem_ref,
    point_ref,
    count_ref,
    out_ref,
    sems,
):
    copies = [
        pltpu.make_async_copy(a, b, sems.at[i])
        for i, (a, b) in enumerate(
            ((elem_hbm, elem_ref), (point_hbm, point_ref), (count_hbm, count_ref))
        )
    ]
    for copy in copies:
        copy.start()
    slab, patch = lax.axis_index("slab"), lax.axis_index("patch")
    last_slab, last_patch = lax.axis_size("slab") - 1, lax.axis_size("patch") - 1
    odd = slab % 2
    even = patch % 2 == 0
    cols, width = state_ref.shape[1], state_ref.shape[2]
    wide = cols + 16
    inside = (slab > 0) & (slab < last_slab)
    col = iota((wide, width), 0)
    valid = (col >= 8) & (col < 8 + cols)
    valid = valid | ((col < 8) & (patch > 0)) | ((col >= 8 + cols) & (patch < last_patch))
    edge = valid.astype(F32)
    keep = edge * inside.astype(F32)
    v_ref[:, 0:8, :] = jnp.zeros((8, 8, width), F32)
    v_ref[:, 8 + cols :, :] = jnp.zeros((8, 8, width), F32)
    r_ref[:, 0:8, :] = jnp.zeros((6, 8, width), F32)
    r_ref[:, 8 + cols :, :] = jnp.zeros((6, 8, width), F32)
    head = 5 * cols + 8
    tail = 3 * cols + 8
    strips = {
        0: (one_ref[0:EDGE], three_ref[0:EDGE]),
        1: (inner_ref[tail : tail + EDGE], inner_ref[tail + EDGE : tail + 2 * EDGE]),
        2: (outer_ref[head : head + EDGE], outer_ref[head + EDGE : head + 2 * EDGE]),
    }
    sides = {}
    for kind, pair in strips.items():
        one, three = (x.astype(F32) for x in pair)
        sides[kind] = (jnp.where(even, three, one), jnp.where(even, one, three))
    lane = iota((1, 128), 1)
    line_ref[...] = jnp.zeros_like(line_ref)
    line_ref[0:2, 0:cols] = scale_ref[...]
    exact = pltpu.roll(line_ref[...], 8, 1)
    table = ((2, 1), (2, 0), (0, 0), (0, 1), (1, 1), (1, 0))
    for r, (kind, i) in enumerate(table):
        if kind == 0:
            row = odd if i == 0 else 1 - odd
            v_ref[r + 1, 8 : 8 + cols, :] = state_ref[row]
            r_ref[r, 8 : 8 + cols, :] = rhs_ref[row]
            line = jnp.where(row == 1, exact[1:2], exact[0:1])
        else:
            if kind == 1:
                value = near_ref[...] if i == 1 else inner_ref[0:cols]
                ref, at = inner_ref, (i + 1) * cols
            else:
                value = outer_ref[i * cols : (i + 1) * cols]
                ref, at = outer_ref, (i + 2) * cols
            v_ref[r + 1, 8 : 8 + cols, :] = value.astype(F32)
            r_ref[r, 8 : 8 + cols, :] = ref[at : at + cols, :].astype(F32)
            below = (3 if kind == 1 else 4) * cols
            both = ref[below : below + 8, :].astype(F32)[i : i + 1]
            line = both[:, :128] + both[:, 128:]
        for side, start in zip(sides[kind], (4, 8 + cols)):
            v_ref[r + 1, start : start + 4, :] = side[4 * i : 4 * i + 4]
            r_ref[r, start : start + 4, :] = side[8 + 4 * i : 12 + 4 * i]
            both = side[16 + i : 17 + i]
            far = pltpu.roll(both[:, :128] + both[:, 128:], 64, 1)
            here = (lane >= start) & (lane < start + 4)
            line = jnp.where(here, far, line)
        line_ref[r : r + 1, :] = jnp.where(line > 0.0, line, 1.0)
    line_ref[6:8, :] = jnp.ones((2, 128), F32)
    v_ref[0, 8 : 8 + cols, :] = outer_ref[4 * cols + 8 : head, :].astype(F32)
    beyond = (slab != 1) & (slab != last_slab - 1)
    v_ref[7, 8 : 8 + cols, :] = relay_ref[...].astype(F32) * beyond.astype(F32)
    for r in range(8):
        v_ref[r] = v_ref[r] * (keep if r < 3 else edge)
    lines = line_ref[...]
    columns = jnp.transpose(lines)
    inverses = jnp.transpose(1.0 / lines)
    for r in range(6):
        s_ref[r] = jnp.broadcast_to(columns[:wide, r : r + 1], (wide, width))
        i_ref[r] = jnp.broadcast_to(inverses[:wide, r : r + 1], (wide, width))
    for sweep in range(SWEEPS):
        a, b = 1 + sweep, 7 - sweep
        n = b - a
        near = v_ref[a - 1 : b + 1].astype(BF).astype(F32)
        mid = near[1 : n + 1]
        nx = (near[0:n] + near[2 : n + 2]).astype(BF)
        ny = (pltpu.roll(mid, 1, 1) + pltpu.roll(mid, wide - 1, 1)).astype(BF)
        flat = (n * wide, width)
        own = jnp.dot(mid.astype(BF).reshape(flat), matrix_ref[...], preferred_element_type=F32)
        side = jnp.dot(nx.reshape(flat), x_ref[...], preferred_element_type=F32)
        side += jnp.dot(ny.reshape(flat), y_ref[...], preferred_element_type=F32)
        scale = s_ref[a - 1 : b - 1].reshape(flat)
        rhs = r_ref[a - 1 : b - 1].reshape(flat)
        residue = (rhs - (scale * own - side)).astype(BF)
        update = jnp.dot(residue, inverse_ref[...], preferred_element_type=F32)
        update = update * i_ref[a - 1 : b - 1].reshape(flat)
        value = v_ref[a:b] + update.reshape(n, wide, width)
        for j in range(n):
            v_ref[a + j] = value[j] * (keep if a + j < 3 else edge)
    out_ref[odd] = v_ref[3, 8 : 8 + cols, :]
    out_ref[1 - odd] = v_ref[4, 8 : 8 + cols, :]
    out = pltpu.make_async_copy(out_ref, out_hbm, sems.at[3])
    out.start()
    final = out_ref[...].astype(BF).reshape(2 * cols, width)
    for copy in copies:
        copy.wait()
    slot_rows(final, tmap_ref[...], elem_ref[0], point_ref[0], count_ref.at[0], rows_ref)
    message_ref[...] = jnp.broadcast_to(rows_ref[...].astype(BF)[None], message_ref.shape)
    out.wait()


def call(kernel, name, out_shape, operands, scratch=(), in_specs=None, out_specs=None):
    return pl.pallas_call(
        kernel,
        out_shape=out_shape,
        in_specs=in_specs or vmem(len(operands)),
        out_specs=out_specs or jax.tree.map(lambda _: vmem(1)[0], out_shape),
        scratch_shapes=list(scratch),
        compiler_params=params(),
        name=name,
    )(*operands)


def shards(
    fluid_state,
    fluid_rhs,
    element_scale,
    element_matrix,
    couple_x,
    couple_y,
    block_inverse,
    traction_map,
    slot_elem,
    slot_point,
    slot_count,
    displacement,
    stiffness,
):
    cols, width = fluid_state.shape[1:]
    slots = slot_elem.shape[2]
    slabs, owners = lax.axis_size("slab"), lax.axis_size("patch")
    shape = jax.ShapeDtypeStruct
    inner_pairs = [(s, s ^ 1) for s in range(slabs)]
    outer_pairs = [(s, (s + 1) % slabs) for s in range(1, slabs, 2)]
    outer_pairs = outer_pairs + [(b, a) for a, b in outer_pairs]
    strip = shape((EDGE + 8, width), BF)
    near, own, to_one, to_three = call(
        near_kernel,
        "near",
        (shape((cols, width), BF), shape((4 * cols + 8, width), BF), strip, strip),
        tuple(
            pltpu.with_memory_space_constraint(x, pltpu.HBM)
            for x in (fluid_state, fluid_rhs, element_scale, displacement)
        ),
        [
            pltpu.VMEM(fluid_state.shape, F32),
            pltpu.VMEM(fluid_rhs.shape, F32),
            pltpu.VMEM(element_scale.shape, F32),
            pltpu.VMEM(displacement.shape, F32),
            pltpu.VMEM((8, 128), F32),
            pltpu.VMEM((2, EDGE + 8, width), F32),
            pltpu.SemaphoreType.DMA((4,)),
        ],
        in_specs=hbm(4),
    )
    inner_near = lax.ppermute(near, "slab", inner_pairs)
    from_three = lax.ppermute(to_three, "patch", patch_pairs(3))
    from_one = lax.ppermute(to_one, "patch", patch_pairs(1))
    strips = [from_one[:EDGE], from_three[:EDGE]]
    outer = lax.ppermute(jnp.concatenate([own, inner_near] + strips), "slab", outer_pairs)
    inner = lax.ppermute(
        jnp.concatenate([own[:cols], own[2 * cols :]] + strips), "slab", inner_pairs
    )
    relay = lax.ppermute(outer[:cols], "slab", inner_pairs)
    wide = cols + 16
    state, message = call(
        sweep_kernel,
        "sweep",
        (shape(fluid_state.shape, F32), shape((slabs, owners, 8, 128), BF)),
        (
            fluid_state,
            fluid_rhs,
            element_scale,
            inner_near,
            inner,
            outer,
            from_one,
            from_three,
            relay,
            element_matrix,
            couple_x,
            couple_y,
            block_inverse,
            traction_map,
            slot_elem,
            slot_point,
            slot_count,
        ),
        [
            pltpu.VMEM((8, wide, width), F32),
            pltpu.VMEM((6, wide, width), F32),
            pltpu.VMEM((6, wide, width), F32),
            pltpu.VMEM((6, wide, width), F32),
            pltpu.VMEM((8, 128), F32),
            pltpu.VMEM((owners, 8, 128), F32),
            pltpu.VMEM((1, 1, slots), I32),
            pltpu.VMEM((1, 1, slots), I32),
            pltpu.VMEM((1, 1, owners), I32),
            pltpu.VMEM(fluid_state.shape, F32),
            pltpu.SemaphoreType.DMA((4,)),
        ],
        in_specs=vmem(14) + hbm(3),
        out_specs=tuple(hbm(1) + vmem(1)),
    )
    kd = call(
        shell_kernel,
        "shell",
        shape(displacement.shape, F32),
        (from_one, from_three, displacement, stiffness),
        [pltpu.VMEM((3, displacement.shape[1] + 16, 128), F32)] * 2,
    )
    new, wall = exchange_and_relax(message, displacement, stiffness, kd)
    return state, new, wall


def solution(mesh):
    return jax.shard_map(
        shards,
        mesh=mesh,
        in_specs=(
            P("slab", "patch", None),
            P("slab", "patch", None),
            P("slab", "patch"),
            P(),
            P(),
            P(),
            P(),
            P(),
            P("slab", "patch", None),
            P("slab", "patch", None),
            P("slab", "patch", None),
            P(None, "patch", None),
            P("patch", None),
        ),
        out_specs=(
            P("slab", "patch", None),
            P(None, "patch", None),
            P(None, "slab", "patch", None),
        ),
        check_vma=False,
    )
```

```python
import jax
import jax.numpy as jnp
from jax import lax
from jax.experimental import pallas as pl
from jax.experimental.pallas import tpu as pltpu
from jax.sharding import PartitionSpec as P

SWEEPS = 3
BF = jnp.bfloat16
F32 = jnp.float32
I32 = jnp.int32
LIMIT = 48 << 20
EDGE = 24


def vmem(n):
    return [pl.BlockSpec(memory_space=pltpu.VMEM)] * n


def hbm(n):
    return [pl.BlockSpec(memory_space=pltpu.HBM)] * n


def iota(shape, dim):
    return lax.broadcasted_iota(I32, shape, dim)


def nt(a, b):
    return lax.dot_general(a, b, (((1,), (1,)), ((), ())), preferred_element_type=F32)


def slot_rows(final, tmap, elem, point, count_ref, rows_ref):
    owners = rows_ref.shape[0]
    slots = elem.shape[1]
    cap = slots // owners
    traction = nt(tmap, final).astype(BF)
    hot = (iota((final.shape[0], slots), 0) == elem).astype(F32).astype(BF)
    pull = jnp.dot(traction, hot, preferred_element_type=F32)
    slot = iota((1, slots), 1)
    owner = slot // cap
    limit = jnp.zeros((1, slots), I32)
    for k in range(owners):
        limit = jnp.where(owner == k, count_ref[0:1, k : k + 1], limit)
    live = (slot - owner * cap) < limit
    row = point // 128
    code = (128 + (point - row * 128)).astype(F32)
    for b in range(6):
        code = code * jnp.where((row >> b) & 1 == 1, F32(2.0 ** (2**b)), F32(1.0))
    code = jnp.where(live, code, 0.0)
    pull = jnp.where(live, pull, 0.0)
    for k in range(owners):
        for j in range(4):
            source = code if j == 3 else pull[j : j + 1]
            for h in range(2):
                start = k * cap + h * 128
                rows_ref[k, 2 * j + h : 2 * j + h + 1, :] = source[:, start : start + 128]


def decode(code):
    row = jnp.zeros(code.shape, F32)
    for b in (5, 4, 3, 2, 1, 0):
        big = code >= F32(128.0 * 2.0 ** (2**b))
        row = row + jnp.where(big, F32(2**b), 0.0)
        code = code * jnp.where(big, F32(2.0 ** -(2**b)), 1.0)
    return row, code - 128.0


def owner_kernel(
    got_ref, disp_ref, stiff_ref, kd_ref, new_ref, r0, r1, r2, r3, row_ref, lane_ref
):
    replies = (r0, r1, r2, r3)
    sources = got_ref.shape[0]
    rows = disp_ref.shape[1]
    patch = lax.axis_index("patch")
    first = lax.axis_index("slab") * 4
    for h in range(2):
        row, lane = decode(got_ref[:, 6 + h, :].astype(F32))
        row_ref[h] = row
        lane_ref[h] = lane
    row_ids = iota((rows, 128), 0).astype(F32).astype(BF)
    lane_ids = iota((128, 128), 0).astype(F32).astype(BF)
    none = jnp.zeros((rows, 128), BF)
    ones, zeros = jnp.ones((128, 128), BF), jnp.zeros((128, 128), BF)
    total = jnp.zeros((3 * rows, 128), F32)
    group = 8
    for base in range(0, sources, group):
        row8 = [row_ref[h, base : base + group, :].astype(BF) for h in range(2)]
        lane8 = [lane_ref[h, base : base + group, :].astype(BF) for h in range(2)]
        for g in range(group):
            vals = got_ref[base + g]
            left, right = [], []
            for h in range(2):
                mask = row_ids == row8[h][g : g + 1]
                left.append(
                    jnp.concatenate(
                        [jnp.where(mask, vals[2 * c + h : 2 * c + h + 1], none) for c in range(3)],
                        axis=0,
                    )
                )
                right.append(jnp.where(lane_ids == lane8[h][g : g + 1], ones, zeros))
            total += nt(jnp.concatenate(left, axis=1), jnp.concatenate(right, axis=1))
    loads = total.reshape(3, rows, 128)
    new = disp_ref[...] + (loads - kd_ref[...]) / (36.0 * stiff_ref[...])[None]
    new_ref[...] = new
    flat = new.reshape(3 * rows, 128)
    high = flat.astype(BF)
    low = (flat - high.astype(F32)).astype(BF)
    row_ids = iota((rows, 128), 0).astype(F32)
    for d in range(4):
        src = first + (patch ^ d)
        for h in range(2):
            row = row_ref[h, pl.ds(src, 1), :]
            lane = lane_ref[h, pl.ds(src, 1), :]
            hot = jnp.where(lane_ids == lane.astype(BF), ones, zeros)
            picked = jnp.dot(high, hot, preferred_element_type=F32)
            picked += jnp.dot(low, hot, preferred_element_type=F32)
            mask = row_ids == row
            for c in range(3):
                part = jnp.where(mask, picked[c * rows : (c + 1) * rows], 0.0)
                replies[d][c : c + 1, h * 128 : (h + 1) * 128] = part.sum(axis=0, keepdims=True)


def store_kernel(value_ref, out_ref, sem):
    copy = pltpu.make_async_copy(value_ref, out_ref, sem)
    copy.start()
    copy.wait()


def store(value, name):
    return pl.pallas_call(
        store_kernel,
        out_shape=jax.ShapeDtypeStruct(value.shape, value.dtype),
        in_specs=vmem(1),
        out_specs=hbm(1)[0],
        scratch_shapes=[pltpu.SemaphoreType.DMA],
        compiler_params=params(),
        name=name,
    )(value)


def finish_kernel(r0, r1, r2, r3, out_ref):
    cap = r0.shape[1]
    patch = lax.axis_index("patch")
    for d, reply in enumerate((r0, r1, r2, r3)):
        start = pl.multiple_of((patch ^ d) * cap, cap)
        for c in range(3):
            out_ref[c, 0, :, pl.ds(start, cap)] = reply[c : c + 1, :]


def shell_kernel(
    one_ref, three_ref, disp_ref, stiff_ref, state_ref, kd_ref, out_ref, field_ref, bend_ref, sem
):
    copy = pltpu.make_async_copy(state_ref, out_ref, sem)
    copy.start()
    rows = disp_ref.shape[1]
    patch = lax.axis_index("patch")
    top = patch > 0
    bottom = patch < 3
    even = patch % 2 == 0
    one, three = (
        ref[EDGE:, :128].astype(F32) + ref[EDGE:, 128:].astype(F32)
        for ref in (one_ref, three_ref)
    )
    above = jnp.where(even, three, one)
    below = jnp.where(even, one, three)
    field_ref[...] = jnp.zeros_like(field_ref)
    bend_ref[...] = jnp.zeros_like(bend_ref)
    field_ref[:, 8 : 8 + rows, :] = disp_ref[...]
    lane = iota((1, 1, 128), 2)

    def sides(x):
        left = jnp.where(lane == 0, 0.0, pltpu.roll(x, 1, 2))
        right = jnp.where(lane == 127, 0.0, pltpu.roll(x, 127, 2))
        return left + right

    for c in range(3):
        field_ref[c, 6:8, :] = jnp.where(top, above[2 * c : 2 * c + 2], 0.0)
        field_ref[c, 8 + rows : 10 + rows, :] = jnp.where(bottom, below[2 * c : 2 * c + 2], 0.0)
    mid = field_ref[:, 7 : 9 + rows, :]
    bend = 4.0 * mid - (
        field_ref[:, 6 : 8 + rows, :] + field_ref[:, 8 : 10 + rows, :] + sides(mid)
    )
    bend_ref[:, 7 : 9 + rows, :] = bend
    for c in range(3):
        bend_ref[c, 7:8, :] = jnp.where(top, bend_ref[c, 7:8, :], 0.0)
        bend_ref[c, 8 + rows : 9 + rows, :] = jnp.where(
            bottom, bend_ref[c, 8 + rows : 9 + rows, :], 0.0
        )
    mid = bend_ref[:, 8 : 8 + rows, :]
    again = 4.0 * mid - (
        bend_ref[:, 7 : 7 + rows, :] + bend_ref[:, 9 : 9 + rows, :] + sides(mid)
    )
    kd_ref[...] = stiff_ref[...][None] * (again + 4.0 * mid)
    copy.wait()


def params():
    return pltpu.CompilerParams(vmem_limit_bytes=LIMIT)


def patch_pairs(d):
    return [(p, p ^ d) for p in range(4)]


def exchange_and_relax(message, displacement, stiffness, kd):
    slabs, owners = lax.axis_size("slab"), lax.axis_size("patch")
    rows = displacement.shape[1]
    sources = slabs * owners
    got = lax.all_to_all(
        message.reshape(sources, 8, 128), ("slab", "patch"), 0, 0, tiled=True
    )
    reply = jax.ShapeDtypeStruct((8, 256), F32)
    new, *replies = pl.pallas_call(
        owner_kernel,
        out_shape=(jax.ShapeDtypeStruct(displacement.shape, F32),) + (reply,) * 4,
        in_specs=vmem(4),
        out_specs=vmem(5),
        scratch_shapes=[
            pltpu.VMEM((2, sources, 128), F32),
            pltpu.VMEM((2, sources, 128), F32),
        ],
        compiler_params=params(),
        name="owner",
    )(got, displacement, stiffness, kd)
    back = [replies[0]] + [
        lax.ppermute(replies[d], "patch", patch_pairs(d)) for d in (1, 2, 3)
    ]
    wall = pl.pallas_call(
        finish_kernel,
        out_shape=jax.ShapeDtypeStruct((3, 1, 1, owners * 256), F32),
        in_specs=vmem(4),
        out_specs=pl.BlockSpec(memory_space=pltpu.VMEM),
        compiler_params=params(),
        name="finish",
    )(*back)
    return store(new, "store_shell"), wall


def halves(value):
    high = value.astype(BF)
    low = (value - high.astype(F32)).astype(BF)
    return jnp.concatenate([high.astype(F32), low.astype(F32)], axis=1)


def lines_of(scale_ref, pad_ref):
    pad_ref[...] = jnp.zeros_like(pad_ref)
    pad_ref[0:2, 0 : scale_ref.shape[1]] = scale_ref[...]
    return pltpu.roll(pad_ref[...], 8, 1)


def near_kernel(
    state_hbm, rhs_hbm, scale_hbm, disp_hbm, near_ref, own_ref, one_ref, three_ref,
    state_ref, rhs_ref, scale_ref, disp_ref, pad_ref, build_ref, sems,
):
    copies = [
        pltpu.make_async_copy(a, b, sems.at[i])
        for i, (a, b) in enumerate(
            (
                (scale_hbm, scale_ref),
                (state_hbm, state_ref),
                (rhs_hbm, rhs_ref),
                (disp_hbm, disp_ref),
            )
        )
    ]
    for copy in copies:
        copy.start()
    odd = lax.axis_index("slab") % 2
    even = lax.axis_index("patch") % 2 == 0
    cols = state_ref.shape[1]
    for copy in copies:
        copy.wait()
    for i, row in enumerate((odd, 1 - odd)):
        for part, ref in ((0, state_ref), (2, rhs_ref)):
            value = ref[row]
            at = part + i
            own_ref[at * cols : (at + 1) * cols, :] = value.astype(BF)
            low, high = value[0:4], value[cols - 4 : cols]
            build_ref[0, 4 * at : 4 * at + 4, :] = jnp.where(even, high, low)
            build_ref[1, 4 * at : 4 * at + 4, :] = jnp.where(even, low, high)
    near_ref[...] = state_ref[1 - odd].astype(BF)
    lines = lines_of(scale_ref, pad_ref)
    flip = odd == 1
    first = jnp.where(flip, lines[1:2], lines[0:1])
    second = jnp.where(flip, lines[0:1], lines[1:2])
    pair = jnp.concatenate([halves(first), halves(second), jnp.zeros((6, 256), F32)], axis=0)
    own_ref[4 * cols :, :] = pair.astype(BF)
    for e in range(2):
        build_ref[e, 16:24, :] = pair
        build_ref[e, EDGE:, :] = jnp.zeros((8, 256), F32)
    rows = disp_ref.shape[1]
    for c in range(3):
        top = halves(disp_ref[c, 0:2, :])
        bottom = halves(disp_ref[c, rows - 2 : rows, :])
        at = EDGE + 2 * c
        build_ref[0, at : at + 2, :] = jnp.where(even, bottom, top)
        build_ref[1, at : at + 2, :] = jnp.where(even, top, bottom)
    one_ref[...] = build_ref[0].astype(BF)
    three_ref[...] = build_ref[1].astype(BF)


def sweep_kernel(
    state_ref,
    rhs_ref,
    scale_ref,
    near_ref,
    inner_ref,
    outer_ref,
    one_ref,
    three_ref,
    relay_ref,
    matrix_ref,
    x_ref,
    y_ref,
    inverse_ref,
    tmap_ref,
    elem_hbm,
    point_hbm,
    count_hbm,
    out_ref,
    message_hbm,
    v_ref,
    r_ref,
    s_ref,
    i_ref,
    line_ref,
    rows_ref,
    elem_ref,
    point_ref,
    count_ref,
    message_ref,
    sems,
):
    copies = [
        pltpu.make_async_copy(a, b, sems.at[i])
        for i, (a, b) in enumerate(
            ((elem_hbm, elem_ref), (point_hbm, point_ref), (count_hbm, count_ref))
        )
    ]
    for copy in copies:
        copy.start()
    slab, patch = lax.axis_index("slab"), lax.axis_index("patch")
    last_slab, last_patch = lax.axis_size("slab") - 1, lax.axis_size("patch") - 1
    odd = slab % 2
    even = patch % 2 == 0
    cols, width = state_ref.shape[1], state_ref.shape[2]
    wide = cols + 16
    inside = (slab > 0) & (slab < last_slab)
    col = iota((wide, width), 0)
    valid = (col >= 8) & (col < 8 + cols)
    valid = valid | ((col < 8) & (patch > 0)) | ((col >= 8 + cols) & (patch < last_patch))
    edge = valid.astype(F32)
    keep = edge * inside.astype(F32)
    v_ref[:, 0:8, :] = jnp.zeros((8, 8, width), F32)
    v_ref[:, 8 + cols :, :] = jnp.zeros((8, 8, width), F32)
    r_ref[:, 0:8, :] = jnp.zeros((6, 8, width), F32)
    r_ref[:, 8 + cols :, :] = jnp.zeros((6, 8, width), F32)
    head = 5 * cols + 8
    tail = 3 * cols + 8
    strips = {
        0: (one_ref[0:EDGE], three_ref[0:EDGE]),
        1: (inner_ref[tail : tail + EDGE], inner_ref[tail + EDGE : tail + 2 * EDGE]),
        2: (outer_ref[head : head + EDGE], outer_ref[head + EDGE : head + 2 * EDGE]),
    }
    sides = {}
    for kind, pair in strips.items():
        one, three = (x.astype(F32) for x in pair)
        sides[kind] = (jnp.where(even, three, one), jnp.where(even, one, three))
    lane = iota((1, 128), 1)
    line_ref[...] = jnp.zeros_like(line_ref)
    line_ref[0:2, 0:cols] = scale_ref[...]
    exact = pltpu.roll(line_ref[...], 8, 1)
    table = ((2, 1), (2, 0), (0, 0), (0, 1), (1, 1), (1, 0))
    for r, (kind, i) in enumerate(table):
        if kind == 0:
            row = odd if i == 0 else 1 - odd
            v_ref[r + 1, 8 : 8 + cols, :] = state_ref[row]
            r_ref[r, 8 : 8 + cols, :] = rhs_ref[row]
            line = jnp.where(row == 1, exact[1:2], exact[0:1])
        else:
            if kind == 1:
                value = near_ref[...] if i == 1 else inner_ref[0:cols]
                ref, at = inner_ref, (i + 1) * cols
            else:
                value = outer_ref[i * cols : (i + 1) * cols]
                ref, at = outer_ref, (i + 2) * cols
            v_ref[r + 1, 8 : 8 + cols, :] = value.astype(F32)
            r_ref[r, 8 : 8 + cols, :] = ref[at : at + cols, :].astype(F32)
            below = (3 if kind == 1 else 4) * cols
            both = ref[below : below + 8, :].astype(F32)[i : i + 1]
            line = both[:, :128] + both[:, 128:]
        for side, start in zip(sides[kind], (4, 8 + cols)):
            v_ref[r + 1, start : start + 4, :] = side[4 * i : 4 * i + 4]
            r_ref[r, start : start + 4, :] = side[8 + 4 * i : 12 + 4 * i]
            both = side[16 + i : 17 + i]
            far = pltpu.roll(both[:, :128] + both[:, 128:], 64, 1)
            here = (lane >= start) & (lane < start + 4)
            line = jnp.where(here, far, line)
        line_ref[r : r + 1, :] = jnp.where(line > 0.0, line, 1.0)
    line_ref[6:8, :] = jnp.ones((2, 128), F32)
    v_ref[0, 8 : 8 + cols, :] = outer_ref[4 * cols + 8 : head, :].astype(F32)
    beyond = (slab != 1) & (slab != last_slab - 1)
    v_ref[7, 8 : 8 + cols, :] = relay_ref[...].astype(F32) * beyond.astype(F32)
    for r in range(8):
        v_ref[r] = v_ref[r] * (keep if r < 3 else edge)
    lines = line_ref[...]
    columns = jnp.transpose(lines)
    inverses = jnp.transpose(1.0 / lines)
    for r in range(6):
        s_ref[r] = jnp.broadcast_to(columns[:wide, r : r + 1], (wide, width))
        i_ref[r] = jnp.broadcast_to(inverses[:wide, r : r + 1], (wide, width))
    for sweep in range(SWEEPS):
        a, b = 1 + sweep, 7 - sweep
        n = b - a
        near = v_ref[a - 1 : b + 1].astype(BF).astype(F32)
        mid = near[1 : n + 1]
        nx = (near[0:n] + near[2 : n + 2]).astype(BF)
        ny = (pltpu.roll(mid, 1, 1) + pltpu.roll(mid, wide - 1, 1)).astype(BF)
        flat = (n * wide, width)
        own = jnp.dot(mid.astype(BF).reshape(flat), matrix_ref[...], preferred_element_type=F32)
        side = jnp.dot(nx.reshape(flat), x_ref[...], preferred_element_type=F32)
        side += jnp.dot(ny.reshape(flat), y_ref[...], preferred_element_type=F32)
        scale = s_ref[a - 1 : b - 1].reshape(flat)
        rhs = r_ref[a - 1 : b - 1].reshape(flat)
        residue = (rhs - (scale * own - side)).astype(BF)
        update = jnp.dot(residue, inverse_ref[...], preferred_element_type=F32)
        update = update * i_ref[a - 1 : b - 1].reshape(flat)
        value = v_ref[a:b] + update.reshape(n, wide, width)
        for j in range(n):
            v_ref[a + j] = value[j] * (keep if a + j < 3 else edge)
    out_ref[odd] = v_ref[3, 8 : 8 + cols, :]
    out_ref[1 - odd] = v_ref[4, 8 : 8 + cols, :]
    final = out_ref[...].astype(BF).reshape(2 * cols, width)
    for copy in copies:
        copy.wait()
    slot_rows(final, tmap_ref[...], elem_ref[0], point_ref[0], count_ref.at[0], rows_ref)
    message_ref[...] = jnp.broadcast_to(rows_ref[...].astype(BF)[None], message_ref.shape)
    part = message_ref.shape[0]
    copies = [
        pltpu.make_async_copy(message_ref, message_hbm.at[i * part : (i + 1) * part], sems.at[3 + i])
        for i in range(message_hbm.shape[0] // part)
    ]
    for copy in copies:
        copy.start()
    for copy in copies:
        copy.wait()


def call(kernel, name, out_shape, operands, scratch=(), in_specs=None, out_specs=None):
    return pl.pallas_call(
        kernel,
        out_shape=out_shape,
        in_specs=in_specs or vmem(len(operands)),
        out_specs=out_specs or jax.tree.map(lambda _: vmem(1)[0], out_shape),
        scratch_shapes=list(scratch),
        compiler_params=params(),
        name=name,
    )(*operands)


def shards(
    fluid_state,
    fluid_rhs,
    element_scale,
    element_matrix,
    couple_x,
    couple_y,
    block_inverse,
    traction_map,
    slot_elem,
    slot_point,
    slot_count,
    displacement,
    stiffness,
):
    cols, width = fluid_state.shape[1:]
    slots = slot_elem.shape[2]
    slabs, owners = lax.axis_size("slab"), lax.axis_size("patch")
    shape = jax.ShapeDtypeStruct
    inner_pairs = [(s, s ^ 1) for s in range(slabs)]
    outer_pairs = [(s, (s + 1) % slabs) for s in range(1, slabs, 2)]
    outer_pairs = outer_pairs + [(b, a) for a, b in outer_pairs]
    strip = shape((EDGE + 8, width), BF)
    near, own, to_one, to_three = call(
        near_kernel,
        "near",
        (shape((cols, width), BF), shape((4 * cols + 8, width), BF), strip, strip),
        tuple(
            pltpu.with_memory_space_constraint(x, pltpu.HBM)
            for x in (fluid_state, fluid_rhs, element_scale, displacement)
        ),
        [
            pltpu.VMEM(fluid_state.shape, F32),
            pltpu.VMEM(fluid_rhs.shape, F32),
            pltpu.VMEM(element_scale.shape, F32),
            pltpu.VMEM(displacement.shape, F32),
            pltpu.VMEM((8, 128), F32),
            pltpu.VMEM((2, EDGE + 8, width), F32),
            pltpu.SemaphoreType.DMA((4,)),
        ],
        in_specs=hbm(4),
    )
    inner_near = lax.ppermute(near, "slab", inner_pairs)
    from_three = lax.ppermute(to_three, "patch", patch_pairs(3))
    from_one = lax.ppermute(to_one, "patch", patch_pairs(1))
    strips = [from_one[:EDGE], from_three[:EDGE]]
    outer = lax.ppermute(jnp.concatenate([own, inner_near] + strips), "slab", outer_pairs)
    inner = lax.ppermute(
        jnp.concatenate([own[:cols], own[2 * cols :]] + strips), "slab", inner_pairs
    )
    relay = lax.ppermute(outer[:cols], "slab", inner_pairs)
    wide = cols + 16
    state, message = call(
        sweep_kernel,
        "sweep",
        (shape(fluid_state.shape, F32), shape((slabs, owners, 8, 128), BF)),
        (
            fluid_state,
            fluid_rhs,
            element_scale,
            inner_near,
            inner,
            outer,
            from_one,
            from_three,
            relay,
            element_matrix,
            couple_x,
            couple_y,
            block_inverse,
            traction_map,
            slot_elem,
            slot_point,
            slot_count,
        ),
        [
            pltpu.VMEM((8, wide, width), F32),
            pltpu.VMEM((6, wide, width), F32),
            pltpu.VMEM((6, wide, width), F32),
            pltpu.VMEM((6, wide, width), F32),
            pltpu.VMEM((8, 128), F32),
            pltpu.VMEM((owners, 8, 128), F32),
            pltpu.VMEM((1, 1, slots), I32),
            pltpu.VMEM((1, 1, slots), I32),
            pltpu.VMEM((1, 1, owners), I32),
            pltpu.VMEM((slabs // 4, owners, 8, 128), BF),
            pltpu.SemaphoreType.DMA((7,)),
        ],
        in_specs=vmem(14) + hbm(3),
        out_specs=tuple(vmem(1) + hbm(1)),
    )
    kd, final = call(
        shell_kernel,
        "shell",
        (shape(displacement.shape, F32), shape(state.shape, F32)),
        (from_one, from_three, displacement, stiffness, state),
        [pltpu.VMEM((3, displacement.shape[1] + 16, 128), F32)] * 2 + [pltpu.SemaphoreType.DMA],
        out_specs=tuple(vmem(1) + hbm(1)),
    )
    new, wall = exchange_and_relax(message, displacement, stiffness, kd)
    return final, new, wall


def solution(mesh):
    return jax.shard_map(
        shards,
        mesh=mesh,
        in_specs=(
            P("slab", "patch", None),
            P("slab", "patch", None),
            P("slab", "patch"),
            P(),
            P(),
            P(),
            P(),
            P(),
            P("slab", "patch", None),
            P("slab", "patch", None),
            P("slab", "patch", None),
            P(None, "patch", None),
            P("patch", None),
        ),
        out_specs=(
            P("slab", "patch", None),
            P(None, "patch", None),
            P(None, "slab", "patch", None),
        ),
        check_vma=False,
    )
```

```python
import jax
import jax.numpy as jnp
from jax import lax
from jax.experimental import pallas as pl
from jax.experimental.pallas import tpu as pltpu
from jax.sharding import PartitionSpec as P

SWEEPS = 3
BF = jnp.bfloat16
F32 = jnp.float32
I32 = jnp.int32
LIMIT = 48 << 20
EDGE = 16
THIN = 8


def vmem(n):
    return [pl.BlockSpec(memory_space=pltpu.VMEM)] * n


def hbm(n):
    return [pl.BlockSpec(memory_space=pltpu.HBM)] * n


def iota(shape, dim):
    return lax.broadcasted_iota(I32, shape, dim)


def nt(a, b):
    return lax.dot_general(a, b, (((1,), (1,)), ((), ())), preferred_element_type=F32)


def slot_codes(point, count_ref, owners):
    slots = point.shape[1]
    cap = slots // owners
    slot = iota((1, slots), 1)
    owner = slot // cap
    limit = jnp.zeros((1, slots), I32)
    for k in range(owners):
        limit = jnp.where(owner == k, count_ref[0:1, k : k + 1], limit)
    live = (slot - owner * cap) < limit
    row = point // 128
    code = (128 + (point - row * 128)).astype(F32)
    for b in range(6):
        code = code * jnp.where((row >> b) & 1 == 1, F32(2.0 ** (2**b)), F32(1.0))
    return live, jnp.where(live, code, 0.0)


def decode(code):
    row = jnp.zeros(code.shape, F32)
    for b in (5, 4, 3, 2, 1, 0):
        big = code >= F32(128.0 * 2.0 ** (2**b))
        row = row + jnp.where(big, F32(2**b), 0.0)
        code = code * jnp.where(big, F32(2.0 ** -(2**b)), 1.0)
    return row, code - 128.0


def owner_kernel(
    got_ref, disp_ref, stiff_ref, kd_ref, new_ref, r0, r1, r2, r3, row_ref, lane_ref
):
    replies = (r0, r1, r2, r3)
    sources = got_ref.shape[0]
    rows = disp_ref.shape[1]
    patch = lax.axis_index("patch")
    first = lax.axis_index("slab") * 4
    for h in range(2):
        row, lane = decode(got_ref[:, 6 + h, :].astype(F32))
        row_ref[h] = row
        lane_ref[h] = lane
    row_ids = iota((rows, 128), 0).astype(F32).astype(BF)
    lane_ids = iota((128, 128), 0).astype(F32).astype(BF)
    none = jnp.zeros((rows, 128), BF)
    ones, zeros = jnp.ones((128, 128), BF), jnp.zeros((128, 128), BF)
    total = jnp.zeros((3 * rows, 128), F32)
    group = 8
    for base in range(0, sources, group):
        row8 = [row_ref[h, base : base + group, :].astype(BF) for h in range(2)]
        lane8 = [lane_ref[h, base : base + group, :].astype(BF) for h in range(2)]
        for g in range(group):
            vals = got_ref[base + g]
            left, right = [], []
            for h in range(2):
                mask = row_ids == row8[h][g : g + 1]
                left.append(
                    jnp.concatenate(
                        [jnp.where(mask, vals[2 * c + h : 2 * c + h + 1], none) for c in range(3)],
                        axis=0,
                    )
                )
                right.append(jnp.where(lane_ids == lane8[h][g : g + 1], ones, zeros))
            total += nt(jnp.concatenate(left, axis=1), jnp.concatenate(right, axis=1))
    loads = total.reshape(3, rows, 128)
    new = disp_ref[...] + (loads - kd_ref[...]) / (36.0 * stiff_ref[...])[None]
    new_ref[...] = new
    flat = new.reshape(3 * rows, 128)
    high = flat.astype(BF)
    low = (flat - high.astype(F32)).astype(BF)
    row_ids = iota((rows, 128), 0).astype(F32)
    for d in range(4):
        src = first + (patch ^ d)
        for h in range(2):
            row = row_ref[h, pl.ds(src, 1), :]
            lane = lane_ref[h, pl.ds(src, 1), :]
            hot = jnp.where(lane_ids == lane.astype(BF), ones, zeros)
            picked = jnp.dot(high, hot, preferred_element_type=F32)
            picked += jnp.dot(low, hot, preferred_element_type=F32)
            mask = row_ids == row
            for c in range(3):
                part = jnp.where(mask, picked[c * rows : (c + 1) * rows], 0.0)
                replies[d][c : c + 1, h * 128 : (h + 1) * 128] = part.sum(axis=0, keepdims=True)


def store_kernel(value_ref, out_ref, sem):
    copy = pltpu.make_async_copy(value_ref, out_ref, sem)
    copy.start()
    copy.wait()


def store(value, name):
    return pl.pallas_call(
        store_kernel,
        out_shape=jax.ShapeDtypeStruct(value.shape, value.dtype),
        in_specs=vmem(1),
        out_specs=hbm(1)[0],
        scratch_shapes=[pltpu.SemaphoreType.DMA],
        compiler_params=params(),
        name=name,
    )(value)


def finish_kernel(r0, r1, r2, r3, out_ref):
    cap = r0.shape[1]
    patch = lax.axis_index("patch")
    for d, reply in enumerate((r0, r1, r2, r3)):
        start = pl.multiple_of((patch ^ d) * cap, cap)
        for c in range(3):
            out_ref[c, 0, :, pl.ds(start, cap)] = reply[c : c + 1, :]


def shell_kernel(
    one_ref, three_ref, disp_ref, stiff_ref, state_ref, kd_ref, out_ref, field_ref, bend_ref, sem
):
    copy = pltpu.make_async_copy(state_ref, out_ref, sem)
    copy.start()
    rows = disp_ref.shape[1]
    patch = lax.axis_index("patch")
    top = patch > 0
    bottom = patch < 3
    even = patch % 2 == 0
    one, three = (
        ref[EDGE:, :128].astype(F32) + ref[EDGE:, 128:].astype(F32)
        for ref in (one_ref, three_ref)
    )
    above = jnp.where(even, three, one)
    below = jnp.where(even, one, three)
    field_ref[...] = jnp.zeros_like(field_ref)
    bend_ref[...] = jnp.zeros_like(bend_ref)
    field_ref[:, 8 : 8 + rows, :] = disp_ref[...]
    lane = iota((1, 1, 128), 2)

    def sides(x):
        left = jnp.where(lane == 0, 0.0, pltpu.roll(x, 1, 2))
        right = jnp.where(lane == 127, 0.0, pltpu.roll(x, 127, 2))
        return left + right

    for c in range(3):
        field_ref[c, 6:8, :] = jnp.where(top, above[2 * c : 2 * c + 2], 0.0)
        field_ref[c, 8 + rows : 10 + rows, :] = jnp.where(bottom, below[2 * c : 2 * c + 2], 0.0)
    mid = field_ref[:, 7 : 9 + rows, :]
    bend = 4.0 * mid - (
        field_ref[:, 6 : 8 + rows, :] + field_ref[:, 8 : 10 + rows, :] + sides(mid)
    )
    bend_ref[:, 7 : 9 + rows, :] = bend
    for c in range(3):
        bend_ref[c, 7:8, :] = jnp.where(top, bend_ref[c, 7:8, :], 0.0)
        bend_ref[c, 8 + rows : 9 + rows, :] = jnp.where(
            bottom, bend_ref[c, 8 + rows : 9 + rows, :], 0.0
        )
    mid = bend_ref[:, 8 : 8 + rows, :]
    again = 4.0 * mid - (
        bend_ref[:, 7 : 7 + rows, :] + bend_ref[:, 9 : 9 + rows, :] + sides(mid)
    )
    kd_ref[...] = stiff_ref[...][None] * (again + 4.0 * mid)
    copy.wait()


def params():
    return pltpu.CompilerParams(vmem_limit_bytes=LIMIT)


def patch_pairs(d):
    return [(p, p ^ d) for p in range(4)]


def exchange_and_relax(message, displacement, stiffness, kd):
    slabs, owners = lax.axis_size("slab"), lax.axis_size("patch")
    rows = displacement.shape[1]
    sources = slabs * owners
    got = lax.all_to_all(
        message.reshape(sources, 8, 128), ("slab", "patch"), 0, 0, tiled=True
    )
    reply = jax.ShapeDtypeStruct((8, 256), F32)
    new, *replies = pl.pallas_call(
        owner_kernel,
        out_shape=(jax.ShapeDtypeStruct(displacement.shape, F32),) + (reply,) * 4,
        in_specs=vmem(4),
        out_specs=vmem(5),
        scratch_shapes=[
            pltpu.VMEM((2, sources, 128), F32),
            pltpu.VMEM((2, sources, 128), F32),
        ],
        compiler_params=params(),
        name="owner",
    )(got, displacement, stiffness, kd)
    back = [replies[0]] + [
        lax.ppermute(replies[d], "patch", patch_pairs(d)) for d in (1, 2, 3)
    ]
    wall = pl.pallas_call(
        finish_kernel,
        out_shape=jax.ShapeDtypeStruct((3, 1, 1, owners * 256), F32),
        in_specs=vmem(4),
        out_specs=pl.BlockSpec(memory_space=pltpu.VMEM),
        compiler_params=params(),
        name="finish",
    )(*back)
    return store(new, "store_shell"), wall


def halves(value):
    high = value.astype(BF)
    low = (value - high.astype(F32)).astype(BF)
    return jnp.concatenate([high.astype(F32), low.astype(F32)], axis=1)


def lines_of(scale_ref, pad_ref):
    pad_ref[...] = jnp.zeros_like(pad_ref)
    pad_ref[0:2, 0 : scale_ref.shape[1]] = scale_ref[...]
    return pltpu.roll(pad_ref[...], 8, 1)


def near_kernel(
    state_hbm, rhs_hbm, scale_hbm, disp_hbm, near_ref, own_ref, one_ref, three_ref,
    state_ref, rhs_ref, scale_ref, disp_ref, pad_ref, build_ref, sems,
):
    copies = [
        pltpu.make_async_copy(a, b, sems.at[i])
        for i, (a, b) in enumerate(
            (
                (scale_hbm, scale_ref),
                (state_hbm, state_ref),
                (rhs_hbm, rhs_ref),
                (disp_hbm, disp_ref),
            )
        )
    ]
    for copy in copies:
        copy.start()
    odd = lax.axis_index("slab") % 2
    even = lax.axis_index("patch") % 2 == 0
    cols = state_ref.shape[1]
    for copy in copies:
        copy.wait()
    for e in range(2):
        build_ref[e] = jnp.zeros((EDGE + 8, 256), F32)
    for i, row in enumerate((odd, 1 - odd)):
        for part, ref, at, third in (
            (0, state_ref, 2 * i, 8 + i),
            (2, rhs_ref, (4, 10)[i], None),
        ):
            value = ref[row]
            block = part + i
            own_ref[block * cols : (block + 1) * cols, :] = value.astype(BF)
            low, high = value[0:2], value[cols - 2 : cols]
            build_ref[0, at : at + 2, :] = jnp.where(even, high, low)
            build_ref[1, at : at + 2, :] = jnp.where(even, low, high)
            if third is not None:
                low, high = value[2:3], value[cols - 3 : cols - 2]
                build_ref[0, third : third + 1, :] = jnp.where(even, high, low)
                build_ref[1, third : third + 1, :] = jnp.where(even, low, high)
    near_ref[...] = state_ref[1 - odd].astype(BF)
    lines = lines_of(scale_ref, pad_ref)
    flip = odd == 1
    first = jnp.where(flip, lines[1:2], lines[0:1])
    second = jnp.where(flip, lines[0:1], lines[1:2])
    pair = jnp.concatenate([halves(first), halves(second), jnp.zeros((6, 256), F32)], axis=0)
    own_ref[4 * cols :, :] = pair.astype(BF)
    for e in range(2):
        build_ref[e, 6:8, :] = pair[0:2]
    rows = disp_ref.shape[1]
    for c in range(3):
        top = halves(disp_ref[c, 0:2, :])
        bottom = halves(disp_ref[c, rows - 2 : rows, :])
        at = EDGE + 2 * c
        build_ref[0, at : at + 2, :] = jnp.where(even, bottom, top)
        build_ref[1, at : at + 2, :] = jnp.where(even, top, bottom)
    one_ref[...] = build_ref[0].astype(BF)
    three_ref[...] = build_ref[1].astype(BF)


def first_kernel(
    state_ref,
    rhs_ref,
    scale_ref,
    near_ref,
    inner_ref,
    outer_ref,
    one_ref,
    three_ref,
    matrix_ref,
    x_ref,
    y_ref,
    inverse_ref,
    tmap_ref,
    elem_hbm,
    point_hbm,
    count_hbm,
    keep_ref,
    rest_ref,
    hot_ref,
    part_ref,
    v_ref,
    r_ref,
    s_ref,
    i_ref,
    line_ref,
    elem_ref,
    point_ref,
    count_ref,
    sems,
):
    copies = [
        pltpu.make_async_copy(a, b, sems.at[i])
        for i, (a, b) in enumerate(
            ((elem_hbm, elem_ref), (point_hbm, point_ref), (count_hbm, count_ref))
        )
    ]
    for copy in copies:
        copy.start()
    slab, patch = lax.axis_index("slab"), lax.axis_index("patch")
    last_slab, last_patch = lax.axis_size("slab") - 1, lax.axis_size("patch") - 1
    odd = slab % 2
    even = patch % 2 == 0
    cols, width = state_ref.shape[1], state_ref.shape[2]
    wide = cols + 16
    inside = (slab > 0) & (slab < last_slab)
    col = iota((wide, width), 0)
    valid = (col >= 8) & (col < 8 + cols)
    valid = valid | ((col < 8) & (patch > 0)) | ((col >= 8 + cols) & (patch < last_patch))
    edge = valid.astype(F32)
    keep = edge * inside.astype(F32)
    v_ref[:, 0:8, :] = jnp.zeros((7, 8, width), F32)
    v_ref[:, 8 + cols :, :] = jnp.zeros((7, 8, width), F32)
    r_ref[:, 0:8, :] = jnp.zeros((6, 8, width), F32)
    r_ref[:, 8 + cols :, :] = jnp.zeros((6, 8, width), F32)
    head = 5 * cols + 8
    tail = 3 * cols + 8
    strips = {
        0: (one_ref[0:EDGE], three_ref[0:EDGE]),
        1: (inner_ref[tail : tail + EDGE], inner_ref[tail + EDGE : tail + 2 * EDGE]),
        2: (outer_ref[head : head + THIN], outer_ref[head + THIN : head + 2 * THIN]),
    }
    sides = {}
    for kind, pair in strips.items():
        one, three = (x.astype(F32) for x in pair)
        sides[kind] = (jnp.where(even, three, one), jnp.where(even, one, three))
    lane = iota((1, 128), 1)
    line_ref[...] = jnp.zeros_like(line_ref)
    line_ref[0:2, 0:cols] = scale_ref[...]
    exact = pltpu.roll(line_ref[...], 8, 1)
    table = ((2, 1), (2, 0), (0, 0), (0, 1), (1, 1), (1, 0))
    for r, (kind, i) in enumerate(table):
        if kind == 0:
            row = odd if i == 0 else 1 - odd
            v_ref[r + 1, 8 : 8 + cols, :] = state_ref[row]
            r_ref[r, 8 : 8 + cols, :] = rhs_ref[row]
            line = jnp.where(row == 1, exact[1:2], exact[0:1])
        else:
            if kind == 1:
                value = near_ref[...] if i == 1 else inner_ref[0:cols]
                ref, at = inner_ref, (i + 1) * cols
            else:
                value = outer_ref[i * cols : (i + 1) * cols]
                ref, at = outer_ref, (i + 2) * cols
            v_ref[r + 1, 8 : 8 + cols, :] = value.astype(F32)
            r_ref[r, 8 : 8 + cols, :] = ref[at : at + cols, :].astype(F32)
            below = (3 if kind == 1 else 4) * cols
            both = ref[below : below + 8, :].astype(F32)[i : i + 1]
            line = both[:, :128] + both[:, 128:]
        for side, start, far in zip(sides[kind], (6, 8 + cols), (5, 10 + cols)):
            v_ref[r + 1, start : start + 2, :] = side[2 * i : 2 * i + 2]
            if i == 0:
                r_ref[r, start : start + 2, :] = side[4:6]
            elif kind < 2:
                r_ref[r, start : start + 2, :] = side[10:12]
            if kind == 0:
                v_ref[r + 1, far : far + 1, :] = side[8 + i : 9 + i]
            both = side[6 + i : 7 + i]
            far = pltpu.roll(both[:, :128] + both[:, 128:], 64, 1)
            here = (lane >= start) & (lane < start + 2)
            line = jnp.where(here, far, line)
        line_ref[r : r + 1, :] = jnp.where(line > 0.0, line, 1.0)
    line_ref[6:8, :] = jnp.ones((2, 128), F32)
    v_ref[0, 8 : 8 + cols, :] = outer_ref[4 * cols + 8 : head, :].astype(F32)
    for r in range(7):
        v_ref[r] = v_ref[r] * (keep if r < 3 else edge)
    lines = line_ref[...]
    columns = jnp.transpose(lines)
    inverses = jnp.transpose(1.0 / lines)
    for r in range(6):
        s_ref[r] = jnp.broadcast_to(columns[:wide, r : r + 1], (wide, width))
        i_ref[r] = jnp.broadcast_to(inverses[:wide, r : r + 1], (wide, width))
    for sweep in range(SWEEPS):
        a, b = 1 + sweep, 6 - sweep
        n = b - a
        if sweep == 0:
            keep_ref[0:2] = v_ref[5:7]
        elif sweep == 1:
            keep_ref[2:4] = v_ref[4:6]
        else:
            keep_ref[4:6] = v_ref[3:5]
        value = relaxed(
            v_ref[a:b],
            v_ref[a - 1 : b - 1],
            v_ref[a + 1 : b + 1],
            r_ref[a - 1 : b - 1],
            s_ref[a - 1 : b - 1],
            i_ref[a - 1 : b - 1],
            (matrix_ref, x_ref, y_ref, inverse_ref),
        )
        for j in range(n):
            v_ref[a + j] = value[j] * (keep if a + j < 3 else edge)
    keep_ref[6] = v_ref[3]
    for i, ref in enumerate((r_ref, s_ref, i_ref)):
        rest_ref[3 * i : 3 * i + 3] = ref[3:6]
    for copy in copies:
        copy.wait()
    elem = elem_ref[0]
    live, code = slot_codes(point_ref[0], count_ref.at[0], part_ref.shape[0])
    place = iota((cols, elem.shape[1]), 0)
    hot = ((place + odd * cols == elem) & live).astype(F32).astype(BF)
    hot_ref[...] = ((place + (1 - odd) * cols == elem) & live).astype(F32).astype(BF)
    final = v_ref[3, 8 : 8 + cols, :].astype(BF)
    pull = jnp.dot(nt(tmap_ref[...], final).astype(BF), hot, preferred_element_type=F32)
    message_rows(pull, part_ref)
    for k in range(part_ref.shape[0]):
        for h in range(2):
            start = k * 256 + h * 128
            part_ref[k, 6 + h : 7 + h, :] = code[:, start : start + 128]


def message_rows(pull, rows_ref):
    for k in range(rows_ref.shape[0]):
        for j in range(3):
            for h in range(2):
                start = k * 256 + h * 128
                rows_ref[k, 2 * j + h : 2 * j + h + 1, :] = pull[j : j + 1, start : start + 128]


def relaxed(center, up, down, rhs, scale, inverse_scale, matrices):
    matrix_ref, x_ref, y_ref, inverse_ref = matrices
    n, wide, width = center.shape
    flat = (n * wide, width)
    up, mid, down = (x.astype(BF).astype(F32) for x in (up, center, down))
    nx = (up + down).astype(BF)
    ny = (pltpu.roll(mid, 1, 1) + pltpu.roll(mid, wide - 1, 1)).astype(BF)
    own = jnp.dot(mid.astype(BF).reshape(flat), matrix_ref[...], preferred_element_type=F32)
    side = jnp.dot(nx.reshape(flat), x_ref[...], preferred_element_type=F32)
    side += jnp.dot(ny.reshape(flat), y_ref[...], preferred_element_type=F32)
    residue = (rhs.reshape(flat) - (scale.reshape(flat) * own - side)).astype(BF)
    update = jnp.dot(residue, inverse_ref[...], preferred_element_type=F32)
    update = update * inverse_scale.reshape(flat)
    return center + update.reshape(center.shape)


def last_kernel(
    keep_ref, rest_ref, hot_ref, part_ref, relay_ref, matrix_ref, x_ref, y_ref, inverse_ref,
    tmap_ref, out_ref, message_hbm, far_ref, rows_ref, message_ref, sems,
):
    slab = lax.axis_index("slab")
    last_slab = lax.axis_size("slab") - 1
    odd = slab % 2
    cols = relay_ref.shape[0]
    matrices = (matrix_ref, x_ref, y_ref, inverse_ref)
    beyond = (slab != 1) & (slab != last_slab - 1)
    far_ref[...] = jnp.zeros_like(far_ref)
    far_ref[0, 8 : 8 + cols, :] = relay_ref[...].astype(F32) * beyond.astype(F32)

    def step(center, up, down, r):
        return relaxed(
            center, up, down, rest_ref[r : r + 1], rest_ref[3 + r : 4 + r],
            rest_ref[6 + r : 7 + r], matrices,
        )

    far = step(keep_ref[1:2], keep_ref[0:1], far_ref[...], 2)
    near = step(keep_ref[3:4], keep_ref[2:3], far, 1)
    own = step(keep_ref[5:6], keep_ref[4:5], near, 0)
    far_ref[...] = own
    inner = far_ref[0, 8 : 8 + cols, :]
    out_ref[odd] = keep_ref[6, 8 : 8 + cols, :]
    out_ref[1 - odd] = inner
    pull = jnp.dot(
        nt(tmap_ref[...], inner.astype(BF)).astype(BF), hot_ref[...], preferred_element_type=F32
    )
    message_rows(pull, rows_ref)
    owners = rows_ref.shape[0]
    for k in range(owners):
        rows_ref[k, 6:8, :] = jnp.zeros((2, 128), F32)
    rows = (rows_ref[...] + part_ref[...]).astype(BF)
    message_ref[...] = jnp.broadcast_to(rows[None], message_ref.shape)
    part = message_ref.shape[0]
    copies = [
        pltpu.make_async_copy(message_ref, message_hbm.at[i * part : (i + 1) * part], sems.at[i])
        for i in range(message_hbm.shape[0] // part)
    ]
    for copy in copies:
        copy.start()
    for copy in copies:
        copy.wait()


def call(kernel, name, out_shape, operands, scratch=(), in_specs=None, out_specs=None):
    return pl.pallas_call(
        kernel,
        out_shape=out_shape,
        in_specs=in_specs or vmem(len(operands)),
        out_specs=out_specs or jax.tree.map(lambda _: vmem(1)[0], out_shape),
        scratch_shapes=list(scratch),
        compiler_params=params(),
        name=name,
    )(*operands)


def shards(
    fluid_state,
    fluid_rhs,
    element_scale,
    element_matrix,
    couple_x,
    couple_y,
    block_inverse,
    traction_map,
    slot_elem,
    slot_point,
    slot_count,
    displacement,
    stiffness,
):
    cols, width = fluid_state.shape[1:]
    slots = slot_elem.shape[2]
    slabs, owners = lax.axis_size("slab"), lax.axis_size("patch")
    shape = jax.ShapeDtypeStruct
    inner_pairs = [(s, s ^ 1) for s in range(slabs)]
    outer_pairs = [(s, (s + 1) % slabs) for s in range(1, slabs, 2)]
    outer_pairs = outer_pairs + [(b, a) for a, b in outer_pairs]
    strip = shape((EDGE + 8, width), BF)
    near, own, to_one, to_three = call(
        near_kernel,
        "near",
        (shape((cols, width), BF), shape((4 * cols + 8, width), BF), strip, strip),
        tuple(
            pltpu.with_memory_space_constraint(x, pltpu.HBM)
            for x in (fluid_state, fluid_rhs, element_scale, displacement)
        ),
        [
            pltpu.VMEM(fluid_state.shape, F32),
            pltpu.VMEM(fluid_rhs.shape, F32),
            pltpu.VMEM(element_scale.shape, F32),
            pltpu.VMEM(displacement.shape, F32),
            pltpu.VMEM((8, 128), F32),
            pltpu.VMEM((2, EDGE + 8, width), F32),
            pltpu.SemaphoreType.DMA((4,)),
        ],
        in_specs=hbm(4),
    )
    inner_near = lax.ppermute(near, "slab", inner_pairs)
    from_three = lax.ppermute(to_three, "patch", patch_pairs(3))
    from_one = lax.ppermute(to_one, "patch", patch_pairs(1))
    strips = [from_one[:EDGE], from_three[:EDGE]]
    thin = [from_one[:THIN], from_three[:THIN]]
    outer = lax.ppermute(jnp.concatenate([own, inner_near] + thin), "slab", outer_pairs)
    inner = lax.ppermute(
        jnp.concatenate([own[:cols], own[2 * cols :]] + strips), "slab", inner_pairs
    )
    relay = lax.ppermute(outer[:cols], "slab", inner_pairs)
    wide = cols + 16
    rows = shape((owners, 8, 128), F32)
    matrices = (element_matrix, couple_x, couple_y, block_inverse)
    left = call(
        first_kernel,
        "first",
        (
            shape((7, wide, width), F32),
            shape((9, wide, width), F32),
            shape((cols, slots), BF),
            rows,
        ),
        (
            fluid_state,
            fluid_rhs,
            element_scale,
            inner_near,
            inner,
            outer,
            from_one,
            from_three,
            *matrices,
            traction_map,
            slot_elem,
            slot_point,
            slot_count,
        ),
        [
            pltpu.VMEM((7, wide, width), F32),
            pltpu.VMEM((6, wide, width), F32),
            pltpu.VMEM((6, wide, width), F32),
            pltpu.VMEM((6, wide, width), F32),
            pltpu.VMEM((8, 128), F32),
            pltpu.VMEM((1, 1, slots), I32),
            pltpu.VMEM((1, 1, slots), I32),
            pltpu.VMEM((1, 1, owners), I32),
            pltpu.SemaphoreType.DMA((3,)),
        ],
        in_specs=vmem(13) + hbm(3),
    )
    state, message = call(
        last_kernel,
        "last",
        (shape(fluid_state.shape, F32), shape((slabs, owners, 8, 128), BF)),
        (*left, relay, *matrices, traction_map),
        [
            pltpu.VMEM((1, wide, width), F32),
            pltpu.VMEM((owners, 8, 128), F32),
            pltpu.VMEM((slabs // 4, owners, 8, 128), BF),
            pltpu.SemaphoreType.DMA((4,)),
        ],
        out_specs=tuple(vmem(1) + hbm(1)),
    )
    kd, final = call(
        shell_kernel,
        "shell",
        (shape(displacement.shape, F32), shape(state.shape, F32)),
        (from_one, from_three, displacement, stiffness, state),
        [pltpu.VMEM((3, displacement.shape[1] + 16, 128), F32)] * 2 + [pltpu.SemaphoreType.DMA],
        out_specs=tuple(vmem(1) + hbm(1)),
    )
    new, wall = exchange_and_relax(message, displacement, stiffness, kd)
    return final, new, wall


def solution(mesh):
    return jax.shard_map(
        shards,
        mesh=mesh,
        in_specs=(
            P("slab", "patch", None),
            P("slab", "patch", None),
            P("slab", "patch"),
            P(),
            P(),
            P(),
            P(),
            P(),
            P("slab", "patch", None),
            P("slab", "patch", None),
            P("slab", "patch", None),
            P(None, "patch", None),
            P("patch", None),
        ),
        out_specs=(
            P("slab", "patch", None),
            P(None, "patch", None),
            P(None, "slab", "patch", None),
        ),
        check_vma=False,
    )
```

```python
import jax
import jax.numpy as jnp
from jax import lax
from jax.experimental import pallas as pl
from jax.experimental.pallas import tpu as pltpu
from jax.sharding import PartitionSpec as P

SWEEPS = 3
BF = jnp.bfloat16
F32 = jnp.float32
I32 = jnp.int32
LIMIT = 48 << 20
EDGE = 16
THIN = 8


def vmem(n):
    return [pl.BlockSpec(memory_space=pltpu.VMEM)] * n


def hbm(n):
    return [pl.BlockSpec(memory_space=pltpu.HBM)] * n


def iota(shape, dim):
    return lax.broadcasted_iota(I32, shape, dim)


def nt(a, b):
    return lax.dot_general(a, b, (((1,), (1,)), ((), ())), preferred_element_type=F32)


def slot_codes(point, count_ref, owners):
    slots = point.shape[1]
    cap = slots // owners
    slot = iota((1, slots), 1)
    owner = slot // cap
    limit = jnp.zeros((1, slots), I32)
    for k in range(owners):
        limit = jnp.where(owner == k, count_ref[0:1, k : k + 1], limit)
    live = (slot - owner * cap) < limit
    row = point // 128
    code = (128 + (point - row * 128)).astype(F32)
    for b in range(6):
        code = code * jnp.where((row >> b) & 1 == 1, F32(2.0 ** (2**b)), F32(1.0))
    return live, jnp.where(live, code, 0.0)


def decode(code):
    row = jnp.zeros(code.shape, F32)
    for b in (5, 4, 3, 2, 1, 0):
        big = code >= F32(128.0 * 2.0 ** (2**b))
        row = row + jnp.where(big, F32(2**b), 0.0)
        code = code * jnp.where(big, F32(2.0 ** -(2**b)), 1.0)
    return row, code - 128.0


def owner_kernel(
    got_ref, disp_ref, stiff_ref, kd_ref, new_ref, r0, r1, r2, r3, row_ref, lane_ref
):
    replies = (r0, r1, r2, r3)
    sources = got_ref.shape[0]
    rows = disp_ref.shape[1]
    patch = lax.axis_index("patch")
    first = lax.axis_index("slab") * 4
    for h in range(2):
        row, lane = decode(got_ref[:, 6 + h, :].astype(F32))
        row_ref[h] = row
        lane_ref[h] = lane
    row_ids = iota((rows, 128), 0).astype(F32).astype(BF)
    lane_ids = iota((128, 128), 0).astype(F32).astype(BF)
    none = jnp.zeros((rows, 128), BF)
    ones, zeros = jnp.ones((128, 128), BF), jnp.zeros((128, 128), BF)
    total = jnp.zeros((3 * rows, 128), F32)
    group = 8
    for base in range(0, sources, group):
        row8 = [row_ref[h, base : base + group, :].astype(BF) for h in range(2)]
        lane8 = [lane_ref[h, base : base + group, :].astype(BF) for h in range(2)]
        for g in range(group):
            vals = got_ref[base + g]
            left, right = [], []
            for h in range(2):
                mask = row_ids == row8[h][g : g + 1]
                left.append(
                    jnp.concatenate(
                        [jnp.where(mask, vals[2 * c + h : 2 * c + h + 1], none) for c in range(3)],
                        axis=0,
                    )
                )
                right.append(jnp.where(lane_ids == lane8[h][g : g + 1], ones, zeros))
            total += nt(jnp.concatenate(left, axis=1), jnp.concatenate(right, axis=1))
    loads = total.reshape(3, rows, 128)
    new = disp_ref[...] + (loads - kd_ref[...]) / (36.0 * stiff_ref[...])[None]
    new_ref[...] = new
    flat = new.reshape(3 * rows, 128)
    high = flat.astype(BF)
    low = (flat - high.astype(F32)).astype(BF)
    row_ids = iota((rows, 128), 0).astype(F32)
    for d in range(4):
        src = first + (patch ^ d)
        for h in range(2):
            row = row_ref[h, pl.ds(src, 1), :]
            lane = lane_ref[h, pl.ds(src, 1), :]
            hot = jnp.where(lane_ids == lane.astype(BF), ones, zeros)
            picked = jnp.dot(high, hot, preferred_element_type=F32)
            picked += jnp.dot(low, hot, preferred_element_type=F32)
            mask = row_ids == row
            for c in range(3):
                part = jnp.where(mask, picked[c * rows : (c + 1) * rows], 0.0)
                replies[d][c : c + 1, h * 128 : (h + 1) * 128] = part.sum(axis=0, keepdims=True)


def store_kernel(value_ref, out_ref, sem):
    copy = pltpu.make_async_copy(value_ref, out_ref, sem)
    copy.start()
    copy.wait()


def store(value, name):
    return pl.pallas_call(
        store_kernel,
        out_shape=jax.ShapeDtypeStruct(value.shape, value.dtype),
        in_specs=vmem(1),
        out_specs=hbm(1)[0],
        scratch_shapes=[pltpu.SemaphoreType.DMA],
        compiler_params=params(),
        name=name,
    )(value)


def finish_kernel(r0, r1, r2, r3, out_ref):
    cap = r0.shape[1]
    patch = lax.axis_index("patch")
    for d, reply in enumerate((r0, r1, r2, r3)):
        start = pl.multiple_of((patch ^ d) * cap, cap)
        for c in range(3):
            out_ref[c, 0, :, pl.ds(start, cap)] = reply[c : c + 1, :]


def shell_kernel(
    one_ref, three_ref, disp_ref, stiff_ref, state_ref, kd_ref, out_ref, field_ref, bend_ref, sem
):
    copy = pltpu.make_async_copy(state_ref, out_ref, sem)
    copy.start()
    rows = disp_ref.shape[1]
    patch = lax.axis_index("patch")
    top = patch > 0
    bottom = patch < 3
    even = patch % 2 == 0
    one, three = (
        ref[:, :128].astype(F32) + ref[:, 128:].astype(F32)
        for ref in (one_ref, three_ref)
    )
    above = jnp.where(even, three, one)
    below = jnp.where(even, one, three)
    field_ref[...] = jnp.zeros_like(field_ref)
    bend_ref[...] = jnp.zeros_like(bend_ref)
    field_ref[:, 8 : 8 + rows, :] = disp_ref[...]
    lane = iota((1, 1, 128), 2)

    def sides(x):
        left = jnp.where(lane == 0, 0.0, pltpu.roll(x, 1, 2))
        right = jnp.where(lane == 127, 0.0, pltpu.roll(x, 127, 2))
        return left + right

    for c in range(3):
        field_ref[c, 6:8, :] = jnp.where(top, above[2 * c : 2 * c + 2], 0.0)
        field_ref[c, 8 + rows : 10 + rows, :] = jnp.where(bottom, below[2 * c : 2 * c + 2], 0.0)
    mid = field_ref[:, 7 : 9 + rows, :]
    bend = 4.0 * mid - (
        field_ref[:, 6 : 8 + rows, :] + field_ref[:, 8 : 10 + rows, :] + sides(mid)
    )
    bend_ref[:, 7 : 9 + rows, :] = bend
    for c in range(3):
        bend_ref[c, 7:8, :] = jnp.where(top, bend_ref[c, 7:8, :], 0.0)
        bend_ref[c, 8 + rows : 9 + rows, :] = jnp.where(
            bottom, bend_ref[c, 8 + rows : 9 + rows, :], 0.0
        )
    mid = bend_ref[:, 8 : 8 + rows, :]
    again = 4.0 * mid - (
        bend_ref[:, 7 : 7 + rows, :] + bend_ref[:, 9 : 9 + rows, :] + sides(mid)
    )
    kd_ref[...] = stiff_ref[...][None] * (again + 4.0 * mid)
    copy.wait()


def params():
    return pltpu.CompilerParams(vmem_limit_bytes=LIMIT)


def patch_pairs(d):
    return [(p, p ^ d) for p in range(4)]


def exchange_and_relax(message, displacement, stiffness, kd):
    slabs, owners = lax.axis_size("slab"), lax.axis_size("patch")
    rows = displacement.shape[1]
    sources = slabs * owners
    got = lax.all_to_all(
        message.reshape(sources, 8, 128), ("slab", "patch"), 0, 0, tiled=True
    )
    reply = jax.ShapeDtypeStruct((8, 256), F32)
    new, *replies = pl.pallas_call(
        owner_kernel,
        out_shape=(jax.ShapeDtypeStruct(displacement.shape, F32),) + (reply,) * 4,
        in_specs=vmem(4),
        out_specs=vmem(5),
        scratch_shapes=[
            pltpu.VMEM((2, sources, 128), F32),
            pltpu.VMEM((2, sources, 128), F32),
        ],
        compiler_params=params(),
        name="owner",
    )(got, displacement, stiffness, kd)
    back = [replies[0]] + [
        lax.ppermute(replies[d], "patch", patch_pairs(d)) for d in (1, 2, 3)
    ]
    wall = pl.pallas_call(
        finish_kernel,
        out_shape=jax.ShapeDtypeStruct((3, 1, 1, owners * 256), F32),
        in_specs=vmem(4),
        out_specs=pl.BlockSpec(memory_space=pltpu.VMEM),
        compiler_params=params(),
        name="finish",
    )(*back)
    return store(new, "store_shell"), wall


def halves(value):
    high = value.astype(BF)
    low = (value - high.astype(F32)).astype(BF)
    return jnp.concatenate([high.astype(F32), low.astype(F32)], axis=1)


def lines_of(scale_ref, pad_ref):
    pad_ref[...] = jnp.zeros_like(pad_ref)
    pad_ref[0:2, 0 : scale_ref.shape[1]] = scale_ref[...]
    return pltpu.roll(pad_ref[...], 8, 1)


def near_kernel(
    state_hbm, rhs_hbm, scale_hbm, disp_hbm, near_ref, own_ref, one_ref, three_ref,
    state_ref, rhs_ref, scale_ref, disp_ref, pad_ref, build_ref, sems,
):
    copies = [
        pltpu.make_async_copy(a, b, sems.at[i])
        for i, (a, b) in enumerate(
            (
                (scale_hbm, scale_ref),
                (state_hbm, state_ref),
                (rhs_hbm, rhs_ref),
                (disp_hbm, disp_ref),
            )
        )
    ]
    for copy in copies:
        copy.start()
    odd = lax.axis_index("slab") % 2
    even = lax.axis_index("patch") % 2 == 0
    cols = state_ref.shape[1]
    for copy in copies:
        copy.wait()
    for e in range(2):
        build_ref[e] = jnp.zeros((EDGE + 8, 256), F32)
    for i, row in enumerate((odd, 1 - odd)):
        for part, ref, at, third in (
            (0, state_ref, 2 * i, 8 + i),
            (2, rhs_ref, (4, 10)[i], None),
        ):
            value = ref[row]
            block = part + i
            own_ref[block * cols : (block + 1) * cols, :] = value.astype(BF)
            low, high = value[0:2], value[cols - 2 : cols]
            build_ref[0, at : at + 2, :] = jnp.where(even, high, low)
            build_ref[1, at : at + 2, :] = jnp.where(even, low, high)
            if third is not None:
                low, high = value[2:3], value[cols - 3 : cols - 2]
                build_ref[0, third : third + 1, :] = jnp.where(even, high, low)
                build_ref[1, third : third + 1, :] = jnp.where(even, low, high)
    near_ref[...] = state_ref[1 - odd].astype(BF)
    lines = lines_of(scale_ref, pad_ref)
    flip = odd == 1
    first = jnp.where(flip, lines[1:2], lines[0:1])
    second = jnp.where(flip, lines[0:1], lines[1:2])
    pair = jnp.concatenate([halves(first), halves(second), jnp.zeros((6, 256), F32)], axis=0)
    own_ref[4 * cols :, :] = pair.astype(BF)
    for e in range(2):
        build_ref[e, 6:8, :] = pair[0:2]
    rows = disp_ref.shape[1]
    for c in range(3):
        top = halves(disp_ref[c, 0:2, :])
        bottom = halves(disp_ref[c, rows - 2 : rows, :])
        at = EDGE + 2 * c
        build_ref[0, at : at + 2, :] = jnp.where(even, bottom, top)
        build_ref[1, at : at + 2, :] = jnp.where(even, top, bottom)
    one_ref[...] = build_ref[0].astype(BF)
    three_ref[...] = build_ref[1].astype(BF)


def sweep_kernel(
    state_ref,
    rhs_ref,
    scale_ref,
    near_ref,
    inner_ref,
    outer_ref,
    rest_ref,
    one_ref,
    three_ref,
    relay_ref,
    matrix_ref,
    x_ref,
    y_ref,
    inverse_ref,
    tmap_ref,
    elem_hbm,
    point_hbm,
    count_hbm,
    out_ref,
    message_hbm,
    v_ref,
    r_ref,
    s_ref,
    i_ref,
    line_ref,
    elem_ref,
    point_ref,
    count_ref,
    rows_ref,
    message_ref,
    sems,
):
    copies = [
        pltpu.make_async_copy(a, b, sems.at[i])
        for i, (a, b) in enumerate(
            ((elem_hbm, elem_ref), (point_hbm, point_ref), (count_hbm, count_ref))
        )
    ]
    for copy in copies:
        copy.start()
    slab, patch = lax.axis_index("slab"), lax.axis_index("patch")
    last_slab, last_patch = lax.axis_size("slab") - 1, lax.axis_size("patch") - 1
    odd = slab % 2
    even = patch % 2 == 0
    cols, width = state_ref.shape[1], state_ref.shape[2]
    wide = cols + 16
    inside = (slab > 0) & (slab < last_slab)
    col = iota((wide, width), 0)
    valid = (col >= 8) & (col < 8 + cols)
    valid = valid | ((col < 8) & (patch > 0)) | ((col >= 8 + cols) & (patch < last_patch))
    edge = valid.astype(F32)
    keep = edge * inside.astype(F32)
    v_ref[:, 0:8, :] = jnp.zeros((8, 8, width), F32)
    v_ref[:, 8 + cols :, :] = jnp.zeros((8, 8, width), F32)
    r_ref[:, 0:8, :] = jnp.zeros((6, 8, width), F32)
    r_ref[:, 8 + cols :, :] = jnp.zeros((6, 8, width), F32)
    tail = 3 * cols + 8
    strips = {
        0: (one_ref[0:EDGE], three_ref[0:EDGE]),
        1: (inner_ref[tail : tail + EDGE], inner_ref[tail + EDGE : tail + 2 * EDGE]),
        2: (rest_ref[cols : cols + THIN], rest_ref[cols + THIN : cols + 2 * THIN]),
    }
    sides = {}
    for kind, pair in strips.items():
        one, three = (x.astype(F32) for x in pair)
        sides[kind] = (jnp.where(even, three, one), jnp.where(even, one, three))
    lane = iota((1, 128), 1)
    line_ref[...] = jnp.zeros_like(line_ref)
    line_ref[0:2, 0:cols] = scale_ref[...]
    exact = pltpu.roll(line_ref[...], 8, 1)
    table = ((2, 1), (2, 0), (0, 0), (0, 1), (1, 1), (1, 0))
    for r, (kind, i) in enumerate(table):
        if kind == 0:
            row = odd if i == 0 else 1 - odd
            v_ref[r + 1, 8 : 8 + cols, :] = state_ref[row]
            r_ref[r, 8 : 8 + cols, :] = rhs_ref[row]
            line = jnp.where(row == 1, exact[1:2], exact[0:1])
        else:
            if kind == 1:
                value = near_ref[...] if i == 1 else inner_ref[0:cols]
                ref, at = inner_ref, (i + 1) * cols
            else:
                value = outer_ref[i * cols : (i + 1) * cols]
                ref, at = outer_ref, (i + 2) * cols
            v_ref[r + 1, 8 : 8 + cols, :] = value.astype(F32)
            r_ref[r, 8 : 8 + cols, :] = ref[at : at + cols, :].astype(F32)
            below = (3 if kind == 1 else 4) * cols
            both = ref[below : below + 8, :].astype(F32)[i : i + 1]
            line = both[:, :128] + both[:, 128:]
        for side, start, far in zip(sides[kind], (6, 8 + cols), (5, 10 + cols)):
            v_ref[r + 1, start : start + 2, :] = side[2 * i : 2 * i + 2]
            if i == 0:
                r_ref[r, start : start + 2, :] = side[4:6]
            elif kind < 2:
                r_ref[r, start : start + 2, :] = side[10:12]
            if kind == 0:
                v_ref[r + 1, far : far + 1, :] = side[8 + i : 9 + i]
            both = side[6 + i : 7 + i]
            far = pltpu.roll(both[:, :128] + both[:, 128:], 64, 1)
            here = (lane >= start) & (lane < start + 2)
            line = jnp.where(here, far, line)
        line_ref[r : r + 1, :] = jnp.where(line > 0.0, line, 1.0)
    line_ref[6:8, :] = jnp.ones((2, 128), F32)
    v_ref[0, 8 : 8 + cols, :] = rest_ref[0:cols, :].astype(F32)
    beyond = (slab != 1) & (slab != last_slab - 1)
    v_ref[7, 8 : 8 + cols, :] = relay_ref[...].astype(F32) * beyond.astype(F32)
    for r in range(8):
        v_ref[r] = v_ref[r] * (keep if r < 3 else edge)
    lines = line_ref[...]
    columns = jnp.transpose(lines)
    inverses = jnp.transpose(1.0 / lines)
    for r in range(6):
        s_ref[r] = jnp.broadcast_to(columns[:wide, r : r + 1], (wide, width))
        i_ref[r] = jnp.broadcast_to(inverses[:wide, r : r + 1], (wide, width))
    for sweep in range(SWEEPS):
        a, b = 1 + sweep, 7 - sweep
        value = relaxed(
            v_ref[a:b],
            v_ref[a - 1 : b - 1],
            v_ref[a + 1 : b + 1],
            r_ref[a - 1 : b - 1],
            s_ref[a - 1 : b - 1],
            i_ref[a - 1 : b - 1],
            (matrix_ref, x_ref, y_ref, inverse_ref),
        )
        for j in range(b - a):
            v_ref[a + j] = value[j] * (keep if a + j < 3 else edge)
    out_ref[odd] = v_ref[3, 8 : 8 + cols, :]
    out_ref[1 - odd] = v_ref[4, 8 : 8 + cols, :]
    final = out_ref[...].astype(BF).reshape(2 * cols, width)
    for copy in copies:
        copy.wait()
    elem = elem_ref[0]
    owners = rows_ref.shape[0]
    live, code = slot_codes(point_ref[0], count_ref.at[0], owners)
    hot = ((iota((2 * cols, elem.shape[1]), 0) == elem) & live).astype(F32).astype(BF)
    pull = jnp.dot(nt(tmap_ref[...], final).astype(BF), hot, preferred_element_type=F32)
    for k in range(owners):
        for j in range(4):
            source = code if j == 3 else pull[j : j + 1]
            for h in range(2):
                start = k * 256 + h * 128
                rows_ref[k, 2 * j + h : 2 * j + h + 1, :] = source[:, start : start + 128]
    message_ref[...] = jnp.broadcast_to(rows_ref[...].astype(BF)[None], message_ref.shape)
    part = message_ref.shape[0]
    copies = [
        pltpu.make_async_copy(message_ref, message_hbm.at[i * part : (i + 1) * part], sems.at[3 + i])
        for i in range(message_hbm.shape[0] // part)
    ]
    for copy in copies:
        copy.start()
    for copy in copies:
        copy.wait()


def relaxed(center, up, down, rhs, scale, inverse_scale, matrices):
    matrix_ref, x_ref, y_ref, inverse_ref = matrices
    n, wide, width = center.shape
    flat = (n * wide, width)
    up, mid, down = (x.astype(BF).astype(F32) for x in (up, center, down))
    nx = (up + down).astype(BF)
    ny = (pltpu.roll(mid, 1, 1) + pltpu.roll(mid, wide - 1, 1)).astype(BF)
    own = jnp.dot(mid.astype(BF).reshape(flat), matrix_ref[...], preferred_element_type=F32)
    side = jnp.dot(nx.reshape(flat), x_ref[...], preferred_element_type=F32)
    side += jnp.dot(ny.reshape(flat), y_ref[...], preferred_element_type=F32)
    residue = (rhs.reshape(flat) - (scale.reshape(flat) * own - side)).astype(BF)
    update = jnp.dot(residue, inverse_ref[...], preferred_element_type=F32)
    update = update * inverse_scale.reshape(flat)
    return center + update.reshape(center.shape)


def call(kernel, name, out_shape, operands, scratch=(), in_specs=None, out_specs=None):
    return pl.pallas_call(
        kernel,
        out_shape=out_shape,
        in_specs=in_specs or vmem(len(operands)),
        out_specs=out_specs or jax.tree.map(lambda _: vmem(1)[0], out_shape),
        scratch_shapes=list(scratch),
        compiler_params=params(),
        name=name,
    )(*operands)


def shards(
    fluid_state,
    fluid_rhs,
    element_scale,
    element_matrix,
    couple_x,
    couple_y,
    block_inverse,
    traction_map,
    slot_elem,
    slot_point,
    slot_count,
    displacement,
    stiffness,
):
    cols, width = fluid_state.shape[1:]
    slots = slot_elem.shape[2]
    slabs, owners = lax.axis_size("slab"), lax.axis_size("patch")
    shape = jax.ShapeDtypeStruct
    inner_pairs = [(s, s ^ 1) for s in range(slabs)]
    outer_pairs = [(s, (s + 1) % slabs) for s in range(1, slabs, 2)]
    outer_pairs = outer_pairs + [(b, a) for a, b in outer_pairs]
    strip = shape((EDGE + 8, width), BF)
    near, own, to_one, to_three = call(
        near_kernel,
        "near",
        (shape((cols, width), BF), shape((4 * cols + 8, width), BF), strip, strip),
        tuple(
            pltpu.with_memory_space_constraint(x, pltpu.HBM)
            for x in (fluid_state, fluid_rhs, element_scale, displacement)
        ),
        [
            pltpu.VMEM(fluid_state.shape, F32),
            pltpu.VMEM(fluid_rhs.shape, F32),
            pltpu.VMEM(element_scale.shape, F32),
            pltpu.VMEM(displacement.shape, F32),
            pltpu.VMEM((8, 128), F32),
            pltpu.VMEM((2, EDGE + 8, width), F32),
            pltpu.SemaphoreType.DMA((4,)),
        ],
        in_specs=hbm(4),
    )
    outer = lax.ppermute(own, "slab", outer_pairs)
    inner_near = lax.ppermute(near, "slab", inner_pairs)
    from_three = lax.ppermute(to_three, "patch", patch_pairs(3))
    from_one = lax.ppermute(to_one, "patch", patch_pairs(1))
    strips = [from_one[:EDGE], from_three[:EDGE]]
    thin = [from_one[:THIN], from_three[:THIN]]
    rest = lax.ppermute(jnp.concatenate([inner_near] + thin), "slab", outer_pairs)
    others = jnp.concatenate([own[:cols], own[2 * cols :]] + strips)
    others, _ = lax.optimization_barrier((others, inner_near))
    inner = lax.ppermute(others, "slab", inner_pairs)
    relay = lax.ppermute(outer[:cols], "slab", inner_pairs)
    wide = cols + 16
    state, message = call(
        sweep_kernel,
        "sweep",
        (shape(fluid_state.shape, F32), shape((slabs, owners, 8, 128), BF)),
        (
            fluid_state,
            fluid_rhs,
            element_scale,
            inner_near,
            inner,
            outer,
            rest,
            from_one,
            from_three,
            relay,
            element_matrix,
            couple_x,
            couple_y,
            block_inverse,
            traction_map,
            slot_elem,
            slot_point,
            slot_count,
        ),
        [
            pltpu.VMEM((8, wide, width), F32),
            pltpu.VMEM((6, wide, width), F32),
            pltpu.VMEM((6, wide, width), F32),
            pltpu.VMEM((6, wide, width), F32),
            pltpu.VMEM((8, 128), F32),
            pltpu.VMEM((1, 1, slots), I32),
            pltpu.VMEM((1, 1, slots), I32),
            pltpu.VMEM((1, 1, owners), I32),
            pltpu.VMEM((owners, 8, 128), F32),
            pltpu.VMEM((slabs // 4, owners, 8, 128), BF),
            pltpu.SemaphoreType.DMA((7,)),
        ],
        in_specs=vmem(15) + hbm(3),
        out_specs=tuple(vmem(1) + hbm(1)),
    )
    kd, final = call(
        shell_kernel,
        "shell",
        (shape(displacement.shape, F32), shape(state.shape, F32)),
        (from_one[EDGE:], from_three[EDGE:], displacement, stiffness, state),
        [pltpu.VMEM((3, displacement.shape[1] + 16, 128), F32)] * 2 + [pltpu.SemaphoreType.DMA],
        out_specs=tuple(vmem(1) + hbm(1)),
    )
    new, wall = exchange_and_relax(message, displacement, stiffness, kd)
    return final, new, wall


def solution(mesh):
    return jax.shard_map(
        shards,
        mesh=mesh,
        in_specs=(
            P("slab", "patch", None),
            P("slab", "patch", None),
            P("slab", "patch"),
            P(),
            P(),
            P(),
            P(),
            P(),
            P("slab", "patch", None),
            P("slab", "patch", None),
            P("slab", "patch", None),
            P(None, "patch", None),
            P("patch", None),
        ),
        out_specs=(
            P("slab", "patch", None),
            P(None, "patch", None),
            P(None, "slab", "patch", None),
        ),
        check_vma=False,
    )
```

```python
import jax
import jax.numpy as jnp
from jax import lax
from jax.experimental import pallas as pl
from jax.experimental.pallas import tpu as pltpu
from jax.sharding import PartitionSpec as P

SWEEPS = 3
BF = jnp.bfloat16
F32 = jnp.float32
I32 = jnp.int32
LIMIT = 48 << 20
EDGE = 16
THIN = 8


def vmem(n):
    return [pl.BlockSpec(memory_space=pltpu.VMEM)] * n


def hbm(n):
    return [pl.BlockSpec(memory_space=pltpu.HBM)] * n


def iota(shape, dim):
    return lax.broadcasted_iota(I32, shape, dim)


def nt(a, b):
    return lax.dot_general(a, b, (((1,), (1,)), ((), ())), preferred_element_type=F32)


def slot_codes(point, count_ref, owners):
    slots = point.shape[1]
    cap = slots // owners
    slot = iota((1, slots), 1)
    owner = slot // cap
    limit = jnp.zeros((1, slots), I32)
    for k in range(owners):
        limit = jnp.where(owner == k, count_ref[0:1, k : k + 1], limit)
    live = (slot - owner * cap) < limit
    row = point // 128
    code = (128 + (point - row * 128)).astype(F32)
    for b in range(6):
        code = code * jnp.where((row >> b) & 1 == 1, F32(2.0 ** (2**b)), F32(1.0))
    return live, jnp.where(live, code, 0.0)


def decode(code):
    row = jnp.zeros(code.shape, F32)
    for b in (5, 4, 3, 2, 1, 0):
        big = code >= F32(128.0 * 2.0 ** (2**b))
        row = row + jnp.where(big, F32(2**b), 0.0)
        code = code * jnp.where(big, F32(2.0 ** -(2**b)), 1.0)
    return row, code - 128.0


def owner_kernel(
    got_ref, disp_ref, stiff_ref, kd_ref, new_ref, r0, r1, r2, r3, row_ref, lane_ref
):
    replies = (r0, r1, r2, r3)
    sources = got_ref.shape[0]
    rows = disp_ref.shape[1]
    patch = lax.axis_index("patch")
    first = lax.axis_index("slab") * 4
    for h in range(2):
        row, lane = decode(got_ref[:, 6 + h, :].astype(F32))
        row_ref[h] = row
        lane_ref[h] = lane
    row_ids = iota((rows, 128), 0).astype(F32).astype(BF)
    lane_ids = iota((128, 128), 0).astype(F32).astype(BF)
    none = jnp.zeros((rows, 128), BF)
    ones, zeros = jnp.ones((128, 128), BF), jnp.zeros((128, 128), BF)
    total = jnp.zeros((3 * rows, 128), F32)
    group = 8
    for base in range(0, sources, group):
        row8 = [row_ref[h, base : base + group, :].astype(BF) for h in range(2)]
        lane8 = [lane_ref[h, base : base + group, :].astype(BF) for h in range(2)]
        for g in range(group):
            vals = got_ref[base + g]
            left, right = [], []
            for h in range(2):
                mask = row_ids == row8[h][g : g + 1]
                left.append(
                    jnp.concatenate(
                        [jnp.where(mask, vals[2 * c + h : 2 * c + h + 1], none) for c in range(3)],
                        axis=0,
                    )
                )
                right.append(jnp.where(lane_ids == lane8[h][g : g + 1], ones, zeros))
            total += nt(jnp.concatenate(left, axis=1), jnp.concatenate(right, axis=1))
    loads = total.reshape(3, rows, 128)
    new = disp_ref[...] + (loads - kd_ref[...]) / (36.0 * stiff_ref[...])[None]
    new_ref[...] = new
    flat = new.reshape(3 * rows, 128)
    high = flat.astype(BF)
    low = (flat - high.astype(F32)).astype(BF)
    row_ids = iota((rows, 128), 0).astype(F32)
    for d in range(4):
        src = first + (patch ^ d)
        for h in range(2):
            row = row_ref[h, pl.ds(src, 1), :]
            lane = lane_ref[h, pl.ds(src, 1), :]
            hot = jnp.where(lane_ids == lane.astype(BF), ones, zeros)
            picked = jnp.dot(high, hot, preferred_element_type=F32)
            picked += jnp.dot(low, hot, preferred_element_type=F32)
            mask = row_ids == row
            for c in range(3):
                part = jnp.where(mask, picked[c * rows : (c + 1) * rows], 0.0)
                replies[d][c : c + 1, h * 128 : (h + 1) * 128] = part.sum(axis=0, keepdims=True)


def store_kernel(value_ref, out_ref, sem):
    copy = pltpu.make_async_copy(value_ref, out_ref, sem)
    copy.start()
    copy.wait()


def store(value, name):
    return pl.pallas_call(
        store_kernel,
        out_shape=jax.ShapeDtypeStruct(value.shape, value.dtype),
        in_specs=vmem(1),
        out_specs=hbm(1)[0],
        scratch_shapes=[pltpu.SemaphoreType.DMA],
        compiler_params=params(),
        name=name,
    )(value)


def finish_kernel(r0, r1, r2, r3, out_ref):
    cap = r0.shape[1]
    patch = lax.axis_index("patch")
    for d, reply in enumerate((r0, r1, r2, r3)):
        start = pl.multiple_of((patch ^ d) * cap, cap)
        for c in range(3):
            out_ref[c, 0, :, pl.ds(start, cap)] = reply[c : c + 1, :]


def shell_kernel(
    one_ref, three_ref, disp_ref, stiff_ref, state_ref, kd_ref, out_ref, field_ref, bend_ref, sem
):
    copy = pltpu.make_async_copy(state_ref, out_ref, sem)
    copy.start()
    rows = disp_ref.shape[1]
    patch = lax.axis_index("patch")
    top = patch > 0
    bottom = patch < 3
    even = patch % 2 == 0
    one, three = (
        ref[:, :128].astype(F32) + ref[:, 128:].astype(F32)
        for ref in (one_ref, three_ref)
    )
    above = jnp.where(even, three, one)
    below = jnp.where(even, one, three)
    field_ref[...] = jnp.zeros_like(field_ref)
    bend_ref[...] = jnp.zeros_like(bend_ref)
    field_ref[:, 8 : 8 + rows, :] = disp_ref[...]
    lane = iota((1, 1, 128), 2)

    def sides(x):
        left = jnp.where(lane == 0, 0.0, pltpu.roll(x, 1, 2))
        right = jnp.where(lane == 127, 0.0, pltpu.roll(x, 127, 2))
        return left + right

    for c in range(3):
        field_ref[c, 6:8, :] = jnp.where(top, above[2 * c : 2 * c + 2], 0.0)
        field_ref[c, 8 + rows : 10 + rows, :] = jnp.where(bottom, below[2 * c : 2 * c + 2], 0.0)
    mid = field_ref[:, 7 : 9 + rows, :]
    bend = 4.0 * mid - (
        field_ref[:, 6 : 8 + rows, :] + field_ref[:, 8 : 10 + rows, :] + sides(mid)
    )
    bend_ref[:, 7 : 9 + rows, :] = bend
    for c in range(3):
        bend_ref[c, 7:8, :] = jnp.where(top, bend_ref[c, 7:8, :], 0.0)
        bend_ref[c, 8 + rows : 9 + rows, :] = jnp.where(
            bottom, bend_ref[c, 8 + rows : 9 + rows, :], 0.0
        )
    mid = bend_ref[:, 8 : 8 + rows, :]
    again = 4.0 * mid - (
        bend_ref[:, 7 : 7 + rows, :] + bend_ref[:, 9 : 9 + rows, :] + sides(mid)
    )
    kd_ref[...] = stiff_ref[...][None] * (again + 4.0 * mid)
    copy.wait()


def params():
    return pltpu.CompilerParams(vmem_limit_bytes=LIMIT)


def patch_pairs(d):
    return [(p, p ^ d) for p in range(4)]


def exchange_and_relax(message, displacement, stiffness, kd):
    slabs, owners = lax.axis_size("slab"), lax.axis_size("patch")
    rows = displacement.shape[1]
    sources = slabs * owners
    got = lax.all_to_all(
        message.reshape(sources, 8, 128), ("slab", "patch"), 0, 0, tiled=True
    )
    reply = jax.ShapeDtypeStruct((8, 256), F32)
    new, *replies = pl.pallas_call(
        owner_kernel,
        out_shape=(jax.ShapeDtypeStruct(displacement.shape, F32),) + (reply,) * 4,
        in_specs=vmem(4),
        out_specs=vmem(5),
        scratch_shapes=[
            pltpu.VMEM((2, sources, 128), F32),
            pltpu.VMEM((2, sources, 128), F32),
        ],
        compiler_params=params(),
        name="owner",
    )(got, displacement, stiffness, kd)
    back = [replies[0]] + [
        lax.ppermute(replies[d], "patch", patch_pairs(d)) for d in (1, 2, 3)
    ]
    wall = pl.pallas_call(
        finish_kernel,
        out_shape=jax.ShapeDtypeStruct((3, 1, 1, owners * 256), F32),
        in_specs=vmem(4),
        out_specs=pl.BlockSpec(memory_space=pltpu.VMEM),
        compiler_params=params(),
        name="finish",
    )(*back)
    return store(new, "store_shell"), wall


def halves(value):
    high = value.astype(BF)
    low = (value - high.astype(F32)).astype(BF)
    return jnp.concatenate([high.astype(F32), low.astype(F32)], axis=1)


def lines_of(scale_ref, pad_ref):
    pad_ref[...] = jnp.zeros_like(pad_ref)
    pad_ref[0:2, 0 : scale_ref.shape[1]] = scale_ref[...]
    return pltpu.roll(pad_ref[...], 8, 1)


def near_kernel(
    state_hbm, rhs_hbm, scale_hbm, disp_hbm, near_ref, own_ref, far_ref, one_ref, three_ref,
    state_ref, rhs_ref, scale_ref, disp_ref, pad_ref, build_ref, sems,
):
    copies = [
        pltpu.make_async_copy(a, b, sems.at[i])
        for i, (a, b) in enumerate(
            (
                (scale_hbm, scale_ref),
                (state_hbm, state_ref),
                (rhs_hbm, rhs_ref),
                (disp_hbm, disp_ref),
            )
        )
    ]
    for copy in copies:
        copy.start()
    odd = lax.axis_index("slab") % 2
    even = lax.axis_index("patch") % 2 == 0
    cols = state_ref.shape[1]
    for copy in copies:
        copy.wait()
    for e in range(2):
        build_ref[e] = jnp.zeros((EDGE + 8, 256), F32)
    for i, row in enumerate((odd, 1 - odd)):
        for part, ref, at, third in (
            (0, state_ref, 2 * i, 8 + i),
            (2, rhs_ref, (4, 10)[i], None),
        ):
            value = ref[row]
            block = part + i
            if block == 3:
                far_ref[...] = value.astype(BF)
            else:
                own_ref[block * cols : (block + 1) * cols, :] = value.astype(BF)
            low, high = value[0:2], value[cols - 2 : cols]
            build_ref[0, at : at + 2, :] = jnp.where(even, high, low)
            build_ref[1, at : at + 2, :] = jnp.where(even, low, high)
            if third is not None:
                low, high = value[2:3], value[cols - 3 : cols - 2]
                build_ref[0, third : third + 1, :] = jnp.where(even, high, low)
                build_ref[1, third : third + 1, :] = jnp.where(even, low, high)
    near_ref[...] = state_ref[1 - odd].astype(BF)
    lines = lines_of(scale_ref, pad_ref)
    flip = odd == 1
    first = jnp.where(flip, lines[1:2], lines[0:1])
    second = jnp.where(flip, lines[0:1], lines[1:2])
    pair = jnp.concatenate([halves(first), halves(second), jnp.zeros((6, 256), F32)], axis=0)
    own_ref[3 * cols :, :] = pair.astype(BF)
    for e in range(2):
        build_ref[e, 6:8, :] = pair[0:2]
    rows = disp_ref.shape[1]
    for c in range(3):
        top = halves(disp_ref[c, 0:2, :])
        bottom = halves(disp_ref[c, rows - 2 : rows, :])
        at = EDGE + 2 * c
        build_ref[0, at : at + 2, :] = jnp.where(even, bottom, top)
        build_ref[1, at : at + 2, :] = jnp.where(even, top, bottom)
    one_ref[...] = build_ref[0].astype(BF)
    three_ref[...] = build_ref[1].astype(BF)


def sweep_kernel(
    state_ref,
    rhs_ref,
    scale_ref,
    near_ref,
    inner_ref,
    outer_ref,
    rest_ref,
    one_ref,
    three_ref,
    relay_ref,
    matrix_ref,
    x_ref,
    y_ref,
    inverse_ref,
    tmap_ref,
    elem_hbm,
    point_hbm,
    count_hbm,
    out_ref,
    message_hbm,
    v_ref,
    r_ref,
    s_ref,
    i_ref,
    line_ref,
    elem_ref,
    point_ref,
    count_ref,
    rows_ref,
    message_ref,
    sems,
):
    copies = [
        pltpu.make_async_copy(a, b, sems.at[i])
        for i, (a, b) in enumerate(
            ((elem_hbm, elem_ref), (point_hbm, point_ref), (count_hbm, count_ref))
        )
    ]
    for copy in copies:
        copy.start()
    slab, patch = lax.axis_index("slab"), lax.axis_index("patch")
    last_slab, last_patch = lax.axis_size("slab") - 1, lax.axis_size("patch") - 1
    odd = slab % 2
    even = patch % 2 == 0
    cols, width = state_ref.shape[1], state_ref.shape[2]
    wide = cols + 16
    inside = (slab > 0) & (slab < last_slab)
    col = iota((wide, width), 0)
    valid = (col >= 8) & (col < 8 + cols)
    valid = valid | ((col < 8) & (patch > 0)) | ((col >= 8 + cols) & (patch < last_patch))
    edge = valid.astype(F32)
    keep = edge * inside.astype(F32)
    v_ref[:, 0:8, :] = jnp.zeros((8, 8, width), F32)
    v_ref[:, 8 + cols :, :] = jnp.zeros((8, 8, width), F32)
    r_ref[:, 0:8, :] = jnp.zeros((6, 8, width), F32)
    r_ref[:, 8 + cols :, :] = jnp.zeros((6, 8, width), F32)
    tail = 3 * cols + 8
    strips = {
        0: (one_ref[0:EDGE], three_ref[0:EDGE]),
        1: (inner_ref[tail : tail + EDGE], inner_ref[tail + EDGE : tail + 2 * EDGE]),
        2: (rest_ref[cols : cols + THIN], rest_ref[cols + THIN : cols + 2 * THIN]),
    }
    sides = {}
    for kind, pair in strips.items():
        one, three = (x.astype(F32) for x in pair)
        sides[kind] = (jnp.where(even, three, one), jnp.where(even, one, three))
    lane = iota((1, 128), 1)
    line_ref[...] = jnp.zeros_like(line_ref)
    line_ref[0:2, 0:cols] = scale_ref[...]
    exact = pltpu.roll(line_ref[...], 8, 1)
    table = ((2, 1), (2, 0), (0, 0), (0, 1), (1, 1), (1, 0))
    for r, (kind, i) in enumerate(table):
        if kind == 0:
            row = odd if i == 0 else 1 - odd
            v_ref[r + 1, 8 : 8 + cols, :] = state_ref[row]
            r_ref[r, 8 : 8 + cols, :] = rhs_ref[row]
            line = jnp.where(row == 1, exact[1:2], exact[0:1])
        else:
            if kind == 1:
                value = near_ref[...] if i == 1 else inner_ref[0:cols]
                rhs = inner_ref[2 * cols + 8 : 3 * cols + 8] if i == 1 else inner_ref[cols : 2 * cols]
                ref, below = inner_ref, 2 * cols
            else:
                value = outer_ref[i * cols : (i + 1) * cols]
                rhs = rest_ref[cols + 2 * THIN :] if i == 1 else outer_ref[2 * cols : 3 * cols]
                ref, below = outer_ref, 3 * cols
            v_ref[r + 1, 8 : 8 + cols, :] = value.astype(F32)
            r_ref[r, 8 : 8 + cols, :] = rhs.astype(F32)
            both = ref[below : below + 8, :].astype(F32)[i : i + 1]
            line = both[:, :128] + both[:, 128:]
        for side, start, far in zip(sides[kind], (6, 8 + cols), (5, 10 + cols)):
            v_ref[r + 1, start : start + 2, :] = side[2 * i : 2 * i + 2]
            if i == 0:
                r_ref[r, start : start + 2, :] = side[4:6]
            elif kind < 2:
                r_ref[r, start : start + 2, :] = side[10:12]
            if kind == 0:
                v_ref[r + 1, far : far + 1, :] = side[8 + i : 9 + i]
            both = side[6 + i : 7 + i]
            far = pltpu.roll(both[:, :128] + both[:, 128:], 64, 1)
            here = (lane >= start) & (lane < start + 2)
            line = jnp.where(here, far, line)
        line_ref[r : r + 1, :] = jnp.where(line > 0.0, line, 1.0)
    line_ref[6:8, :] = jnp.ones((2, 128), F32)
    v_ref[0, 8 : 8 + cols, :] = rest_ref[0:cols, :].astype(F32)
    beyond = (slab != 1) & (slab != last_slab - 1)
    v_ref[7, 8 : 8 + cols, :] = relay_ref[...].astype(F32) * beyond.astype(F32)
    for r in range(8):
        v_ref[r] = v_ref[r] * (keep if r < 3 else edge)
    lines = line_ref[...]
    columns = jnp.transpose(lines)
    inverses = jnp.transpose(1.0 / lines)
    for r in range(6):
        s_ref[r] = jnp.broadcast_to(columns[:wide, r : r + 1], (wide, width))
        i_ref[r] = jnp.broadcast_to(inverses[:wide, r : r + 1], (wide, width))
    for sweep in range(SWEEPS):
        a, b = 1 + sweep, 7 - sweep
        value = relaxed(
            v_ref[a:b],
            v_ref[a - 1 : b - 1],
            v_ref[a + 1 : b + 1],
            r_ref[a - 1 : b - 1],
            s_ref[a - 1 : b - 1],
            i_ref[a - 1 : b - 1],
            (matrix_ref, x_ref, y_ref, inverse_ref),
        )
        for j in range(b - a):
            v_ref[a + j] = value[j] * (keep if a + j < 3 else edge)
    out_ref[odd] = v_ref[3, 8 : 8 + cols, :]
    out_ref[1 - odd] = v_ref[4, 8 : 8 + cols, :]
    final = out_ref[...].astype(BF).reshape(2 * cols, width)
    for copy in copies:
        copy.wait()
    elem = elem_ref[0]
    owners = rows_ref.shape[0]
    live, code = slot_codes(point_ref[0], count_ref.at[0], owners)
    hot = ((iota((2 * cols, elem.shape[1]), 0) == elem) & live).astype(F32).astype(BF)
    pull = jnp.dot(nt(tmap_ref[...], final).astype(BF), hot, preferred_element_type=F32)
    for k in range(owners):
        for j in range(4):
            source = code if j == 3 else pull[j : j + 1]
            for h in range(2):
                start = k * 256 + h * 128
                rows_ref[k, 2 * j + h : 2 * j + h + 1, :] = source[:, start : start + 128]
    message_ref[...] = jnp.broadcast_to(rows_ref[...].astype(BF)[None], message_ref.shape)
    part = message_ref.shape[0]
    copies = [
        pltpu.make_async_copy(message_ref, message_hbm.at[i * part : (i + 1) * part], sems.at[3 + i])
        for i in range(message_hbm.shape[0] // part)
    ]
    for copy in copies:
        copy.start()
    for copy in copies:
        copy.wait()


def relaxed(center, up, down, rhs, scale, inverse_scale, matrices):
    matrix_ref, x_ref, y_ref, inverse_ref = matrices
    n, wide, width = center.shape
    flat = (n * wide, width)
    up, mid, down = (x.astype(BF).astype(F32) for x in (up, center, down))
    nx = (up + down).astype(BF)
    ny = (pltpu.roll(mid, 1, 1) + pltpu.roll(mid, wide - 1, 1)).astype(BF)
    own = jnp.dot(mid.astype(BF).reshape(flat), matrix_ref[...], preferred_element_type=F32)
    side = jnp.dot(nx.reshape(flat), x_ref[...], preferred_element_type=F32)
    side += jnp.dot(ny.reshape(flat), y_ref[...], preferred_element_type=F32)
    residue = (rhs.reshape(flat) - (scale.reshape(flat) * own - side)).astype(BF)
    update = jnp.dot(residue, inverse_ref[...], preferred_element_type=F32)
    update = update * inverse_scale.reshape(flat)
    return center + update.reshape(center.shape)


def call(kernel, name, out_shape, operands, scratch=(), in_specs=None, out_specs=None):
    return pl.pallas_call(
        kernel,
        out_shape=out_shape,
        in_specs=in_specs or vmem(len(operands)),
        out_specs=out_specs or jax.tree.map(lambda _: vmem(1)[0], out_shape),
        scratch_shapes=list(scratch),
        compiler_params=params(),
        name=name,
    )(*operands)


def shards(
    fluid_state,
    fluid_rhs,
    element_scale,
    element_matrix,
    couple_x,
    couple_y,
    block_inverse,
    traction_map,
    slot_elem,
    slot_point,
    slot_count,
    displacement,
    stiffness,
):
    cols, width = fluid_state.shape[1:]
    slots = slot_elem.shape[2]
    slabs, owners = lax.axis_size("slab"), lax.axis_size("patch")
    shape = jax.ShapeDtypeStruct
    inner_pairs = [(s, s ^ 1) for s in range(slabs)]
    outer_pairs = [(s, (s + 1) % slabs) for s in range(1, slabs, 2)]
    outer_pairs = outer_pairs + [(b, a) for a, b in outer_pairs]
    strip = shape((EDGE + 8, width), BF)
    row = shape((cols, width), BF)
    near, own, far, to_one, to_three = call(
        near_kernel,
        "near",
        (row, shape((3 * cols + 8, width), BF), row, strip, strip),
        tuple(
            pltpu.with_memory_space_constraint(x, pltpu.HBM)
            for x in (fluid_state, fluid_rhs, element_scale, displacement)
        ),
        [
            pltpu.VMEM(fluid_state.shape, F32),
            pltpu.VMEM(fluid_rhs.shape, F32),
            pltpu.VMEM(element_scale.shape, F32),
            pltpu.VMEM(displacement.shape, F32),
            pltpu.VMEM((8, 128), F32),
            pltpu.VMEM((2, EDGE + 8, width), F32),
            pltpu.SemaphoreType.DMA((4,)),
        ],
        in_specs=hbm(4),
    )
    outer = lax.ppermute(own, "slab", outer_pairs)
    inner_near = lax.ppermute(near, "slab", inner_pairs)
    from_three = lax.ppermute(to_three, "patch", patch_pairs(3))
    from_one = lax.ppermute(to_one, "patch", patch_pairs(1))
    strips = [from_one[:EDGE], from_three[:EDGE]]
    thin = [from_one[:THIN], from_three[:THIN]]
    rest = lax.ppermute(jnp.concatenate([inner_near] + thin + [far]), "slab", outer_pairs)
    others = jnp.concatenate([own[:cols], own[2 * cols :], far] + strips)
    others, _ = lax.optimization_barrier((others, inner_near))
    inner = lax.ppermute(others, "slab", inner_pairs)
    relay = lax.ppermute(outer[:cols], "slab", inner_pairs)
    wide = cols + 16
    state, message = call(
        sweep_kernel,
        "sweep",
        (shape(fluid_state.shape, F32), shape((slabs, owners, 8, 128), BF)),
        (
            fluid_state,
            fluid_rhs,
            element_scale,
            inner_near,
            inner,
            outer,
            rest,
            from_one,
            from_three,
            relay,
            element_matrix,
            couple_x,
            couple_y,
            block_inverse,
            traction_map,
            slot_elem,
            slot_point,
            slot_count,
        ),
        [
            pltpu.VMEM((8, wide, width), F32),
            pltpu.VMEM((6, wide, width), F32),
            pltpu.VMEM((6, wide, width), F32),
            pltpu.VMEM((6, wide, width), F32),
            pltpu.VMEM((8, 128), F32),
            pltpu.VMEM((1, 1, slots), I32),
            pltpu.VMEM((1, 1, slots), I32),
            pltpu.VMEM((1, 1, owners), I32),
            pltpu.VMEM((owners, 8, 128), F32),
            pltpu.VMEM((slabs // 4, owners, 8, 128), BF),
            pltpu.SemaphoreType.DMA((7,)),
        ],
        in_specs=vmem(15) + hbm(3),
        out_specs=tuple(vmem(1) + hbm(1)),
    )
    kd, final = call(
        shell_kernel,
        "shell",
        (shape(displacement.shape, F32), shape(state.shape, F32)),
        (from_one[EDGE:], from_three[EDGE:], displacement, stiffness, state),
        [pltpu.VMEM((3, displacement.shape[1] + 16, 128), F32)] * 2 + [pltpu.SemaphoreType.DMA],
        out_specs=tuple(vmem(1) + hbm(1)),
    )
    new, wall = exchange_and_relax(message, displacement, stiffness, kd)
    return final, new, wall


def solution(mesh):
    return jax.shard_map(
        shards,
        mesh=mesh,
        in_specs=(
            P("slab", "patch", None),
            P("slab", "patch", None),
            P("slab", "patch"),
            P(),
            P(),
            P(),
            P(),
            P(),
            P("slab", "patch", None),
            P("slab", "patch", None),
            P("slab", "patch", None),
            P(None, "patch", None),
            P("patch", None),
        ),
        out_specs=(
            P("slab", "patch", None),
            P(None, "patch", None),
            P(None, "slab", "patch", None),
        ),
        check_vma=False,
    )
```

```python
import jax
import jax.numpy as jnp
from jax import lax
from jax.experimental import pallas as pl
from jax.experimental.pallas import tpu as pltpu
from jax.sharding import PartitionSpec as P

SWEEPS = 3
BF = jnp.bfloat16
F32 = jnp.float32
I32 = jnp.int32
LIMIT = 48 << 20
EDGE = 16
THIN = 8


def vmem(n):
    return [pl.BlockSpec(memory_space=pltpu.VMEM)] * n


def hbm(n):
    return [pl.BlockSpec(memory_space=pltpu.HBM)] * n


def iota(shape, dim):
    return lax.broadcasted_iota(I32, shape, dim)


def nt(a, b):
    return lax.dot_general(a, b, (((1,), (1,)), ((), ())), preferred_element_type=F32)


def slot_codes(point, count_ref, owners):
    slots = point.shape[1]
    cap = slots // owners
    slot = iota((1, slots), 1)
    owner = slot // cap
    limit = jnp.zeros((1, slots), I32)
    for k in range(owners):
        limit = jnp.where(owner == k, count_ref[0:1, k : k + 1], limit)
    live = (slot - owner * cap) < limit
    row = point // 128
    code = (128 + (point - row * 128)).astype(F32)
    for b in range(6):
        code = code * jnp.where((row >> b) & 1 == 1, F32(2.0 ** (2**b)), F32(1.0))
    return live, jnp.where(live, code, 0.0)


def decode(code):
    row = jnp.zeros(code.shape, F32)
    for b in (5, 4, 3, 2, 1, 0):
        big = code >= F32(128.0 * 2.0 ** (2**b))
        row = row + jnp.where(big, F32(2**b), 0.0)
        code = code * jnp.where(big, F32(2.0 ** -(2**b)), 1.0)
    return row, code - 128.0


def owner_kernel(got_ref, disp_ref, stiff_ref, kd_ref, new_ref, r0, r1, r2, r3, pick_ref):
    sources = got_ref.shape[0]
    rows = disp_ref.shape[1]
    patch = lax.axis_index("patch")
    first = lax.axis_index("slab") * 4
    row_ids = iota((rows, 128), 0).astype(F32).astype(BF)
    lane_ids = iota((128, 128), 0).astype(F32).astype(BF)
    none = jnp.zeros((rows, 128), BF)
    ones, zeros = jnp.ones((128, 128), BF), jnp.zeros((128, 128), BF)
    total = jnp.zeros((3 * rows, 128), F32)
    group = 8
    for base in range(0, sources, group):
        codes = [decode(got_ref[base : base + group, 6 + h, :].astype(F32)) for h in range(2)]
        row8 = [row.astype(BF) for row, _ in codes]
        lane8 = [lane.astype(BF) for _, lane in codes]
        for g in range(group):
            vals = got_ref[base + g]
            left, right = [], []
            for h in range(2):
                mask = row_ids == row8[h][g : g + 1]
                left.append(
                    jnp.concatenate(
                        [jnp.where(mask, vals[2 * c + h : 2 * c + h + 1], none) for c in range(3)],
                        axis=0,
                    )
                )
                right.append(jnp.where(lane_ids == lane8[h][g : g + 1], ones, zeros))
            total += nt(jnp.concatenate(left, axis=1), jnp.concatenate(right, axis=1))
    loads = total.reshape(3, rows, 128)
    new = disp_ref[...] + (loads - kd_ref[...]) / (36.0 * stiff_ref[...])[None]
    new_ref[...] = new
    flat = new.reshape(3 * rows, 128)
    high = flat.astype(BF)
    low = (flat - high.astype(F32)).astype(BF)
    both = jnp.concatenate([high, low], axis=0)
    for d in range(4):
        for h in range(2):
            code = got_ref[pl.ds(first + (patch ^ d), 1), 6 + h, :]
            pick_ref[2 * d + h : 2 * d + h + 1, :] = code.astype(F32)
    row, lane = decode(pick_ref[...])
    wide_ids = iota((rows, 256), 0).astype(F32)
    for d, reply in enumerate((r0, r1, r2, r3)):
        at = 2 * d
        hot = jnp.concatenate(
            [
                jnp.where(lane_ids == lane[at + h : at + h + 1].astype(BF), ones, zeros)
                for h in range(2)
            ],
            axis=1,
        )
        picked = jnp.dot(both, hot, preferred_element_type=F32)
        mask = wide_ids == jnp.concatenate([row[at : at + 1], row[at + 1 : at + 2]], axis=1)
        for c in range(3):
            part = picked[c * rows : (c + 1) * rows] + picked[(c + 3) * rows : (c + 4) * rows]
            reply[c : c + 1, :] = jnp.where(mask, part, 0.0).sum(axis=0, keepdims=True)


def store_kernel(value_ref, out_ref, sem):
    copy = pltpu.make_async_copy(value_ref, out_ref, sem)
    copy.start()
    copy.wait()


def store(value, name):
    return pl.pallas_call(
        store_kernel,
        out_shape=jax.ShapeDtypeStruct(value.shape, value.dtype),
        in_specs=vmem(1),
        out_specs=hbm(1)[0],
        scratch_shapes=[pltpu.SemaphoreType.DMA],
        compiler_params=params(),
        name=name,
    )(value)


def finish_kernel(r0, r1, r2, r3, out_ref):
    cap = r0.shape[1]
    patch = lax.axis_index("patch")
    for d, reply in enumerate((r0, r1, r2, r3)):
        start = pl.multiple_of((patch ^ d) * cap, cap)
        for c in range(3):
            out_ref[c, 0, :, pl.ds(start, cap)] = reply[c : c + 1, :]


def shell_kernel(
    one_ref, three_ref, disp_ref, stiff_ref, state_ref, kd_ref, out_ref, field_ref, bend_ref, sem
):
    copy = pltpu.make_async_copy(state_ref, out_ref, sem)
    copy.start()
    rows = disp_ref.shape[1]
    patch = lax.axis_index("patch")
    top = patch > 0
    bottom = patch < 3
    even = patch % 2 == 0
    one, three = (
        ref[:, :128].astype(F32) + ref[:, 128:].astype(F32)
        for ref in (one_ref, three_ref)
    )
    above = jnp.where(even, three, one)
    below = jnp.where(even, one, three)
    field_ref[...] = jnp.zeros_like(field_ref)
    bend_ref[...] = jnp.zeros_like(bend_ref)
    field_ref[:, 8 : 8 + rows, :] = disp_ref[...]
    lane = iota((1, 1, 128), 2)

    def sides(x):
        left = jnp.where(lane == 0, 0.0, pltpu.roll(x, 1, 2))
        right = jnp.where(lane == 127, 0.0, pltpu.roll(x, 127, 2))
        return left + right

    for c in range(3):
        field_ref[c, 6:8, :] = jnp.where(top, above[2 * c : 2 * c + 2], 0.0)
        field_ref[c, 8 + rows : 10 + rows, :] = jnp.where(bottom, below[2 * c : 2 * c + 2], 0.0)
    mid = field_ref[:, 7 : 9 + rows, :]
    bend = 4.0 * mid - (
        field_ref[:, 6 : 8 + rows, :] + field_ref[:, 8 : 10 + rows, :] + sides(mid)
    )
    bend_ref[:, 7 : 9 + rows, :] = bend
    for c in range(3):
        bend_ref[c, 7:8, :] = jnp.where(top, bend_ref[c, 7:8, :], 0.0)
        bend_ref[c, 8 + rows : 9 + rows, :] = jnp.where(
            bottom, bend_ref[c, 8 + rows : 9 + rows, :], 0.0
        )
    mid = bend_ref[:, 8 : 8 + rows, :]
    again = 4.0 * mid - (
        bend_ref[:, 7 : 7 + rows, :] + bend_ref[:, 9 : 9 + rows, :] + sides(mid)
    )
    kd_ref[...] = stiff_ref[...][None] * (again + 4.0 * mid)
    copy.wait()


def params():
    return pltpu.CompilerParams(vmem_limit_bytes=LIMIT)


def patch_pairs(d):
    return [(p, p ^ d) for p in range(4)]


def exchange_and_relax(message, displacement, stiffness, kd):
    slabs, owners = lax.axis_size("slab"), lax.axis_size("patch")
    rows = displacement.shape[1]
    sources = slabs * owners
    got = lax.all_to_all(
        message.reshape(sources, 8, 128), ("slab", "patch"), 0, 0, tiled=True
    )
    reply = jax.ShapeDtypeStruct((8, 256), F32)
    new, *replies = pl.pallas_call(
        owner_kernel,
        out_shape=(jax.ShapeDtypeStruct(displacement.shape, F32),) + (reply,) * 4,
        in_specs=vmem(4),
        out_specs=vmem(5),
        scratch_shapes=[pltpu.VMEM((8, 128), F32)],
        compiler_params=params(),
        name="owner",
    )(got, displacement, stiffness, kd)
    back = [replies[0]] + [
        lax.ppermute(replies[d], "patch", patch_pairs(d)) for d in (1, 2, 3)
    ]
    wall = pl.pallas_call(
        finish_kernel,
        out_shape=jax.ShapeDtypeStruct((3, 1, 1, owners * 256), F32),
        in_specs=vmem(4),
        out_specs=pl.BlockSpec(memory_space=pltpu.VMEM),
        compiler_params=params(),
        name="finish",
    )(*back)
    return store(new, "store_shell"), wall


def halves(value):
    high = value.astype(BF)
    low = (value - high.astype(F32)).astype(BF)
    return jnp.concatenate([high.astype(F32), low.astype(F32)], axis=1)


def lines_of(scale_ref, pad_ref):
    pad_ref[...] = jnp.zeros_like(pad_ref)
    pad_ref[0:2, 0 : scale_ref.shape[1]] = scale_ref[...]
    return pltpu.roll(pad_ref[...], 8, 1)


def near_kernel(
    state_hbm, rhs_hbm, scale_hbm, disp_hbm, near_ref, own_ref, far_ref, one_ref, three_ref,
    state_ref, rhs_ref, scale_ref, disp_ref, pad_ref, build_ref, sems,
):
    copies = [
        pltpu.make_async_copy(a, b, sems.at[i])
        for i, (a, b) in enumerate(
            (
                (scale_hbm, scale_ref),
                (state_hbm, state_ref),
                (rhs_hbm, rhs_ref),
                (disp_hbm, disp_ref),
            )
        )
    ]
    for copy in copies:
        copy.start()
    odd = lax.axis_index("slab") % 2
    even = lax.axis_index("patch") % 2 == 0
    cols = state_ref.shape[1]
    for copy in copies:
        copy.wait()
    for e in range(2):
        build_ref[e] = jnp.zeros((EDGE + 8, 256), F32)
    for i, row in enumerate((odd, 1 - odd)):
        for part, ref, at, third in (
            (0, state_ref, 2 * i, 8 + i),
            (2, rhs_ref, (4, 10)[i], None),
        ):
            value = ref[row]
            block = part + i
            if block == 3:
                far_ref[...] = value.astype(BF)
            else:
                own_ref[block * cols : (block + 1) * cols, :] = value.astype(BF)
            low, high = value[0:2], value[cols - 2 : cols]
            build_ref[0, at : at + 2, :] = jnp.where(even, high, low)
            build_ref[1, at : at + 2, :] = jnp.where(even, low, high)
            if third is not None:
                low, high = value[2:3], value[cols - 3 : cols - 2]
                build_ref[0, third : third + 1, :] = jnp.where(even, high, low)
                build_ref[1, third : third + 1, :] = jnp.where(even, low, high)
    near_ref[...] = state_ref[1 - odd].astype(BF)
    lines = lines_of(scale_ref, pad_ref)
    flip = odd == 1
    first = jnp.where(flip, lines[1:2], lines[0:1])
    second = jnp.where(flip, lines[0:1], lines[1:2])
    pair = jnp.concatenate([halves(first), halves(second), jnp.zeros((6, 256), F32)], axis=0)
    own_ref[3 * cols :, :] = pair.astype(BF)
    for e in range(2):
        build_ref[e, 6:8, :] = pair[0:2]
    rows = disp_ref.shape[1]
    for c in range(3):
        top = halves(disp_ref[c, 0:2, :])
        bottom = halves(disp_ref[c, rows - 2 : rows, :])
        at = EDGE + 2 * c
        build_ref[0, at : at + 2, :] = jnp.where(even, bottom, top)
        build_ref[1, at : at + 2, :] = jnp.where(even, top, bottom)
    one_ref[...] = build_ref[0].astype(BF)
    three_ref[...] = build_ref[1].astype(BF)


def sweep_kernel(
    state_ref,
    rhs_ref,
    scale_ref,
    near_ref,
    inner_ref,
    outer_ref,
    rest_ref,
    one_ref,
    three_ref,
    relay_ref,
    matrix_ref,
    x_ref,
    y_ref,
    inverse_ref,
    tmap_ref,
    elem_hbm,
    point_hbm,
    count_hbm,
    out_ref,
    message_hbm,
    v_ref,
    r_ref,
    s_ref,
    i_ref,
    line_ref,
    elem_ref,
    point_ref,
    count_ref,
    rows_ref,
    message_ref,
    sems,
):
    copies = [
        pltpu.make_async_copy(a, b, sems.at[i])
        for i, (a, b) in enumerate(
            ((elem_hbm, elem_ref), (point_hbm, point_ref), (count_hbm, count_ref))
        )
    ]
    for copy in copies:
        copy.start()
    slab, patch = lax.axis_index("slab"), lax.axis_index("patch")
    last_slab, last_patch = lax.axis_size("slab") - 1, lax.axis_size("patch") - 1
    odd = slab % 2
    even = patch % 2 == 0
    cols, width = state_ref.shape[1], state_ref.shape[2]
    wide = cols + 16
    inside = (slab > 0) & (slab < last_slab)
    col = iota((wide, width), 0)
    valid = (col >= 8) & (col < 8 + cols)
    valid = valid | ((col < 8) & (patch > 0)) | ((col >= 8 + cols) & (patch < last_patch))
    edge = valid.astype(F32)
    keep = edge * inside.astype(F32)
    v_ref[:, 0:8, :] = jnp.zeros((8, 8, width), F32)
    v_ref[:, 8 + cols :, :] = jnp.zeros((8, 8, width), F32)
    r_ref[:, 0:8, :] = jnp.zeros((6, 8, width), F32)
    r_ref[:, 8 + cols :, :] = jnp.zeros((6, 8, width), F32)
    tail = 3 * cols + 8
    strips = {
        0: (one_ref[0:EDGE], three_ref[0:EDGE]),
        1: (inner_ref[tail : tail + EDGE], inner_ref[tail + EDGE : tail + 2 * EDGE]),
        2: (rest_ref[cols : cols + THIN], rest_ref[cols + THIN : cols + 2 * THIN]),
    }
    sides = {}
    for kind, pair in strips.items():
        one, three = (x.astype(F32) for x in pair)
        sides[kind] = (jnp.where(even, three, one), jnp.where(even, one, three))
    lane = iota((1, 128), 1)
    line_ref[...] = jnp.zeros_like(line_ref)
    line_ref[0:2, 0:cols] = scale_ref[...]
    exact = pltpu.roll(line_ref[...], 8, 1)
    table = ((2, 1), (2, 0), (0, 0), (0, 1), (1, 1), (1, 0))
    for r, (kind, i) in enumerate(table):
        if kind == 0:
            row = odd if i == 0 else 1 - odd
            v_ref[r + 1, 8 : 8 + cols, :] = state_ref[row]
            r_ref[r, 8 : 8 + cols, :] = rhs_ref[row]
            line = jnp.where(row == 1, exact[1:2], exact[0:1])
        else:
            if kind == 1:
                value = near_ref[...] if i == 1 else inner_ref[0:cols]
                rhs = inner_ref[2 * cols + 8 : 3 * cols + 8] if i == 1 else inner_ref[cols : 2 * cols]
                ref, below = inner_ref, 2 * cols
            else:
                value = outer_ref[i * cols : (i + 1) * cols]
                rhs = rest_ref[cols + 2 * THIN :] if i == 1 else outer_ref[2 * cols : 3 * cols]
                ref, below = outer_ref, 3 * cols
            v_ref[r + 1, 8 : 8 + cols, :] = value.astype(F32)
            r_ref[r, 8 : 8 + cols, :] = rhs.astype(F32)
            both = ref[below : below + 8, :].astype(F32)[i : i + 1]
            line = both[:, :128] + both[:, 128:]
        for side, start, far in zip(sides[kind], (6, 8 + cols), (5, 10 + cols)):
            v_ref[r + 1, start : start + 2, :] = side[2 * i : 2 * i + 2]
            if i == 0:
                r_ref[r, start : start + 2, :] = side[4:6]
            elif kind < 2:
                r_ref[r, start : start + 2, :] = side[10:12]
            if kind == 0:
                v_ref[r + 1, far : far + 1, :] = side[8 + i : 9 + i]
            both = side[6 + i : 7 + i]
            far = pltpu.roll(both[:, :128] + both[:, 128:], 64, 1)
            here = (lane >= start) & (lane < start + 2)
            line = jnp.where(here, far, line)
        line_ref[r : r + 1, :] = jnp.where(line > 0.0, line, 1.0)
    line_ref[6:8, :] = jnp.ones((2, 128), F32)
    v_ref[0, 8 : 8 + cols, :] = rest_ref[0:cols, :].astype(F32)
    beyond = (slab != 1) & (slab != last_slab - 1)
    v_ref[7, 8 : 8 + cols, :] = relay_ref[...].astype(F32) * beyond.astype(F32)
    for r in range(8):
        v_ref[r] = v_ref[r] * (keep if r < 3 else edge)
    lines = line_ref[...]
    columns = jnp.transpose(lines)
    inverses = jnp.transpose(1.0 / lines)
    for r in range(6):
        s_ref[r] = jnp.broadcast_to(columns[:wide, r : r + 1], (wide, width))
        i_ref[r] = jnp.broadcast_to(inverses[:wide, r : r + 1], (wide, width))
    for sweep in range(SWEEPS):
        a, b = 1 + sweep, 7 - sweep
        value = relaxed(
            v_ref[a:b],
            v_ref[a - 1 : b - 1],
            v_ref[a + 1 : b + 1],
            r_ref[a - 1 : b - 1],
            s_ref[a - 1 : b - 1],
            i_ref[a - 1 : b - 1],
            (matrix_ref, x_ref, y_ref, inverse_ref),
        )
        for j in range(b - a):
            v_ref[a + j] = value[j] * (keep if a + j < 3 else edge)
    out_ref[odd] = v_ref[3, 8 : 8 + cols, :]
    out_ref[1 - odd] = v_ref[4, 8 : 8 + cols, :]
    final = out_ref[...].astype(BF).reshape(2 * cols, width)
    for copy in copies:
        copy.wait()
    elem = elem_ref[0]
    owners = rows_ref.shape[0]
    live, code = slot_codes(point_ref[0], count_ref.at[0], owners)
    hot = ((iota((2 * cols, elem.shape[1]), 0) == elem) & live).astype(F32).astype(BF)
    pull = jnp.dot(nt(tmap_ref[...], final).astype(BF), hot, preferred_element_type=F32)
    for k in range(owners):
        for j in range(4):
            source = code if j == 3 else pull[j : j + 1]
            for h in range(2):
                start = k * 256 + h * 128
                rows_ref[k, 2 * j + h : 2 * j + h + 1, :] = source[:, start : start + 128]
    message_ref[...] = jnp.broadcast_to(rows_ref[...].astype(BF)[None], message_ref.shape)
    part = message_ref.shape[0]
    copies = [
        pltpu.make_async_copy(message_ref, message_hbm.at[i * part : (i + 1) * part], sems.at[3 + i])
        for i in range(message_hbm.shape[0] // part)
    ]
    for copy in copies:
        copy.start()
    for copy in copies:
        copy.wait()


def relaxed(center, up, down, rhs, scale, inverse_scale, matrices):
    matrix_ref, x_ref, y_ref, inverse_ref = matrices
    n, wide, width = center.shape
    flat = (n * wide, width)
    up, mid, down = (x.astype(BF).astype(F32) for x in (up, center, down))
    nx = (up + down).astype(BF)
    ny = (pltpu.roll(mid, 1, 1) + pltpu.roll(mid, wide - 1, 1)).astype(BF)
    own = jnp.dot(mid.astype(BF).reshape(flat), matrix_ref[...], preferred_element_type=F32)
    side = jnp.dot(nx.reshape(flat), x_ref[...], preferred_element_type=F32)
    side += jnp.dot(ny.reshape(flat), y_ref[...], preferred_element_type=F32)
    residue = (rhs.reshape(flat) - (scale.reshape(flat) * own - side)).astype(BF)
    update = jnp.dot(residue, inverse_ref[...], preferred_element_type=F32)
    update = update * inverse_scale.reshape(flat)
    return center + update.reshape(center.shape)


def call(kernel, name, out_shape, operands, scratch=(), in_specs=None, out_specs=None):
    return pl.pallas_call(
        kernel,
        out_shape=out_shape,
        in_specs=in_specs or vmem(len(operands)),
        out_specs=out_specs or jax.tree.map(lambda _: vmem(1)[0], out_shape),
        scratch_shapes=list(scratch),
        compiler_params=params(),
        name=name,
    )(*operands)


def shards(
    fluid_state,
    fluid_rhs,
    element_scale,
    element_matrix,
    couple_x,
    couple_y,
    block_inverse,
    traction_map,
    slot_elem,
    slot_point,
    slot_count,
    displacement,
    stiffness,
):
    cols, width = fluid_state.shape[1:]
    slots = slot_elem.shape[2]
    slabs, owners = lax.axis_size("slab"), lax.axis_size("patch")
    shape = jax.ShapeDtypeStruct
    inner_pairs = [(s, s ^ 1) for s in range(slabs)]
    outer_pairs = [(s, (s + 1) % slabs) for s in range(1, slabs, 2)]
    outer_pairs = outer_pairs + [(b, a) for a, b in outer_pairs]
    strip = shape((EDGE + 8, width), BF)
    row = shape((cols, width), BF)
    near, own, far, to_one, to_three = call(
        near_kernel,
        "near",
        (row, shape((3 * cols + 8, width), BF), row, strip, strip),
        tuple(
            pltpu.with_memory_space_constraint(x, pltpu.HBM)
            for x in (fluid_state, fluid_rhs, element_scale, displacement)
        ),
        [
            pltpu.VMEM(fluid_state.shape, F32),
            pltpu.VMEM(fluid_rhs.shape, F32),
            pltpu.VMEM(element_scale.shape, F32),
            pltpu.VMEM(displacement.shape, F32),
            pltpu.VMEM((8, 128), F32),
            pltpu.VMEM((2, EDGE + 8, width), F32),
            pltpu.SemaphoreType.DMA((4,)),
        ],
        in_specs=hbm(4),
    )
    outer = lax.ppermute(own, "slab", outer_pairs)
    inner_near = lax.ppermute(near, "slab", inner_pairs)
    from_three = lax.ppermute(to_three, "patch", patch_pairs(3))
    from_one = lax.ppermute(to_one, "patch", patch_pairs(1))
    strips = [from_one[:EDGE], from_three[:EDGE]]
    thin = [from_one[:THIN], from_three[:THIN]]
    rest = lax.ppermute(jnp.concatenate([inner_near] + thin + [far]), "slab", outer_pairs)
    others = jnp.concatenate([own[:cols], own[2 * cols :], far] + strips)
    others, _ = lax.optimization_barrier((others, inner_near))
    inner = lax.ppermute(others, "slab", inner_pairs)
    relay = lax.ppermute(outer[:cols], "slab", inner_pairs)
    wide = cols + 16
    state, message = call(
        sweep_kernel,
        "sweep",
        (shape(fluid_state.shape, F32), shape((slabs, owners, 8, 128), BF)),
        (
            fluid_state,
            fluid_rhs,
            element_scale,
            inner_near,
            inner,
            outer,
            rest,
            from_one,
            from_three,
            relay,
            element_matrix,
            couple_x,
            couple_y,
            block_inverse,
            traction_map,
            slot_elem,
            slot_point,
            slot_count,
        ),
        [
            pltpu.VMEM((8, wide, width), F32),
            pltpu.VMEM((6, wide, width), F32),
            pltpu.VMEM((6, wide, width), F32),
            pltpu.VMEM((6, wide, width), F32),
            pltpu.VMEM((8, 128), F32),
            pltpu.VMEM((1, 1, slots), I32),
            pltpu.VMEM((1, 1, slots), I32),
            pltpu.VMEM((1, 1, owners), I32),
            pltpu.VMEM((owners, 8, 128), F32),
            pltpu.VMEM((slabs // 4, owners, 8, 128), BF),
            pltpu.SemaphoreType.DMA((7,)),
        ],
        in_specs=vmem(15) + hbm(3),
        out_specs=tuple(vmem(1) + hbm(1)),
    )
    kd, final = call(
        shell_kernel,
        "shell",
        (shape(displacement.shape, F32), shape(state.shape, F32)),
        (from_one[EDGE:], from_three[EDGE:], displacement, stiffness, state),
        [pltpu.VMEM((3, displacement.shape[1] + 16, 128), F32)] * 2 + [pltpu.SemaphoreType.DMA],
        out_specs=tuple(vmem(1) + hbm(1)),
    )
    new, wall = exchange_and_relax(message, displacement, stiffness, kd)
    return final, new, wall


def solution(mesh):
    return jax.shard_map(
        shards,
        mesh=mesh,
        in_specs=(
            P("slab", "patch", None),
            P("slab", "patch", None),
            P("slab", "patch"),
            P(),
            P(),
            P(),
            P(),
            P(),
            P("slab", "patch", None),
            P("slab", "patch", None),
            P("slab", "patch", None),
            P(None, "patch", None),
            P("patch", None),
        ),
        out_specs=(
            P("slab", "patch", None),
            P(None, "patch", None),
            P(None, "slab", "patch", None),
        ),
        check_vma=False,
    )
```

```python
import jax
import jax.numpy as jnp
from jax import lax
from jax.experimental import pallas as pl
from jax.experimental.pallas import tpu as pltpu
from jax.sharding import PartitionSpec as P

SWEEPS = 3
BF = jnp.bfloat16
F32 = jnp.float32
I32 = jnp.int32
LIMIT = 48 << 20
EDGE = 16
THIN = 8


def vmem(n):
    return [pl.BlockSpec(memory_space=pltpu.VMEM)] * n


def hbm(n):
    return [pl.BlockSpec(memory_space=pltpu.HBM)] * n


def iota(shape, dim):
    return lax.broadcasted_iota(I32, shape, dim)


def nt(a, b):
    return lax.dot_general(a, b, (((1,), (1,)), ((), ())), preferred_element_type=F32)


def slot_codes(point, count_ref, owners):
    slots = point.shape[1]
    cap = slots // owners
    slot = iota((1, slots), 1)
    owner = slot // cap
    limit = jnp.zeros((1, slots), I32)
    for k in range(owners):
        limit = jnp.where(owner == k, count_ref[0:1, k : k + 1], limit)
    live = (slot - owner * cap) < limit
    row = point // 128
    code = (128 + (point - row * 128)).astype(F32)
    for b in range(6):
        code = code * jnp.where((row >> b) & 1 == 1, F32(2.0 ** (2**b)), F32(1.0))
    return live, jnp.where(live, code, 0.0)


def decode(code):
    row = jnp.zeros(code.shape, F32)
    for b in (5, 4, 3, 2, 1, 0):
        big = code >= F32(128.0 * 2.0 ** (2**b))
        row = row + jnp.where(big, F32(2**b), 0.0)
        code = code * jnp.where(big, F32(2.0 ** -(2**b)), 1.0)
    return row, code - 128.0


def owner_kernel(got_ref, disp_ref, stiff_ref, kd_ref, new_ref, r0, r1, r2, r3, pick_ref):
    sources = got_ref.shape[0]
    rows = disp_ref.shape[1]
    patch = lax.axis_index("patch")
    first = lax.axis_index("slab") * 4
    row_ids = iota((rows, 128), 0).astype(F32).astype(BF)
    lane_ids = iota((128, 128), 0).astype(F32).astype(BF)
    none = jnp.zeros((rows, 128), BF)
    ones, zeros = jnp.ones((128, 128), BF), jnp.zeros((128, 128), BF)
    total = jnp.zeros((3 * rows, 128), F32)
    group = 8
    for base in range(0, sources, group):
        codes = [decode(got_ref[base : base + group, 6 + h, :].astype(F32)) for h in range(2)]
        row8 = [row.astype(BF) for row, _ in codes]
        lane8 = [lane.astype(BF) for _, lane in codes]
        for g in range(group):
            vals = got_ref[base + g]
            left, right = [], []
            for h in range(2):
                mask = row_ids == row8[h][g : g + 1]
                left.append(
                    jnp.concatenate(
                        [jnp.where(mask, vals[2 * c + h : 2 * c + h + 1], none) for c in range(3)],
                        axis=0,
                    )
                )
                right.append(jnp.where(lane_ids == lane8[h][g : g + 1], ones, zeros))
            total += nt(jnp.concatenate(left, axis=1), jnp.concatenate(right, axis=1))
    loads = total.reshape(3, rows, 128)
    new = disp_ref[...] + (loads - kd_ref[...]) / (36.0 * stiff_ref[...])[None]
    new_ref[...] = new
    flat = new.reshape(3 * rows, 128)
    high = flat.astype(BF)
    low = (flat - high.astype(F32)).astype(BF)
    both = jnp.concatenate([high, low], axis=0)
    for d in range(4):
        for h in range(2):
            code = got_ref[pl.ds(first + (patch ^ d), 1), 6 + h, :]
            pick_ref[2 * d + h : 2 * d + h + 1, :] = code.astype(F32)
    row, lane = decode(pick_ref[...])
    wide_ids = iota((rows, 256), 0).astype(F32)
    for d, reply in enumerate((r0, r1, r2, r3)):
        at = 2 * d
        hot = jnp.concatenate(
            [
                jnp.where(lane_ids == lane[at + h : at + h + 1].astype(BF), ones, zeros)
                for h in range(2)
            ],
            axis=1,
        )
        picked = jnp.dot(both, hot, preferred_element_type=F32)
        mask = wide_ids == jnp.concatenate([row[at : at + 1], row[at + 1 : at + 2]], axis=1)
        for c in range(3):
            part = picked[c * rows : (c + 1) * rows] + picked[(c + 3) * rows : (c + 4) * rows]
            reply[c : c + 1, :] = jnp.where(mask, part, 0.0).sum(axis=0, keepdims=True)


def store_kernel(value_ref, out_ref, sem):
    copy = pltpu.make_async_copy(value_ref, out_ref, sem)
    copy.start()
    copy.wait()


def store(value, name):
    return pl.pallas_call(
        store_kernel,
        out_shape=jax.ShapeDtypeStruct(value.shape, value.dtype),
        in_specs=vmem(1),
        out_specs=hbm(1)[0],
        scratch_shapes=[pltpu.SemaphoreType.DMA],
        compiler_params=params(),
        name=name,
    )(value)


def finish_kernel(r3, r2, r1, r0, out_ref):
    cap = r0.shape[1]
    patch = lax.axis_index("patch")
    for d, reply in enumerate((r0, r1, r2, r3)):
        start = pl.multiple_of((patch ^ d) * cap, cap)
        for c in range(3):
            out_ref[c, 0, :, pl.ds(start, cap)] = reply[c : c + 1, :]


def shell_kernel(
    one_ref, three_ref, disp_ref, stiff_ref, state_ref, kd_ref, out_ref, field_ref, bend_ref, sem
):
    copy = pltpu.make_async_copy(state_ref, out_ref, sem)
    copy.start()
    rows = disp_ref.shape[1]
    patch = lax.axis_index("patch")
    top = patch > 0
    bottom = patch < 3
    even = patch % 2 == 0
    one, three = (
        ref[:, :128].astype(F32) + ref[:, 128:].astype(F32)
        for ref in (one_ref, three_ref)
    )
    above = jnp.where(even, three, one)
    below = jnp.where(even, one, three)
    field_ref[...] = jnp.zeros_like(field_ref)
    bend_ref[...] = jnp.zeros_like(bend_ref)
    field_ref[:, 8 : 8 + rows, :] = disp_ref[...]
    lane = iota((1, 1, 128), 2)

    def sides(x):
        left = jnp.where(lane == 0, 0.0, pltpu.roll(x, 1, 2))
        right = jnp.where(lane == 127, 0.0, pltpu.roll(x, 127, 2))
        return left + right

    for c in range(3):
        field_ref[c, 6:8, :] = jnp.where(top, above[2 * c : 2 * c + 2], 0.0)
        field_ref[c, 8 + rows : 10 + rows, :] = jnp.where(bottom, below[2 * c : 2 * c + 2], 0.0)
    mid = field_ref[:, 7 : 9 + rows, :]
    bend = 4.0 * mid - (
        field_ref[:, 6 : 8 + rows, :] + field_ref[:, 8 : 10 + rows, :] + sides(mid)
    )
    bend_ref[:, 7 : 9 + rows, :] = bend
    for c in range(3):
        bend_ref[c, 7:8, :] = jnp.where(top, bend_ref[c, 7:8, :], 0.0)
        bend_ref[c, 8 + rows : 9 + rows, :] = jnp.where(
            bottom, bend_ref[c, 8 + rows : 9 + rows, :], 0.0
        )
    mid = bend_ref[:, 8 : 8 + rows, :]
    again = 4.0 * mid - (
        bend_ref[:, 7 : 7 + rows, :] + bend_ref[:, 9 : 9 + rows, :] + sides(mid)
    )
    kd_ref[...] = stiff_ref[...][None] * (again + 4.0 * mid)
    copy.wait()


def params():
    return pltpu.CompilerParams(vmem_limit_bytes=LIMIT)


def patch_pairs(d):
    return [(p, p ^ d) for p in range(4)]


def exchange_and_relax(message, displacement, stiffness, kd):
    slabs, owners = lax.axis_size("slab"), lax.axis_size("patch")
    rows = displacement.shape[1]
    sources = slabs * owners
    got = lax.all_to_all(
        message.reshape(sources, 8, 128), ("slab", "patch"), 0, 0, tiled=True
    )
    reply = jax.ShapeDtypeStruct((8, 256), F32)
    new, *replies = pl.pallas_call(
        owner_kernel,
        out_shape=(jax.ShapeDtypeStruct(displacement.shape, F32),) + (reply,) * 4,
        in_specs=vmem(4),
        out_specs=vmem(5),
        scratch_shapes=[pltpu.VMEM((8, 128), F32)],
        compiler_params=params(),
        name="owner",
    )(got, displacement, stiffness, kd)
    back = [lax.ppermute(replies[d], "patch", patch_pairs(d)) for d in (3, 2, 1)]
    back.append(replies[0])
    wall = pl.pallas_call(
        finish_kernel,
        out_shape=jax.ShapeDtypeStruct((3, 1, 1, owners * 256), F32),
        in_specs=vmem(4),
        out_specs=pl.BlockSpec(memory_space=pltpu.VMEM),
        compiler_params=params(),
        name="finish",
    )(*back)
    return store(new, "store_shell"), wall


def halves(value):
    high = value.astype(BF)
    low = (value - high.astype(F32)).astype(BF)
    return jnp.concatenate([high.astype(F32), low.astype(F32)], axis=1)


def lines_of(scale_ref, pad_ref):
    pad_ref[...] = jnp.zeros_like(pad_ref)
    pad_ref[0:2, 0 : scale_ref.shape[1]] = scale_ref[...]
    return pltpu.roll(pad_ref[...], 8, 1)


def near_kernel(
    state_hbm, rhs_hbm, scale_hbm, disp_hbm, near_ref, own_ref, far_ref, one_ref, three_ref,
    state_ref, rhs_ref, scale_ref, disp_ref, pad_ref, build_ref, sems,
):
    copies = [
        pltpu.make_async_copy(a, b, sems.at[i])
        for i, (a, b) in enumerate(
            (
                (scale_hbm, scale_ref),
                (state_hbm, state_ref),
                (rhs_hbm, rhs_ref),
                (disp_hbm, disp_ref),
            )
        )
    ]
    for copy in copies:
        copy.start()
    odd = lax.axis_index("slab") % 2
    even = lax.axis_index("patch") % 2 == 0
    cols = state_ref.shape[1]
    for copy in copies:
        copy.wait()
    for e in range(2):
        build_ref[e] = jnp.zeros((EDGE + 8, 256), F32)
    for i, row in enumerate((odd, 1 - odd)):
        for part, ref, at, third in (
            (0, state_ref, 2 * i, 8 + i),
            (2, rhs_ref, (4, 10)[i], None),
        ):
            value = ref[row]
            block = part + i
            if block == 3:
                far_ref[...] = value.astype(BF)
            else:
                own_ref[block * cols : (block + 1) * cols, :] = value.astype(BF)
            low, high = value[0:2], value[cols - 2 : cols]
            build_ref[0, at : at + 2, :] = jnp.where(even, high, low)
            build_ref[1, at : at + 2, :] = jnp.where(even, low, high)
            if third is not None:
                low, high = value[2:3], value[cols - 3 : cols - 2]
                build_ref[0, third : third + 1, :] = jnp.where(even, high, low)
                build_ref[1, third : third + 1, :] = jnp.where(even, low, high)
    near_ref[...] = state_ref[1 - odd].astype(BF)
    lines = lines_of(scale_ref, pad_ref)
    flip = odd == 1
    first = jnp.where(flip, lines[1:2], lines[0:1])
    second = jnp.where(flip, lines[0:1], lines[1:2])
    pair = jnp.concatenate([halves(first), halves(second), jnp.zeros((6, 256), F32)], axis=0)
    own_ref[3 * cols :, :] = pair.astype(BF)
    for e in range(2):
        build_ref[e, 6:8, :] = pair[0:2]
    rows = disp_ref.shape[1]
    for c in range(3):
        top = halves(disp_ref[c, 0:2, :])
        bottom = halves(disp_ref[c, rows - 2 : rows, :])
        at = EDGE + 2 * c
        build_ref[0, at : at + 2, :] = jnp.where(even, bottom, top)
        build_ref[1, at : at + 2, :] = jnp.where(even, top, bottom)
    one_ref[...] = build_ref[0].astype(BF)
    three_ref[...] = build_ref[1].astype(BF)


def sweep_kernel(
    state_ref,
    rhs_ref,
    scale_ref,
    near_ref,
    inner_ref,
    outer_ref,
    rest_ref,
    one_ref,
    three_ref,
    relay_ref,
    matrix_ref,
    x_ref,
    y_ref,
    inverse_ref,
    tmap_ref,
    elem_hbm,
    point_hbm,
    count_hbm,
    out_ref,
    message_hbm,
    v_ref,
    r_ref,
    s_ref,
    i_ref,
    line_ref,
    elem_ref,
    point_ref,
    count_ref,
    rows_ref,
    message_ref,
    sems,
):
    copies = [
        pltpu.make_async_copy(a, b, sems.at[i])
        for i, (a, b) in enumerate(
            ((elem_hbm, elem_ref), (point_hbm, point_ref), (count_hbm, count_ref))
        )
    ]
    for copy in copies:
        copy.start()
    slab, patch = lax.axis_index("slab"), lax.axis_index("patch")
    last_slab, last_patch = lax.axis_size("slab") - 1, lax.axis_size("patch") - 1
    odd = slab % 2
    even = patch % 2 == 0
    cols, width = state_ref.shape[1], state_ref.shape[2]
    wide = cols + 16
    inside = (slab > 0) & (slab < last_slab)
    col = iota((wide, width), 0)
    valid = (col >= 8) & (col < 8 + cols)
    valid = valid | ((col < 8) & (patch > 0)) | ((col >= 8 + cols) & (patch < last_patch))
    edge = valid.astype(F32)
    keep = edge * inside.astype(F32)
    v_ref[:, 0:8, :] = jnp.zeros((8, 8, width), F32)
    v_ref[:, 8 + cols :, :] = jnp.zeros((8, 8, width), F32)
    r_ref[:, 0:8, :] = jnp.zeros((6, 8, width), F32)
    r_ref[:, 8 + cols :, :] = jnp.zeros((6, 8, width), F32)
    tail = 3 * cols + 8
    strips = {
        0: (one_ref[0:EDGE], three_ref[0:EDGE]),
        1: (inner_ref[tail : tail + EDGE], inner_ref[tail + EDGE : tail + 2 * EDGE]),
        2: (rest_ref[cols : cols + THIN], rest_ref[cols + THIN : cols + 2 * THIN]),
    }
    sides = {}
    for kind, pair in strips.items():
        one, three = (x.astype(F32) for x in pair)
        sides[kind] = (jnp.where(even, three, one), jnp.where(even, one, three))
    lane = iota((1, 128), 1)
    line_ref[...] = jnp.zeros_like(line_ref)
    line_ref[0:2, 0:cols] = scale_ref[...]
    exact = pltpu.roll(line_ref[...], 8, 1)
    table = ((2, 1), (2, 0), (0, 0), (0, 1), (1, 1), (1, 0))
    for r, (kind, i) in enumerate(table):
        if kind == 0:
            row = odd if i == 0 else 1 - odd
            v_ref[r + 1, 8 : 8 + cols, :] = state_ref[row]
            r_ref[r, 8 : 8 + cols, :] = rhs_ref[row]
            line = jnp.where(row == 1, exact[1:2], exact[0:1])
        else:
            if kind == 1:
                value = near_ref[...] if i == 1 else inner_ref[0:cols]
                rhs = inner_ref[2 * cols + 8 : 3 * cols + 8] if i == 1 else inner_ref[cols : 2 * cols]
                ref, below = inner_ref, 2 * cols
            else:
                value = outer_ref[i * cols : (i + 1) * cols]
                rhs = rest_ref[cols + 2 * THIN :] if i == 1 else outer_ref[2 * cols : 3 * cols]
                ref, below = outer_ref, 3 * cols
            v_ref[r + 1, 8 : 8 + cols, :] = value.astype(F32)
            r_ref[r, 8 : 8 + cols, :] = rhs.astype(F32)
            both = ref[below : below + 8, :].astype(F32)[i : i + 1]
            line = both[:, :128] + both[:, 128:]
        for side, start, far in zip(sides[kind], (6, 8 + cols), (5, 10 + cols)):
            v_ref[r + 1, start : start + 2, :] = side[2 * i : 2 * i + 2]
            if i == 0:
                r_ref[r, start : start + 2, :] = side[4:6]
            elif kind < 2:
                r_ref[r, start : start + 2, :] = side[10:12]
            if kind == 0:
                v_ref[r + 1, far : far + 1, :] = side[8 + i : 9 + i]
            both = side[6 + i : 7 + i]
            far = pltpu.roll(both[:, :128] + both[:, 128:], 64, 1)
            here = (lane >= start) & (lane < start + 2)
            line = jnp.where(here, far, line)
        line_ref[r : r + 1, :] = jnp.where(line > 0.0, line, 1.0)
    line_ref[6:8, :] = jnp.ones((2, 128), F32)
    v_ref[0, 8 : 8 + cols, :] = rest_ref[0:cols, :].astype(F32)
    beyond = (slab != 1) & (slab != last_slab - 1)
    v_ref[7, 8 : 8 + cols, :] = relay_ref[...].astype(F32) * beyond.astype(F32)
    for r in range(8):
        v_ref[r] = v_ref[r] * (keep if r < 3 else edge)
    lines = line_ref[...]
    columns = jnp.transpose(lines)
    inverses = jnp.transpose(1.0 / lines)
    for r in range(6):
        s_ref[r] = jnp.broadcast_to(columns[:wide, r : r + 1], (wide, width))
        i_ref[r] = jnp.broadcast_to(inverses[:wide, r : r + 1], (wide, width))
    for copy in copies:
        copy.wait()
    elem = elem_ref[0]
    owners = rows_ref.shape[0]
    live, code = slot_codes(point_ref[0], count_ref.at[0], owners)
    hot = ((iota((2 * cols, elem.shape[1]), 0) == elem) & live).astype(F32).astype(BF)
    for sweep in range(SWEEPS):
        a, b = 1 + sweep, 7 - sweep
        value = relaxed(
            v_ref[a:b],
            v_ref[a - 1 : b - 1],
            v_ref[a + 1 : b + 1],
            r_ref[a - 1 : b - 1],
            s_ref[a - 1 : b - 1],
            i_ref[a - 1 : b - 1],
            (matrix_ref, x_ref, y_ref, inverse_ref),
        )
        for j in range(b - a):
            v_ref[a + j] = value[j] * (keep if a + j < 3 else edge)
    out_ref[odd] = v_ref[3, 8 : 8 + cols, :]
    out_ref[1 - odd] = v_ref[4, 8 : 8 + cols, :]
    final = out_ref[...].astype(BF).reshape(2 * cols, width)
    pull = jnp.dot(nt(tmap_ref[...], final).astype(BF), hot, preferred_element_type=F32)
    for k in range(owners):
        for j in range(4):
            source = code if j == 3 else pull[j : j + 1]
            for h in range(2):
                start = k * 256 + h * 128
                rows_ref[k, 2 * j + h : 2 * j + h + 1, :] = source[:, start : start + 128]
    message_ref[...] = jnp.broadcast_to(rows_ref[...].astype(BF)[None], message_ref.shape)
    part = message_ref.shape[0]
    copies = [
        pltpu.make_async_copy(message_ref, message_hbm.at[i * part : (i + 1) * part], sems.at[3 + i])
        for i in range(message_hbm.shape[0] // part)
    ]
    for copy in copies:
        copy.start()
    for copy in copies:
        copy.wait()


def relaxed(center, up, down, rhs, scale, inverse_scale, matrices):
    matrix_ref, x_ref, y_ref, inverse_ref = matrices
    n, wide, width = center.shape
    flat = (n * wide, width)
    up, mid, down = (x.astype(BF).astype(F32) for x in (up, center, down))
    nx = (up + down).astype(BF)
    ny = (pltpu.roll(mid, 1, 1) + pltpu.roll(mid, wide - 1, 1)).astype(BF)
    own = jnp.dot(mid.astype(BF).reshape(flat), matrix_ref[...], preferred_element_type=F32)
    both = jnp.concatenate([nx.reshape(flat), ny.reshape(flat)], axis=1)
    couple = jnp.concatenate([x_ref[...], y_ref[...]], axis=0)
    side = jnp.dot(both, couple, preferred_element_type=F32)
    residue = (rhs.reshape(flat) - (scale.reshape(flat) * own - side)).astype(BF)
    update = jnp.dot(residue, inverse_ref[...], preferred_element_type=F32)
    update = update * inverse_scale.reshape(flat)
    return center + update.reshape(center.shape)


def call(kernel, name, out_shape, operands, scratch=(), in_specs=None, out_specs=None):
    return pl.pallas_call(
        kernel,
        out_shape=out_shape,
        in_specs=in_specs or vmem(len(operands)),
        out_specs=out_specs or jax.tree.map(lambda _: vmem(1)[0], out_shape),
        scratch_shapes=list(scratch),
        compiler_params=params(),
        name=name,
    )(*operands)


def shards(
    fluid_state,
    fluid_rhs,
    element_scale,
    element_matrix,
    couple_x,
    couple_y,
    block_inverse,
    traction_map,
    slot_elem,
    slot_point,
    slot_count,
    displacement,
    stiffness,
):
    cols, width = fluid_state.shape[1:]
    slots = slot_elem.shape[2]
    slabs, owners = lax.axis_size("slab"), lax.axis_size("patch")
    shape = jax.ShapeDtypeStruct
    inner_pairs = [(s, s ^ 1) for s in range(slabs)]
    outer_pairs = [(s, (s + 1) % slabs) for s in range(1, slabs, 2)]
    outer_pairs = outer_pairs + [(b, a) for a, b in outer_pairs]
    strip = shape((EDGE + 8, width), BF)
    row = shape((cols, width), BF)
    near, own, far, to_one, to_three = call(
        near_kernel,
        "near",
        (row, shape((3 * cols + 8, width), BF), row, strip, strip),
        tuple(
            pltpu.with_memory_space_constraint(x, pltpu.HBM)
            for x in (fluid_state, fluid_rhs, element_scale, displacement)
        ),
        [
            pltpu.VMEM(fluid_state.shape, F32),
            pltpu.VMEM(fluid_rhs.shape, F32),
            pltpu.VMEM(element_scale.shape, F32),
            pltpu.VMEM(displacement.shape, F32),
            pltpu.VMEM((8, 128), F32),
            pltpu.VMEM((2, EDGE + 8, width), F32),
            pltpu.SemaphoreType.DMA((4,)),
        ],
        in_specs=hbm(4),
    )
    outer = lax.ppermute(own, "slab", outer_pairs)
    inner_near = lax.ppermute(near, "slab", inner_pairs)
    from_three = lax.ppermute(to_three, "patch", patch_pairs(3))
    from_one = lax.ppermute(to_one, "patch", patch_pairs(1))
    strips = [from_one[:EDGE], from_three[:EDGE]]
    thin = [from_one[:THIN], from_three[:THIN]]
    rest = lax.ppermute(jnp.concatenate([inner_near] + thin + [far]), "slab", outer_pairs)
    others = jnp.concatenate([own[:cols], own[2 * cols :], far] + strips)
    others, _ = lax.optimization_barrier((others, inner_near))
    inner = lax.ppermute(others, "slab", inner_pairs)
    relay = lax.ppermute(outer[:cols], "slab", inner_pairs)
    wide = cols + 16
    state, message = call(
        sweep_kernel,
        "sweep",
        (shape(fluid_state.shape, F32), shape((slabs, owners, 8, 128), BF)),
        (
            fluid_state,
            fluid_rhs,
            element_scale,
            inner_near,
            inner,
            outer,
            rest,
            from_one,
            from_three,
            relay,
            element_matrix,
            couple_x,
            couple_y,
            block_inverse,
            traction_map,
            slot_elem,
            slot_point,
            slot_count,
        ),
        [
            pltpu.VMEM((8, wide, width), F32),
            pltpu.VMEM((6, wide, width), F32),
            pltpu.VMEM((6, wide, width), F32),
            pltpu.VMEM((6, wide, width), F32),
            pltpu.VMEM((8, 128), F32),
            pltpu.VMEM((1, 1, slots), I32),
            pltpu.VMEM((1, 1, slots), I32),
            pltpu.VMEM((1, 1, owners), I32),
            pltpu.VMEM((owners, 8, 128), F32),
            pltpu.VMEM((slabs // 4, owners, 8, 128), BF),
            pltpu.SemaphoreType.DMA((7,)),
        ],
        in_specs=vmem(15) + hbm(3),
        out_specs=tuple(vmem(1) + hbm(1)),
    )
    kd, final = call(
        shell_kernel,
        "shell",
        (shape(displacement.shape, F32), shape(state.shape, F32)),
        (from_one[EDGE:], from_three[EDGE:], displacement, stiffness, state),
        [pltpu.VMEM((3, displacement.shape[1] + 16, 128), F32)] * 2 + [pltpu.SemaphoreType.DMA],
        out_specs=tuple(vmem(1) + hbm(1)),
    )
    new, wall = exchange_and_relax(message, displacement, stiffness, kd)
    return final, new, wall


def solution(mesh):
    return jax.shard_map(
        shards,
        mesh=mesh,
        in_specs=(
            P("slab", "patch", None),
            P("slab", "patch", None),
            P("slab", "patch"),
            P(),
            P(),
            P(),
            P(),
            P(),
            P("slab", "patch", None),
            P("slab", "patch", None),
            P("slab", "patch", None),
            P(None, "patch", None),
            P("patch", None),
        ),
        out_specs=(
            P("slab", "patch", None),
            P(None, "patch", None),
            P(None, "slab", "patch", None),
        ),
        check_vma=False,
    )
```

```python
import jax
import jax.numpy as jnp
from jax import lax
from jax.experimental import pallas as pl
from jax.experimental.pallas import tpu as pltpu
from jax.sharding import PartitionSpec as P

SWEEPS = 3
BF = jnp.bfloat16
F32 = jnp.float32
I32 = jnp.int32
LIMIT = 48 << 20
EDGE = 16
THIN = 8


def vmem(n):
    return [pl.BlockSpec(memory_space=pltpu.VMEM)] * n


def hbm(n):
    return [pl.BlockSpec(memory_space=pltpu.HBM)] * n


def iota(shape, dim):
    return lax.broadcasted_iota(I32, shape, dim)


def nt(a, b):
    return lax.dot_general(a, b, (((1,), (1,)), ((), ())), preferred_element_type=F32)


def slot_codes(point, count_ref, owners):
    slots = point.shape[1]
    cap = slots // owners
    slot = iota((1, slots), 1)
    owner = slot // cap
    limit = jnp.zeros((1, slots), I32)
    for k in range(owners):
        limit = jnp.where(owner == k, count_ref[0:1, k : k + 1], limit)
    live = (slot - owner * cap) < limit
    row = point // 128
    code = (128 + (point - row * 128)).astype(F32)
    for b in range(6):
        code = code * jnp.where((row >> b) & 1 == 1, F32(2.0 ** (2**b)), F32(1.0))
    return live, jnp.where(live, code, 0.0)


def decode(code):
    row = jnp.zeros(code.shape, F32)
    for b in (5, 4, 3, 2, 1, 0):
        big = code >= F32(128.0 * 2.0 ** (2**b))
        row = row + jnp.where(big, F32(2**b), 0.0)
        code = code * jnp.where(big, F32(2.0 ** -(2**b)), 1.0)
    return row, code - 128.0


def owner_kernel(got_ref, disp_ref, stiff_ref, kd_ref, new_ref, r0, r1, r2, r3, pick_ref):
    sources = got_ref.shape[0]
    rows = disp_ref.shape[1]
    patch = lax.axis_index("patch")
    first = lax.axis_index("slab") * 4
    row_ids = iota((rows, 128), 0).astype(F32).astype(BF)
    lane_ids = iota((128, 128), 0).astype(F32).astype(BF)
    none = jnp.zeros((rows, 128), BF)
    ones, zeros = jnp.ones((128, 128), BF), jnp.zeros((128, 128), BF)
    total = jnp.zeros((3 * rows, 128), F32)
    group = 8
    for base in range(0, sources, group):
        codes = [decode(got_ref[base : base + group, 6 + h, :].astype(F32)) for h in range(2)]
        row8 = [row.astype(BF) for row, _ in codes]
        lane8 = [lane.astype(BF) for _, lane in codes]
        for g in range(group):
            vals = got_ref[base + g]
            left, right = [], []
            for h in range(2):
                mask = row_ids == row8[h][g : g + 1]
                left.append(
                    jnp.concatenate(
                        [jnp.where(mask, vals[2 * c + h : 2 * c + h + 1], none) for c in range(3)],
                        axis=0,
                    )
                )
                right.append(jnp.where(lane_ids == lane8[h][g : g + 1], ones, zeros))
            total += nt(jnp.concatenate(left, axis=1), jnp.concatenate(right, axis=1))
    loads = total.reshape(3, rows, 128)
    new = disp_ref[...] + (loads - kd_ref[...]) / (36.0 * stiff_ref[...])[None]
    new_ref[...] = new
    flat = new.reshape(3 * rows, 128)
    high = flat.astype(BF)
    low = (flat - high.astype(F32)).astype(BF)
    both = jnp.concatenate([high, low], axis=0)
    for d in range(4):
        for h in range(2):
            code = got_ref[pl.ds(first + (patch ^ d), 1), 6 + h, :]
            pick_ref[2 * d + h : 2 * d + h + 1, :] = code.astype(F32)
    row, lane = decode(pick_ref[...])
    wide_ids = iota((rows, 256), 0).astype(F32)
    for d, reply in enumerate((r0, r1, r2, r3)):
        at = 2 * d
        hot = jnp.concatenate(
            [
                jnp.where(lane_ids == lane[at + h : at + h + 1].astype(BF), ones, zeros)
                for h in range(2)
            ],
            axis=1,
        )
        picked = jnp.dot(both, hot, preferred_element_type=F32)
        mask = wide_ids == jnp.concatenate([row[at : at + 1], row[at + 1 : at + 2]], axis=1)
        for c in range(3):
            part = picked[c * rows : (c + 1) * rows] + picked[(c + 3) * rows : (c + 4) * rows]
            reply[c : c + 1, :] = jnp.where(mask, part, 0.0).sum(axis=0, keepdims=True)


def store_kernel(value_ref, out_ref, sem):
    copy = pltpu.make_async_copy(value_ref, out_ref, sem)
    copy.start()
    copy.wait()


def store(value, name):
    return pl.pallas_call(
        store_kernel,
        out_shape=jax.ShapeDtypeStruct(value.shape, value.dtype),
        in_specs=vmem(1),
        out_specs=hbm(1)[0],
        scratch_shapes=[pltpu.SemaphoreType.DMA],
        compiler_params=params(),
        name=name,
    )(value)


def finish_kernel(r3, r2, r1, r0, out_ref):
    cap = r0.shape[1]
    patch = lax.axis_index("patch")
    for d, reply in enumerate((r0, r1, r2, r3)):
        start = pl.multiple_of((patch ^ d) * cap, cap)
        for c in range(3):
            out_ref[c, 0, :, pl.ds(start, cap)] = reply[c : c + 1, :]


def shell_kernel(
    one_ref, three_ref, disp_ref, stiff_ref, state_ref, kd_ref, out_ref, field_ref, bend_ref, sem
):
    copy = pltpu.make_async_copy(state_ref, out_ref, sem)
    copy.start()
    rows = disp_ref.shape[1]
    patch = lax.axis_index("patch")
    top = patch > 0
    bottom = patch < 3
    even = patch % 2 == 0
    one, three = (
        ref[:, :128].astype(F32) + ref[:, 128:].astype(F32)
        for ref in (one_ref, three_ref)
    )
    above = jnp.where(even, three, one)
    below = jnp.where(even, one, three)
    field_ref[...] = jnp.zeros_like(field_ref)
    bend_ref[...] = jnp.zeros_like(bend_ref)
    field_ref[:, 8 : 8 + rows, :] = disp_ref[...]
    lane = iota((1, 1, 128), 2)

    def sides(x):
        left = jnp.where(lane == 0, 0.0, pltpu.roll(x, 1, 2))
        right = jnp.where(lane == 127, 0.0, pltpu.roll(x, 127, 2))
        return left + right

    for c in range(3):
        field_ref[c, 6:8, :] = jnp.where(top, above[2 * c : 2 * c + 2], 0.0)
        field_ref[c, 8 + rows : 10 + rows, :] = jnp.where(bottom, below[2 * c : 2 * c + 2], 0.0)
    mid = field_ref[:, 7 : 9 + rows, :]
    bend = 4.0 * mid - (
        field_ref[:, 6 : 8 + rows, :] + field_ref[:, 8 : 10 + rows, :] + sides(mid)
    )
    bend_ref[:, 7 : 9 + rows, :] = bend
    for c in range(3):
        bend_ref[c, 7:8, :] = jnp.where(top, bend_ref[c, 7:8, :], 0.0)
        bend_ref[c, 8 + rows : 9 + rows, :] = jnp.where(
            bottom, bend_ref[c, 8 + rows : 9 + rows, :], 0.0
        )
    mid = bend_ref[:, 8 : 8 + rows, :]
    again = 4.0 * mid - (
        bend_ref[:, 7 : 7 + rows, :] + bend_ref[:, 9 : 9 + rows, :] + sides(mid)
    )
    kd_ref[...] = stiff_ref[...][None] * (again + 4.0 * mid)
    copy.wait()


def params():
    return pltpu.CompilerParams(vmem_limit_bytes=LIMIT)


def patch_pairs(d):
    return [(p, p ^ d) for p in range(4)]


def exchange_and_relax(message, displacement, stiffness, kd):
    slabs, owners = lax.axis_size("slab"), lax.axis_size("patch")
    rows = displacement.shape[1]
    sources = slabs * owners
    got = lax.all_to_all(
        message.reshape(sources, 8, 128), ("slab", "patch"), 0, 0, tiled=True
    )
    reply = jax.ShapeDtypeStruct((8, 256), F32)
    new, *replies = pl.pallas_call(
        owner_kernel,
        out_shape=(jax.ShapeDtypeStruct(displacement.shape, F32),) + (reply,) * 4,
        in_specs=vmem(4),
        out_specs=vmem(5),
        scratch_shapes=[pltpu.VMEM((8, 128), F32)],
        compiler_params=params(),
        name="owner",
    )(got, displacement, stiffness, kd)
    back = [lax.ppermute(replies[d], "patch", patch_pairs(d)) for d in (3, 2, 1)]
    back.append(replies[0])
    wall = pl.pallas_call(
        finish_kernel,
        out_shape=jax.ShapeDtypeStruct((3, 1, 1, owners * 256), F32),
        in_specs=vmem(4),
        out_specs=pl.BlockSpec(memory_space=pltpu.VMEM),
        compiler_params=params(),
        name="finish",
    )(*back)
    return store(new, "store_shell"), wall


def halves(value):
    high = value.astype(BF)
    low = (value - high.astype(F32)).astype(BF)
    return jnp.concatenate([high.astype(F32), low.astype(F32)], axis=1)


def lines_of(scale_ref, pad_ref):
    pad_ref[...] = jnp.zeros_like(pad_ref)
    pad_ref[0:2, 0 : scale_ref.shape[1]] = scale_ref[...]
    return pltpu.roll(pad_ref[...], 8, 1)


def near_kernel(
    state_hbm, rhs_hbm, scale_hbm, disp_hbm, near_ref, own_ref, far_ref, one_ref, three_ref,
    state_ref, rhs_ref, scale_ref, disp_ref, pad_ref, build_ref, sems,
):
    copies = [
        pltpu.make_async_copy(a, b, sems.at[i])
        for i, (a, b) in enumerate(
            (
                (scale_hbm, scale_ref),
                (state_hbm, state_ref),
                (rhs_hbm, rhs_ref),
                (disp_hbm, disp_ref),
            )
        )
    ]
    for copy in copies:
        copy.start()
    odd = lax.axis_index("slab") % 2
    even = lax.axis_index("patch") % 2 == 0
    cols = state_ref.shape[1]
    for copy in copies:
        copy.wait()
    for e in range(2):
        build_ref[e] = jnp.zeros((EDGE + 8, 256), F32)
    for i, row in enumerate((odd, 1 - odd)):
        for part, ref, at, third in (
            (0, state_ref, 2 * i, 8 + i),
            (2, rhs_ref, (4, 10)[i], None),
        ):
            value = ref[row]
            block = part + i
            if block == 3:
                far_ref[...] = value.astype(BF)
            else:
                own_ref[block * cols : (block + 1) * cols, :] = value.astype(BF)
            low, high = value[0:2], value[cols - 2 : cols]
            build_ref[0, at : at + 2, :] = jnp.where(even, high, low)
            build_ref[1, at : at + 2, :] = jnp.where(even, low, high)
            if third is not None:
                low, high = value[2:3], value[cols - 3 : cols - 2]
                build_ref[0, third : third + 1, :] = jnp.where(even, high, low)
                build_ref[1, third : third + 1, :] = jnp.where(even, low, high)
    near_ref[...] = state_ref[1 - odd].astype(BF)
    lines = lines_of(scale_ref, pad_ref)
    flip = odd == 1
    first = jnp.where(flip, lines[1:2], lines[0:1])
    second = jnp.where(flip, lines[0:1], lines[1:2])
    pair = jnp.concatenate([halves(first), halves(second), jnp.zeros((6, 256), F32)], axis=0)
    own_ref[3 * cols :, :] = pair.astype(BF)
    for e in range(2):
        build_ref[e, 6:8, :] = pair[0:2]
    rows = disp_ref.shape[1]
    for c in range(3):
        top = halves(disp_ref[c, 0:2, :])
        bottom = halves(disp_ref[c, rows - 2 : rows, :])
        at = EDGE + 2 * c
        build_ref[0, at : at + 2, :] = jnp.where(even, bottom, top)
        build_ref[1, at : at + 2, :] = jnp.where(even, top, bottom)
    one_ref[...] = build_ref[0].astype(BF)
    three_ref[...] = build_ref[1].astype(BF)


def sweep_kernel(
    state_ref,
    rhs_ref,
    scale_ref,
    near_ref,
    inner_ref,
    outer_ref,
    rest_ref,
    one_ref,
    three_ref,
    relay_ref,
    matrix_ref,
    x_ref,
    y_ref,
    inverse_ref,
    tmap_ref,
    elem_hbm,
    point_hbm,
    count_hbm,
    out_ref,
    message_hbm,
    v_ref,
    r_ref,
    s_ref,
    i_ref,
    line_ref,
    elem_ref,
    point_ref,
    count_ref,
    rows_ref,
    message_ref,
    sems,
):
    copies = [
        pltpu.make_async_copy(a, b, sems.at[i])
        for i, (a, b) in enumerate(
            ((elem_hbm, elem_ref), (point_hbm, point_ref), (count_hbm, count_ref))
        )
    ]
    for copy in copies:
        copy.start()
    slab, patch = lax.axis_index("slab"), lax.axis_index("patch")
    last_slab, last_patch = lax.axis_size("slab") - 1, lax.axis_size("patch") - 1
    odd = slab % 2
    even = patch % 2 == 0
    cols, width = state_ref.shape[1], state_ref.shape[2]
    wide = cols + 16
    inside = (slab > 0) & (slab < last_slab)
    col = iota((wide, width), 0)
    valid = (col >= 8) & (col < 8 + cols)
    valid = valid | ((col < 8) & (patch > 0)) | ((col >= 8 + cols) & (patch < last_patch))
    edge = valid.astype(F32)
    keep = edge * inside.astype(F32)
    v_ref[:, 0:8, :] = jnp.zeros((8, 8, width), F32)
    v_ref[:, 8 + cols :, :] = jnp.zeros((8, 8, width), F32)
    r_ref[:, 0:8, :] = jnp.zeros((6, 8, width), F32)
    r_ref[:, 8 + cols :, :] = jnp.zeros((6, 8, width), F32)
    tail = 3 * cols + 8
    strips = {
        0: (one_ref[0:EDGE], three_ref[0:EDGE]),
        1: (inner_ref[tail : tail + EDGE], inner_ref[tail + EDGE : tail + 2 * EDGE]),
        2: (rest_ref[cols : cols + THIN], rest_ref[cols + THIN : cols + 2 * THIN]),
    }
    sides = {}
    for kind, pair in strips.items():
        one, three = (x.astype(F32) for x in pair)
        sides[kind] = (jnp.where(even, three, one), jnp.where(even, one, three))
    lane = iota((1, 128), 1)
    line_ref[...] = jnp.zeros_like(line_ref)
    line_ref[0:2, 0:cols] = scale_ref[...]
    exact = pltpu.roll(line_ref[...], 8, 1)
    table = ((2, 1), (2, 0), (0, 0), (0, 1), (1, 1), (1, 0))
    for r, (kind, i) in enumerate(table):
        if kind == 0:
            row = odd if i == 0 else 1 - odd
            v_ref[r + 1, 8 : 8 + cols, :] = state_ref[row]
            r_ref[r, 8 : 8 + cols, :] = rhs_ref[row]
            line = jnp.where(row == 1, exact[1:2], exact[0:1])
        else:
            if kind == 1:
                value = near_ref[...] if i == 1 else inner_ref[0:cols]
                rhs = inner_ref[2 * cols + 8 : 3 * cols + 8] if i == 1 else inner_ref[cols : 2 * cols]
                ref, below = inner_ref, 2 * cols
            else:
                value = outer_ref[i * cols : (i + 1) * cols]
                rhs = rest_ref[cols + 2 * THIN :] if i == 1 else outer_ref[2 * cols : 3 * cols]
                ref, below = outer_ref, 3 * cols
            v_ref[r + 1, 8 : 8 + cols, :] = value.astype(F32)
            r_ref[r, 8 : 8 + cols, :] = rhs.astype(F32)
            both = ref[below : below + 8, :].astype(F32)[i : i + 1]
            line = both[:, :128] + both[:, 128:]
        for side, start, far in zip(sides[kind], (6, 8 + cols), (5, 10 + cols)):
            v_ref[r + 1, start : start + 2, :] = side[2 * i : 2 * i + 2]
            if i == 0:
                r_ref[r, start : start + 2, :] = side[4:6]
            elif kind < 2:
                r_ref[r, start : start + 2, :] = side[10:12]
            if kind == 0:
                v_ref[r + 1, far : far + 1, :] = side[8 + i : 9 + i]
            both = side[6 + i : 7 + i]
            far = pltpu.roll(both[:, :128] + both[:, 128:], 64, 1)
            here = (lane >= start) & (lane < start + 2)
            line = jnp.where(here, far, line)
        line_ref[r : r + 1, :] = jnp.where(line > 0.0, line, 1.0)
    line_ref[6:8, :] = jnp.ones((2, 128), F32)
    v_ref[0, 8 : 8 + cols, :] = rest_ref[0:cols, :].astype(F32)
    beyond = (slab != 1) & (slab != last_slab - 1)
    v_ref[7, 8 : 8 + cols, :] = relay_ref[...].astype(F32) * beyond.astype(F32)
    for r in range(8):
        v_ref[r] = v_ref[r] * (keep if r < 3 else edge)
    lines = line_ref[...]
    columns = jnp.transpose(lines)
    inverses = jnp.transpose(1.0 / lines)
    for r in range(6):
        s_ref[r] = jnp.broadcast_to(columns[:wide, r : r + 1], (wide, width))
        i_ref[r] = jnp.broadcast_to(inverses[:wide, r : r + 1], (wide, width))
    for sweep in range(SWEEPS):
        a, b = 1 + sweep, 7 - sweep
        value = relaxed(
            v_ref[a:b],
            v_ref[a - 1 : b - 1],
            v_ref[a + 1 : b + 1],
            r_ref[a - 1 : b - 1],
            s_ref[a - 1 : b - 1],
            i_ref[a - 1 : b - 1],
            (matrix_ref, x_ref, y_ref, inverse_ref),
        )
        for j in range(b - a):
            v_ref[a + j] = value[j] * (keep if a + j < 3 else edge)
    out_ref[odd] = v_ref[3, 8 : 8 + cols, :]
    out_ref[1 - odd] = v_ref[4, 8 : 8 + cols, :]
    final = out_ref[...].astype(BF).reshape(2 * cols, width)
    for copy in copies:
        copy.wait()
    elem = elem_ref[0]
    owners = rows_ref.shape[0]
    live, code = slot_codes(point_ref[0], count_ref.at[0], owners)
    hot = ((iota((2 * cols, elem.shape[1]), 0) == elem) & live).astype(F32).astype(BF)
    pull = jnp.dot(nt(tmap_ref[...], final).astype(BF), hot, preferred_element_type=F32)
    for k in range(owners):
        for j in range(4):
            source = code if j == 3 else pull[j : j + 1]
            for h in range(2):
                start = k * 256 + h * 128
                rows_ref[k, 2 * j + h : 2 * j + h + 1, :] = source[:, start : start + 128]
    message_ref[...] = jnp.broadcast_to(rows_ref[...].astype(BF)[None], message_ref.shape)
    part = message_ref.shape[0]
    copies = [
        pltpu.make_async_copy(message_ref, message_hbm.at[i * part : (i + 1) * part], sems.at[3 + i])
        for i in range(message_hbm.shape[0] // part)
    ]
    for copy in copies:
        copy.start()
    for copy in copies:
        copy.wait()


def relaxed(center, up, down, rhs, scale, inverse_scale, matrices):
    matrix_ref, x_ref, y_ref, inverse_ref = matrices
    n, wide, width = center.shape
    flat = (n * wide, width)
    up, mid, down = (x.astype(BF).astype(F32) for x in (up, center, down))
    nx = (up + down).astype(BF)
    ny = (pltpu.roll(mid, 1, 1) + pltpu.roll(mid, wide - 1, 1)).astype(BF)
    own = jnp.dot(mid.astype(BF).reshape(flat), matrix_ref[...], preferred_element_type=F32)
    side = jnp.dot(nx.reshape(flat), x_ref[...], preferred_element_type=F32)
    side += jnp.dot(ny.reshape(flat), y_ref[...], preferred_element_type=F32)
    residue = (rhs.reshape(flat) - (scale.reshape(flat) * own - side)).astype(BF)
    update = jnp.dot(residue, inverse_ref[...], preferred_element_type=F32)
    update = update * inverse_scale.reshape(flat)
    return center + update.reshape(center.shape)


def call(kernel, name, out_shape, operands, scratch=(), in_specs=None, out_specs=None):
    return pl.pallas_call(
        kernel,
        out_shape=out_shape,
        in_specs=in_specs or vmem(len(operands)),
        out_specs=out_specs or jax.tree.map(lambda _: vmem(1)[0], out_shape),
        scratch_shapes=list(scratch),
        compiler_params=params(),
        name=name,
    )(*operands)


def shards(
    fluid_state,
    fluid_rhs,
    element_scale,
    element_matrix,
    couple_x,
    couple_y,
    block_inverse,
    traction_map,
    slot_elem,
    slot_point,
    slot_count,
    displacement,
    stiffness,
):
    cols, width = fluid_state.shape[1:]
    slots = slot_elem.shape[2]
    slabs, owners = lax.axis_size("slab"), lax.axis_size("patch")
    shape = jax.ShapeDtypeStruct
    inner_pairs = [(s, s ^ 1) for s in range(slabs)]
    outer_pairs = [(s, (s + 1) % slabs) for s in range(1, slabs, 2)]
    outer_pairs = outer_pairs + [(b, a) for a, b in outer_pairs]
    strip = shape((EDGE + 8, width), BF)
    row = shape((cols, width), BF)
    near, own, far, to_one, to_three = call(
        near_kernel,
        "near",
        (row, shape((3 * cols + 8, width), BF), row, strip, strip),
        tuple(
            pltpu.with_memory_space_constraint(x, pltpu.HBM)
            for x in (fluid_state, fluid_rhs, element_scale, displacement)
        ),
        [
            pltpu.VMEM(fluid_state.shape, F32),
            pltpu.VMEM(fluid_rhs.shape, F32),
            pltpu.VMEM(element_scale.shape, F32),
            pltpu.VMEM(displacement.shape, F32),
            pltpu.VMEM((8, 128), F32),
            pltpu.VMEM((2, EDGE + 8, width), F32),
            pltpu.SemaphoreType.DMA((4,)),
        ],
        in_specs=hbm(4),
    )
    outer = lax.ppermute(own, "slab", outer_pairs)
    inner_near = lax.ppermute(near, "slab", inner_pairs)
    from_three = lax.ppermute(to_three, "patch", patch_pairs(3))
    from_one = lax.ppermute(to_one, "patch", patch_pairs(1))
    strips = [from_one[:EDGE], from_three[:EDGE]]
    thin = [from_one[:THIN], from_three[:THIN]]
    rest = lax.ppermute(jnp.concatenate([inner_near] + thin + [far]), "slab", outer_pairs)
    others = jnp.concatenate([own[:cols], own[2 * cols :], far] + strips)
    others, _ = lax.optimization_barrier((others, inner_near))
    inner = lax.ppermute(others, "slab", inner_pairs)
    relay = lax.ppermute(outer[:cols], "slab", inner_pairs)
    wide = cols + 16
    state, message = call(
        sweep_kernel,
        "sweep",
        (shape(fluid_state.shape, F32), shape((slabs, owners, 8, 128), BF)),
        (
            fluid_state,
            fluid_rhs,
            element_scale,
            inner_near,
            inner,
            outer,
            rest,
            from_one,
            from_three,
            relay,
            element_matrix,
            couple_x,
            couple_y,
            block_inverse,
            traction_map,
            slot_elem,
            slot_point,
            slot_count,
        ),
        [
            pltpu.VMEM((8, wide, width), F32),
            pltpu.VMEM((6, wide, width), F32),
            pltpu.VMEM((6, wide, width), F32),
            pltpu.VMEM((6, wide, width), F32),
            pltpu.VMEM((8, 128), F32),
            pltpu.VMEM((1, 1, slots), I32),
            pltpu.VMEM((1, 1, slots), I32),
            pltpu.VMEM((1, 1, owners), I32),
            pltpu.VMEM((owners, 8, 128), F32),
            pltpu.VMEM((slabs // 4, owners, 8, 128), BF),
            pltpu.SemaphoreType.DMA((7,)),
        ],
        in_specs=vmem(15) + hbm(3),
        out_specs=tuple(vmem(1) + hbm(1)),
    )
    kd, final = call(
        shell_kernel,
        "shell",
        (shape(displacement.shape, F32), shape(state.shape, F32)),
        (from_one[EDGE:], from_three[EDGE:], displacement, stiffness, state),
        [pltpu.VMEM((3, displacement.shape[1] + 16, 128), F32)] * 2 + [pltpu.SemaphoreType.DMA],
        out_specs=tuple(vmem(1) + hbm(1)),
    )
    new, wall = exchange_and_relax(message, displacement, stiffness, kd)
    return final, new, wall


def solution(mesh):
    return jax.shard_map(
        shards,
        mesh=mesh,
        in_specs=(
            P("slab", "patch", None),
            P("slab", "patch", None),
            P("slab", "patch"),
            P(),
            P(),
            P(),
            P(),
            P(),
            P("slab", "patch", None),
            P("slab", "patch", None),
            P("slab", "patch", None),
            P(None, "patch", None),
            P("patch", None),
        ),
        out_specs=(
            P("slab", "patch", None),
            P(None, "patch", None),
            P(None, "slab", "patch", None),
        ),
        check_vma=False,
    )
```

```python
import jax
import jax.numpy as jnp
from jax import lax
from jax.experimental import pallas as pl
from jax.experimental.pallas import tpu as pltpu
from jax.sharding import PartitionSpec as P

SWEEPS = 3
BF = jnp.bfloat16
F32 = jnp.float32
I32 = jnp.int32
LIMIT = 48 << 20
EDGE = 16
THIN = 8


def vmem(n):
    return [pl.BlockSpec(memory_space=pltpu.VMEM)] * n


def hbm(n):
    return [pl.BlockSpec(memory_space=pltpu.HBM)] * n


def iota(shape, dim):
    return lax.broadcasted_iota(I32, shape, dim)


def nt(a, b):
    return lax.dot_general(a, b, (((1,), (1,)), ((), ())), preferred_element_type=F32)


def slot_codes(point, count_ref, owners):
    slots = point.shape[1]
    cap = slots // owners
    slot = iota((1, slots), 1)
    owner = slot // cap
    limit = jnp.zeros((1, slots), I32)
    for k in range(owners):
        limit = jnp.where(owner == k, count_ref[0:1, k : k + 1], limit)
    live = (slot - owner * cap) < limit
    row = point // 128
    code = (128 + (point - row * 128)).astype(F32)
    for b in range(6):
        code = code * jnp.where((row >> b) & 1 == 1, F32(2.0 ** (2**b)), F32(1.0))
    return live, jnp.where(live, code, 0.0)


def decode(code):
    row = jnp.zeros(code.shape, F32)
    for b in (5, 4, 3, 2, 1, 0):
        big = code >= F32(128.0 * 2.0 ** (2**b))
        row = row + jnp.where(big, F32(2**b), 0.0)
        code = code * jnp.where(big, F32(2.0 ** -(2**b)), 1.0)
    return row, code - 128.0


def owner_kernel(got_ref, disp_ref, stiff_ref, kd_ref, new_ref, r0, r1, r2, r3, pick_ref):
    sources = got_ref.shape[0]
    rows = disp_ref.shape[1]
    patch = lax.axis_index("patch")
    first = lax.axis_index("slab") * 4
    row_ids = iota((rows, 128), 0).astype(F32).astype(BF)
    lane_ids = iota((128, 128), 0).astype(F32).astype(BF)
    none = jnp.zeros((rows, 128), BF)
    ones, zeros = jnp.ones((128, 128), BF), jnp.zeros((128, 128), BF)
    total = jnp.zeros((3 * rows, 128), F32)
    group = 8
    for base in range(0, sources, group):
        codes = [decode(got_ref[base : base + group, 6 + h, :].astype(F32)) for h in range(2)]
        row8 = [row.astype(BF) for row, _ in codes]
        lane8 = [lane.astype(BF) for _, lane in codes]
        for g in range(group):
            vals = got_ref[base + g]
            left, right = [], []
            for h in range(2):
                mask = row_ids == row8[h][g : g + 1]
                left.append(
                    jnp.concatenate(
                        [jnp.where(mask, vals[2 * c + h : 2 * c + h + 1], none) for c in range(3)],
                        axis=0,
                    )
                )
                right.append(jnp.where(lane_ids == lane8[h][g : g + 1], ones, zeros))
            total += nt(jnp.concatenate(left, axis=1), jnp.concatenate(right, axis=1))
    loads = total.reshape(3, rows, 128)
    new = disp_ref[...] + (loads - kd_ref[...]) / (36.0 * stiff_ref[...])[None]
    new_ref[...] = new
    flat = new.reshape(3 * rows, 128)
    high = flat.astype(BF)
    low = (flat - high.astype(F32)).astype(BF)
    both = jnp.concatenate([high, low], axis=0)
    for d in range(4):
        for h in range(2):
            code = got_ref[pl.ds(first + (patch ^ d), 1), 6 + h, :]
            pick_ref[2 * d + h : 2 * d + h + 1, :] = code.astype(F32)
    row, lane = decode(pick_ref[...])
    wide_ids = iota((rows, 256), 0).astype(F32)
    for d, reply in enumerate((r0, r1, r2, r3)):
        at = 2 * d
        hot = jnp.concatenate(
            [
                jnp.where(lane_ids == lane[at + h : at + h + 1].astype(BF), ones, zeros)
                for h in range(2)
            ],
            axis=1,
        )
        picked = jnp.dot(both, hot, preferred_element_type=F32)
        mask = wide_ids == jnp.concatenate([row[at : at + 1], row[at + 1 : at + 2]], axis=1)
        for c in range(3):
            part = picked[c * rows : (c + 1) * rows] + picked[(c + 3) * rows : (c + 4) * rows]
            reply[c : c + 1, :] = jnp.where(mask, part, 0.0).sum(axis=0, keepdims=True)


def store_kernel(value_ref, out_ref, sem):
    copy = pltpu.make_async_copy(value_ref, out_ref, sem)
    copy.start()
    copy.wait()


def store(value, name):
    return pl.pallas_call(
        store_kernel,
        out_shape=jax.ShapeDtypeStruct(value.shape, value.dtype),
        in_specs=vmem(1),
        out_specs=hbm(1)[0],
        scratch_shapes=[pltpu.SemaphoreType.DMA],
        compiler_params=params(),
        name=name,
    )(value)


def finish_kernel(r3, r2, r1, r0, out_ref):
    cap = r0.shape[1]
    patch = lax.axis_index("patch")
    for d, reply in enumerate((r0, r1, r2, r3)):
        start = pl.multiple_of((patch ^ d) * cap, cap)
        for c in range(3):
            out_ref[c, 0, :, pl.ds(start, cap)] = reply[c : c + 1, :]


def shell_kernel(
    one_ref, three_ref, disp_ref, stiff_ref, state_ref, kd_ref, out_ref, field_ref, bend_ref, sem
):
    copy = pltpu.make_async_copy(state_ref, out_ref, sem)
    copy.start()
    rows = disp_ref.shape[1]
    patch = lax.axis_index("patch")
    top = patch > 0
    bottom = patch < 3
    even = patch % 2 == 0
    one, three = (
        ref[:, :128].astype(F32) + ref[:, 128:].astype(F32)
        for ref in (one_ref, three_ref)
    )
    above = jnp.where(even, three, one)
    below = jnp.where(even, one, three)
    field_ref[...] = jnp.zeros_like(field_ref)
    bend_ref[...] = jnp.zeros_like(bend_ref)
    field_ref[:, 8 : 8 + rows, :] = disp_ref[...]
    lane = iota((1, 1, 128), 2)

    def sides(x):
        left = jnp.where(lane == 0, 0.0, pltpu.roll(x, 1, 2))
        right = jnp.where(lane == 127, 0.0, pltpu.roll(x, 127, 2))
        return left + right

    for c in range(3):
        field_ref[c, 6:8, :] = jnp.where(top, above[2 * c : 2 * c + 2], 0.0)
        field_ref[c, 8 + rows : 10 + rows, :] = jnp.where(bottom, below[2 * c : 2 * c + 2], 0.0)
    mid = field_ref[:, 7 : 9 + rows, :]
    bend = 4.0 * mid - (
        field_ref[:, 6 : 8 + rows, :] + field_ref[:, 8 : 10 + rows, :] + sides(mid)
    )
    bend_ref[:, 7 : 9 + rows, :] = bend
    for c in range(3):
        bend_ref[c, 7:8, :] = jnp.where(top, bend_ref[c, 7:8, :], 0.0)
        bend_ref[c, 8 + rows : 9 + rows, :] = jnp.where(
            bottom, bend_ref[c, 8 + rows : 9 + rows, :], 0.0
        )
    mid = bend_ref[:, 8 : 8 + rows, :]
    again = 4.0 * mid - (
        bend_ref[:, 7 : 7 + rows, :] + bend_ref[:, 9 : 9 + rows, :] + sides(mid)
    )
    kd_ref[...] = stiff_ref[...][None] * (again + 4.0 * mid)
    copy.wait()


def params():
    return pltpu.CompilerParams(vmem_limit_bytes=LIMIT)


def patch_pairs(d):
    return [(p, p ^ d) for p in range(4)]


def exchange_and_relax(message, displacement, stiffness, kd):
    slabs, owners = lax.axis_size("slab"), lax.axis_size("patch")
    rows = displacement.shape[1]
    sources = slabs * owners
    got = lax.all_to_all(
        message.reshape(sources, 8, 128), ("slab", "patch"), 0, 0, tiled=True
    )
    reply = jax.ShapeDtypeStruct((8, 256), F32)
    new, *replies = pl.pallas_call(
        owner_kernel,
        out_shape=(jax.ShapeDtypeStruct(displacement.shape, F32),) + (reply,) * 4,
        in_specs=vmem(4),
        out_specs=vmem(5),
        scratch_shapes=[pltpu.VMEM((8, 128), F32)],
        compiler_params=params(),
        name="owner",
    )(got, displacement, stiffness, kd)
    back = [lax.ppermute(replies[d], "patch", patch_pairs(d)) for d in (3, 2, 1)]
    back.append(replies[0])
    wall = pl.pallas_call(
        finish_kernel,
        out_shape=jax.ShapeDtypeStruct((3, 1, 1, owners * 256), F32),
        in_specs=vmem(4),
        out_specs=pl.BlockSpec(memory_space=pltpu.VMEM),
        compiler_params=params(),
        name="finish",
    )(*back)
    return store(new, "store_shell"), wall


def halves(value):
    high = value.astype(BF)
    low = (value - high.astype(F32)).astype(BF)
    return jnp.concatenate([high.astype(F32), low.astype(F32)], axis=1)


def lines_of(scale_ref, pad_ref):
    pad_ref[...] = jnp.zeros_like(pad_ref)
    pad_ref[0:2, 0 : scale_ref.shape[1]] = scale_ref[...]
    return pltpu.roll(pad_ref[...], 8, 1)


def near_kernel(
    state_hbm, rhs_hbm, scale_hbm, disp_hbm, near_ref, own_ref, far_ref, one_ref, three_ref,
    state_ref, rhs_ref, scale_ref, disp_ref, pad_ref, build_ref, sems,
):
    rows = disp_hbm.shape[1]
    copies = [
        pltpu.make_async_copy(a, b, sems.at[i])
        for i, (a, b) in enumerate(
            (
                (scale_hbm, scale_ref),
                (state_hbm, state_ref),
                (rhs_hbm, rhs_ref),
                (disp_hbm.at[:, 0:8], disp_ref.at[:, 0:8]),
                (disp_hbm.at[:, rows - 8 : rows], disp_ref.at[:, 8:16]),
            )
        )
    ]
    for copy in copies:
        copy.start()
    odd = lax.axis_index("slab") % 2
    even = lax.axis_index("patch") % 2 == 0
    cols = state_ref.shape[1]
    for e in range(2):
        build_ref[e] = jnp.zeros((EDGE + 8, 256), F32)
    copies[0].wait()
    lines = lines_of(scale_ref, pad_ref)
    flip = odd == 1
    first = jnp.where(flip, lines[1:2], lines[0:1])
    second = jnp.where(flip, lines[0:1], lines[1:2])
    pair = jnp.concatenate([halves(first), halves(second), jnp.zeros((6, 256), F32)], axis=0)
    own_ref[3 * cols :, :] = pair.astype(BF)
    for e in range(2):
        build_ref[e, 6:8, :] = pair[0:2]
    copies[1].wait()
    copies[2].wait()
    for i, row in enumerate((odd, 1 - odd)):
        for part, ref, at, third in (
            (0, state_ref, 2 * i, 8 + i),
            (2, rhs_ref, (4, 10)[i], None),
        ):
            value = ref[row]
            block = part + i
            if block == 3:
                far_ref[...] = value.astype(BF)
            else:
                own_ref[block * cols : (block + 1) * cols, :] = value.astype(BF)
            low, high = value[0:2], value[cols - 2 : cols]
            build_ref[0, at : at + 2, :] = jnp.where(even, high, low)
            build_ref[1, at : at + 2, :] = jnp.where(even, low, high)
            if third is not None:
                low, high = value[2:3], value[cols - 3 : cols - 2]
                build_ref[0, third : third + 1, :] = jnp.where(even, high, low)
                build_ref[1, third : third + 1, :] = jnp.where(even, low, high)
    near_ref[...] = state_ref[1 - odd].astype(BF)
    copies[3].wait()
    copies[4].wait()
    for c in range(3):
        top = halves(disp_ref[c, 0:2, :])
        bottom = halves(disp_ref[c, 14:16, :])
        at = EDGE + 2 * c
        build_ref[0, at : at + 2, :] = jnp.where(even, bottom, top)
        build_ref[1, at : at + 2, :] = jnp.where(even, top, bottom)
    one_ref[...] = build_ref[0].astype(BF)
    three_ref[...] = build_ref[1].astype(BF)


def sweep_kernel(
    state_ref,
    rhs_ref,
    scale_ref,
    near_ref,
    inner_ref,
    outer_ref,
    rest_ref,
    one_ref,
    three_ref,
    relay_ref,
    matrix_ref,
    x_ref,
    y_ref,
    inverse_ref,
    tmap_ref,
    elem_hbm,
    point_hbm,
    count_hbm,
    out_ref,
    message_hbm,
    v_ref,
    r_ref,
    s_ref,
    i_ref,
    line_ref,
    elem_ref,
    point_ref,
    count_ref,
    rows_ref,
    message_ref,
    sems,
):
    copies = [
        pltpu.make_async_copy(a, b, sems.at[i])
        for i, (a, b) in enumerate(
            ((elem_hbm, elem_ref), (point_hbm, point_ref), (count_hbm, count_ref))
        )
    ]
    for copy in copies:
        copy.start()
    slab, patch = lax.axis_index("slab"), lax.axis_index("patch")
    last_slab, last_patch = lax.axis_size("slab") - 1, lax.axis_size("patch") - 1
    odd = slab % 2
    even = patch % 2 == 0
    cols, width = state_ref.shape[1], state_ref.shape[2]
    wide = cols + 16
    inside = (slab > 0) & (slab < last_slab)
    col = iota((wide, width), 0)
    valid = (col >= 8) & (col < 8 + cols)
    valid = valid | ((col < 8) & (patch > 0)) | ((col >= 8 + cols) & (patch < last_patch))
    edge = valid.astype(F32)
    keep = edge * inside.astype(F32)
    v_ref[:, 0:8, :] = jnp.zeros((8, 8, width), F32)
    v_ref[:, 8 + cols :, :] = jnp.zeros((8, 8, width), F32)
    r_ref[:, 0:8, :] = jnp.zeros((6, 8, width), F32)
    r_ref[:, 8 + cols :, :] = jnp.zeros((6, 8, width), F32)
    tail = 3 * cols + 8
    strips = {
        0: (one_ref[0:EDGE], three_ref[0:EDGE]),
        1: (inner_ref[tail : tail + EDGE], inner_ref[tail + EDGE : tail + 2 * EDGE]),
        2: (rest_ref[cols : cols + THIN], rest_ref[cols + THIN : cols + 2 * THIN]),
    }
    sides = {}
    for kind, pair in strips.items():
        one, three = (x.astype(F32) for x in pair)
        sides[kind] = (jnp.where(even, three, one), jnp.where(even, one, three))
    lane = iota((1, 128), 1)
    line_ref[...] = jnp.zeros_like(line_ref)
    line_ref[0:2, 0:cols] = scale_ref[...]
    exact = pltpu.roll(line_ref[...], 8, 1)
    table = ((2, 1), (2, 0), (0, 0), (0, 1), (1, 1), (1, 0))
    for r, (kind, i) in enumerate(table):
        if kind == 0:
            row = odd if i == 0 else 1 - odd
            v_ref[r + 1, 8 : 8 + cols, :] = state_ref[row]
            r_ref[r, 8 : 8 + cols, :] = rhs_ref[row]
            line = jnp.where(row == 1, exact[1:2], exact[0:1])
        else:
            if kind == 1:
                value = near_ref[...] if i == 1 else inner_ref[0:cols]
                rhs = inner_ref[2 * cols + 8 : 3 * cols + 8] if i == 1 else inner_ref[cols : 2 * cols]
                ref, below = inner_ref, 2 * cols
            else:
                value = outer_ref[i * cols : (i + 1) * cols]
                rhs = rest_ref[cols + 2 * THIN :] if i == 1 else outer_ref[2 * cols : 3 * cols]
                ref, below = outer_ref, 3 * cols
            v_ref[r + 1, 8 : 8 + cols, :] = value.astype(F32)
            r_ref[r, 8 : 8 + cols, :] = rhs.astype(F32)
            both = ref[below : below + 8, :].astype(F32)[i : i + 1]
            line = both[:, :128] + both[:, 128:]
        for side, start, far in zip(sides[kind], (6, 8 + cols), (5, 10 + cols)):
            v_ref[r + 1, start : start + 2, :] = side[2 * i : 2 * i + 2]
            if i == 0:
                r_ref[r, start : start + 2, :] = side[4:6]
            elif kind < 2:
                r_ref[r, start : start + 2, :] = side[10:12]
            if kind == 0:
                v_ref[r + 1, far : far + 1, :] = side[8 + i : 9 + i]
            both = side[6 + i : 7 + i]
            far = pltpu.roll(both[:, :128] + both[:, 128:], 64, 1)
            here = (lane >= start) & (lane < start + 2)
            line = jnp.where(here, far, line)
        line_ref[r : r + 1, :] = jnp.where(line > 0.0, line, 1.0)
    line_ref[6:8, :] = jnp.ones((2, 128), F32)
    v_ref[0, 8 : 8 + cols, :] = rest_ref[0:cols, :].astype(F32)
    beyond = (slab != 1) & (slab != last_slab - 1)
    v_ref[7, 8 : 8 + cols, :] = relay_ref[...].astype(F32) * beyond.astype(F32)
    for r in range(8):
        v_ref[r] = v_ref[r] * (keep if r < 3 else edge)
    lines = line_ref[...]
    columns = jnp.transpose(lines)
    inverses = jnp.transpose(1.0 / lines)
    for r in range(6):
        s_ref[r] = jnp.broadcast_to(columns[:wide, r : r + 1], (wide, width))
        i_ref[r] = jnp.broadcast_to(inverses[:wide, r : r + 1], (wide, width))
    for sweep in range(SWEEPS):
        a, b = 1 + sweep, 7 - sweep
        value = relaxed(
            v_ref[a:b],
            v_ref[a - 1 : b - 1],
            v_ref[a + 1 : b + 1],
            r_ref[a - 1 : b - 1],
            s_ref[a - 1 : b - 1],
            i_ref[a - 1 : b - 1],
            (matrix_ref, x_ref, y_ref, inverse_ref),
        )
        for j in range(b - a):
            v_ref[a + j] = value[j] * (keep if a + j < 3 else edge)
    out_ref[odd] = v_ref[3, 8 : 8 + cols, :]
    out_ref[1 - odd] = v_ref[4, 8 : 8 + cols, :]
    final = out_ref[...].astype(BF).reshape(2 * cols, width)
    for copy in copies:
        copy.wait()
    elem = elem_ref[0]
    owners = rows_ref.shape[0]
    live, code = slot_codes(point_ref[0], count_ref.at[0], owners)
    hot = ((iota((2 * cols, elem.shape[1]), 0) == elem) & live).astype(F32).astype(BF)
    pull = jnp.dot(nt(tmap_ref[...], final).astype(BF), hot, preferred_element_type=F32)
    for k in range(owners):
        for j in range(4):
            source = code if j == 3 else pull[j : j + 1]
            for h in range(2):
                start = k * 256 + h * 128
                rows_ref[k, 2 * j + h : 2 * j + h + 1, :] = source[:, start : start + 128]
    message_ref[...] = jnp.broadcast_to(rows_ref[...].astype(BF)[None], message_ref.shape)
    part = message_ref.shape[0]
    copies = [
        pltpu.make_async_copy(message_ref, message_hbm.at[i * part : (i + 1) * part], sems.at[3 + i])
        for i in range(message_hbm.shape[0] // part)
    ]
    for copy in copies:
        copy.start()
    for copy in copies:
        copy.wait()


def relaxed(center, up, down, rhs, scale, inverse_scale, matrices):
    matrix_ref, x_ref, y_ref, inverse_ref = matrices
    n, wide, width = center.shape
    flat = (n * wide, width)
    up, mid, down = (x.astype(BF).astype(F32) for x in (up, center, down))
    nx = (up + down).astype(BF)
    ny = (pltpu.roll(mid, 1, 1) + pltpu.roll(mid, wide - 1, 1)).astype(BF)
    own = jnp.dot(mid.astype(BF).reshape(flat), matrix_ref[...], preferred_element_type=F32)
    side = jnp.dot(nx.reshape(flat), x_ref[...], preferred_element_type=F32)
    side += jnp.dot(ny.reshape(flat), y_ref[...], preferred_element_type=F32)
    residue = (rhs.reshape(flat) - (scale.reshape(flat) * own - side)).astype(BF)
    update = jnp.dot(residue, inverse_ref[...], preferred_element_type=F32)
    update = update * inverse_scale.reshape(flat)
    return center + update.reshape(center.shape)


def call(kernel, name, out_shape, operands, scratch=(), in_specs=None, out_specs=None):
    return pl.pallas_call(
        kernel,
        out_shape=out_shape,
        in_specs=in_specs or vmem(len(operands)),
        out_specs=out_specs or jax.tree.map(lambda _: vmem(1)[0], out_shape),
        scratch_shapes=list(scratch),
        compiler_params=params(),
        name=name,
    )(*operands)


def shards(
    fluid_state,
    fluid_rhs,
    element_scale,
    element_matrix,
    couple_x,
    couple_y,
    block_inverse,
    traction_map,
    slot_elem,
    slot_point,
    slot_count,
    displacement,
    stiffness,
):
    cols, width = fluid_state.shape[1:]
    slots = slot_elem.shape[2]
    slabs, owners = lax.axis_size("slab"), lax.axis_size("patch")
    shape = jax.ShapeDtypeStruct
    inner_pairs = [(s, s ^ 1) for s in range(slabs)]
    outer_pairs = [(s, (s + 1) % slabs) for s in range(1, slabs, 2)]
    outer_pairs = outer_pairs + [(b, a) for a, b in outer_pairs]
    strip = shape((EDGE + 8, width), BF)
    row = shape((cols, width), BF)
    near, own, far, to_one, to_three = call(
        near_kernel,
        "near",
        (row, shape((3 * cols + 8, width), BF), row, strip, strip),
        tuple(
            pltpu.with_memory_space_constraint(x, pltpu.HBM)
            for x in (fluid_state, fluid_rhs, element_scale, displacement)
        ),
        [
            pltpu.VMEM(fluid_state.shape, F32),
            pltpu.VMEM(fluid_rhs.shape, F32),
            pltpu.VMEM(element_scale.shape, F32),
            pltpu.VMEM((displacement.shape[0], 16, displacement.shape[2]), F32),
            pltpu.VMEM((8, 128), F32),
            pltpu.VMEM((2, EDGE + 8, width), F32),
            pltpu.SemaphoreType.DMA((5,)),
        ],
        in_specs=hbm(4),
    )
    outer = lax.ppermute(own, "slab", outer_pairs)
    inner_near = lax.ppermute(near, "slab", inner_pairs)
    from_three = lax.ppermute(to_three, "patch", patch_pairs(3))
    from_one = lax.ppermute(to_one, "patch", patch_pairs(1))
    strips = [from_one[:EDGE], from_three[:EDGE]]
    thin = [from_one[:THIN], from_three[:THIN]]
    rest = lax.ppermute(jnp.concatenate([inner_near] + thin + [far]), "slab", outer_pairs)
    others = jnp.concatenate([own[:cols], own[2 * cols :], far] + strips)
    others, _ = lax.optimization_barrier((others, inner_near))
    inner = lax.ppermute(others, "slab", inner_pairs)
    relay = lax.ppermute(outer[:cols], "slab", inner_pairs)
    wide = cols + 16
    state, message = call(
        sweep_kernel,
        "sweep",
        (shape(fluid_state.shape, F32), shape((slabs, owners, 8, 128), BF)),
        (
            fluid_state,
            fluid_rhs,
            element_scale,
            inner_near,
            inner,
            outer,
            rest,
            from_one,
            from_three,
            relay,
            element_matrix,
            couple_x,
            couple_y,
            block_inverse,
            traction_map,
            slot_elem,
            slot_point,
            slot_count,
        ),
        [
            pltpu.VMEM((8, wide, width), F32),
            pltpu.VMEM((6, wide, width), F32),
            pltpu.VMEM((6, wide, width), F32),
            pltpu.VMEM((6, wide, width), F32),
            pltpu.VMEM((8, 128), F32),
            pltpu.VMEM((1, 1, slots), I32),
            pltpu.VMEM((1, 1, slots), I32),
            pltpu.VMEM((1, 1, owners), I32),
            pltpu.VMEM((owners, 8, 128), F32),
            pltpu.VMEM((slabs // 4, owners, 8, 128), BF),
            pltpu.SemaphoreType.DMA((7,)),
        ],
        in_specs=vmem(15) + hbm(3),
        out_specs=tuple(vmem(1) + hbm(1)),
    )
    kd, final = call(
        shell_kernel,
        "shell",
        (shape(displacement.shape, F32), shape(state.shape, F32)),
        (from_one[EDGE:], from_three[EDGE:], displacement, stiffness, state),
        [pltpu.VMEM((3, displacement.shape[1] + 16, 128), F32)] * 2 + [pltpu.SemaphoreType.DMA],
        out_specs=tuple(vmem(1) + hbm(1)),
    )
    new, wall = exchange_and_relax(message, displacement, stiffness, kd)
    return final, new, wall


def solution(mesh):
    return jax.shard_map(
        shards,
        mesh=mesh,
        in_specs=(
            P("slab", "patch", None),
            P("slab", "patch", None),
            P("slab", "patch"),
            P(),
            P(),
            P(),
            P(),
            P(),
            P("slab", "patch", None),
            P("slab", "patch", None),
            P("slab", "patch", None),
            P(None, "patch", None),
            P("patch", None),
        ),
        out_specs=(
            P("slab", "patch", None),
            P(None, "patch", None),
            P(None, "slab", "patch", None),
        ),
        check_vma=False,
    )
```

```python
import jax
import jax.numpy as jnp
from jax import lax
from jax.experimental import pallas as pl
from jax.experimental.pallas import tpu as pltpu
from jax.sharding import PartitionSpec as P

SWEEPS = 3
BF = jnp.bfloat16
F32 = jnp.float32
I32 = jnp.int32
LIMIT = 48 << 20
EDGE = 16
THIN = 8


def vmem(n):
    return [pl.BlockSpec(memory_space=pltpu.VMEM)] * n


def hbm(n):
    return [pl.BlockSpec(memory_space=pltpu.HBM)] * n


def iota(shape, dim):
    return lax.broadcasted_iota(I32, shape, dim)


def nt(a, b):
    return lax.dot_general(a, b, (((1,), (1,)), ((), ())), preferred_element_type=F32)


def slot_codes(point, count_ref, owners):
    slots = point.shape[1]
    cap = slots // owners
    slot = iota((1, slots), 1)
    owner = slot // cap
    limit = jnp.zeros((1, slots), I32)
    for k in range(owners):
        limit = jnp.where(owner == k, count_ref[0:1, k : k + 1], limit)
    live = (slot - owner * cap) < limit
    row = point // 128
    code = (128 + (point - row * 128)).astype(F32)
    for b in range(6):
        code = code * jnp.where((row >> b) & 1 == 1, F32(2.0 ** (2**b)), F32(1.0))
    return live, jnp.where(live, code, 0.0)


def decode(code):
    row = jnp.zeros(code.shape, F32)
    for b in (5, 4, 3, 2, 1, 0):
        big = code >= F32(128.0 * 2.0 ** (2**b))
        row = row + jnp.where(big, F32(2**b), 0.0)
        code = code * jnp.where(big, F32(2.0 ** -(2**b)), 1.0)
    return row, code - 128.0


def owner_kernel(got_ref, disp_ref, stiff_ref, kd_ref, new_ref, r0, r1, r2, r3, pick_ref):
    sources = got_ref.shape[0]
    rows = disp_ref.shape[1]
    patch = lax.axis_index("patch")
    first = lax.axis_index("slab") * 4
    row_ids = iota((rows, 128), 0).astype(F32).astype(BF)
    lane_ids = iota((128, 128), 0).astype(F32).astype(BF)
    none = jnp.zeros((rows, 128), BF)
    ones, zeros = jnp.ones((128, 128), BF), jnp.zeros((128, 128), BF)
    total = jnp.zeros((3 * rows, 128), F32)
    group = 8
    for base in range(0, sources, group):
        codes = [decode(got_ref[base : base + group, 6 + h, :].astype(F32)) for h in range(2)]
        row8 = [row.astype(BF) for row, _ in codes]
        lane8 = [lane.astype(BF) for _, lane in codes]
        for g in range(group):
            vals = got_ref[base + g]
            left, right = [], []
            for h in range(2):
                mask = row_ids == row8[h][g : g + 1]
                left.append(
                    jnp.concatenate(
                        [jnp.where(mask, vals[2 * c + h : 2 * c + h + 1], none) for c in range(3)],
                        axis=0,
                    )
                )
                right.append(jnp.where(lane_ids == lane8[h][g : g + 1], ones, zeros))
            total += nt(jnp.concatenate(left, axis=1), jnp.concatenate(right, axis=1))
    loads = total.reshape(3, rows, 128)
    new = disp_ref[...] + (loads - kd_ref[...]) / (36.0 * stiff_ref[...])[None]
    new_ref[...] = new
    flat = new.reshape(3 * rows, 128)
    high = flat.astype(BF)
    low = (flat - high.astype(F32)).astype(BF)
    both = jnp.concatenate([high, low], axis=0)
    for d in range(4):
        for h in range(2):
            code = got_ref[pl.ds(first + (patch ^ d), 1), 6 + h, :]
            pick_ref[2 * d + h : 2 * d + h + 1, :] = code.astype(F32)
    row, lane = decode(pick_ref[...])
    wide_ids = iota((rows, 256), 0).astype(F32)
    for d, reply in enumerate((r0, r1, r2, r3)):
        at = 2 * d
        hot = jnp.concatenate(
            [
                jnp.where(lane_ids == lane[at + h : at + h + 1].astype(BF), ones, zeros)
                for h in range(2)
            ],
            axis=1,
        )
        picked = jnp.dot(both, hot, preferred_element_type=F32)
        mask = wide_ids == jnp.concatenate([row[at : at + 1], row[at + 1 : at + 2]], axis=1)
        for c in range(3):
            part = picked[c * rows : (c + 1) * rows] + picked[(c + 3) * rows : (c + 4) * rows]
            reply[c : c + 1, :] = jnp.where(mask, part, 0.0).sum(axis=0, keepdims=True)


def store_kernel(value_ref, out_ref, sem):
    copy = pltpu.make_async_copy(value_ref, out_ref, sem)
    copy.start()
    copy.wait()


def store(value, name):
    return pl.pallas_call(
        store_kernel,
        out_shape=jax.ShapeDtypeStruct(value.shape, value.dtype),
        in_specs=vmem(1),
        out_specs=hbm(1)[0],
        scratch_shapes=[pltpu.SemaphoreType.DMA],
        compiler_params=params(),
        name=name,
    )(value)


def finish_kernel(r3, r2, r1, r0, out_ref):
    cap = r0.shape[1]
    patch = lax.axis_index("patch")
    for d, reply in enumerate((r0, r1, r2, r3)):
        start = pl.multiple_of((patch ^ d) * cap, cap)
        for c in range(3):
            out_ref[c, 0, :, pl.ds(start, cap)] = reply[c : c + 1, :]


def shell_kernel(
    one_ref, three_ref, disp_ref, stiff_ref, state_ref, kd_ref, out_ref, field_ref, bend_ref, sem
):
    copy = pltpu.make_async_copy(state_ref, out_ref, sem)
    copy.start()
    rows = disp_ref.shape[1]
    patch = lax.axis_index("patch")
    top = patch > 0
    bottom = patch < 3
    even = patch % 2 == 0
    one, three = (
        ref[:, :128].astype(F32) + ref[:, 128:].astype(F32)
        for ref in (one_ref, three_ref)
    )
    above = jnp.where(even, three, one)
    below = jnp.where(even, one, three)
    field_ref[...] = jnp.zeros_like(field_ref)
    bend_ref[...] = jnp.zeros_like(bend_ref)
    field_ref[:, 8 : 8 + rows, :] = disp_ref[...]
    lane = iota((1, 1, 128), 2)

    def sides(x):
        left = jnp.where(lane == 0, 0.0, pltpu.roll(x, 1, 2))
        right = jnp.where(lane == 127, 0.0, pltpu.roll(x, 127, 2))
        return left + right

    for c in range(3):
        field_ref[c, 6:8, :] = jnp.where(top, above[2 * c : 2 * c + 2], 0.0)
        field_ref[c, 8 + rows : 10 + rows, :] = jnp.where(bottom, below[2 * c : 2 * c + 2], 0.0)
    mid = field_ref[:, 7 : 9 + rows, :]
    bend = 4.0 * mid - (
        field_ref[:, 6 : 8 + rows, :] + field_ref[:, 8 : 10 + rows, :] + sides(mid)
    )
    bend_ref[:, 7 : 9 + rows, :] = bend
    for c in range(3):
        bend_ref[c, 7:8, :] = jnp.where(top, bend_ref[c, 7:8, :], 0.0)
        bend_ref[c, 8 + rows : 9 + rows, :] = jnp.where(
            bottom, bend_ref[c, 8 + rows : 9 + rows, :], 0.0
        )
    mid = bend_ref[:, 8 : 8 + rows, :]
    again = 4.0 * mid - (
        bend_ref[:, 7 : 7 + rows, :] + bend_ref[:, 9 : 9 + rows, :] + sides(mid)
    )
    kd_ref[...] = stiff_ref[...][None] * (again + 4.0 * mid)
    copy.wait()


def params():
    return pltpu.CompilerParams(vmem_limit_bytes=LIMIT)


def patch_pairs(d):
    return [(p, p ^ d) for p in range(4)]


def exchange_and_relax(message, displacement, stiffness, kd):
    slabs, owners = lax.axis_size("slab"), lax.axis_size("patch")
    rows = displacement.shape[1]
    sources = slabs * owners
    got = lax.all_to_all(
        message.reshape(sources, 8, 128), ("slab", "patch"), 0, 0, tiled=True
    )
    reply = jax.ShapeDtypeStruct((8, 256), F32)
    new, *replies = pl.pallas_call(
        owner_kernel,
        out_shape=(jax.ShapeDtypeStruct(displacement.shape, F32),) + (reply,) * 4,
        in_specs=vmem(4),
        out_specs=vmem(5),
        scratch_shapes=[pltpu.VMEM((8, 128), F32)],
        compiler_params=params(),
        name="owner",
    )(got, displacement, stiffness, kd)
    back = [lax.ppermute(replies[d], "patch", patch_pairs(d)) for d in (3, 2, 1)]
    back.append(replies[0])
    wall = pl.pallas_call(
        finish_kernel,
        out_shape=jax.ShapeDtypeStruct((3, 1, 1, owners * 256), F32),
        in_specs=vmem(4),
        out_specs=pl.BlockSpec(memory_space=pltpu.VMEM),
        compiler_params=params(),
        name="finish",
    )(*back)
    return store(new, "store_shell"), wall


def halves(value):
    high = value.astype(BF)
    low = (value - high.astype(F32)).astype(BF)
    return jnp.concatenate([high.astype(F32), low.astype(F32)], axis=1)


def lines_of(scale_ref, pad_ref):
    pad_ref[...] = jnp.zeros_like(pad_ref)
    pad_ref[0:2, 0 : scale_ref.shape[1]] = scale_ref[...]
    return pltpu.roll(pad_ref[...], 8, 1)


def near_kernel(
    state_hbm, rhs_hbm, scale_hbm, disp_hbm, near_ref, own_ref, far_ref, one_ref, three_ref,
    state_ref, rhs_ref, scale_ref, disp_ref, pad_ref, build_ref, sems,
):
    rows = disp_hbm.shape[1]
    copies = [
        pltpu.make_async_copy(a, b, sems.at[i])
        for i, (a, b) in enumerate(
            (
                (scale_hbm, scale_ref),
                (state_hbm, state_ref),
                (rhs_hbm, rhs_ref),
                (disp_hbm.at[:, 0:8], disp_ref.at[:, 0:8]),
                (disp_hbm.at[:, rows - 8 : rows], disp_ref.at[:, 8:16]),
            )
        )
    ]
    for copy in copies:
        copy.start()
    odd = lax.axis_index("slab") % 2
    even = lax.axis_index("patch") % 2 == 0
    cols = state_ref.shape[1]
    for e in range(2):
        build_ref[e] = jnp.zeros((EDGE + 8, 256), F32)
    copies[0].wait()
    lines = lines_of(scale_ref, pad_ref)
    flip = odd == 1
    first = jnp.where(flip, lines[1:2], lines[0:1])
    second = jnp.where(flip, lines[0:1], lines[1:2])
    pair = jnp.concatenate([halves(first), halves(second), jnp.zeros((6, 256), F32)], axis=0)
    own_ref[3 * cols :, :] = pair.astype(BF)
    for e in range(2):
        build_ref[e, 6:8, :] = pair[0:2]
    copies[1].wait()
    copies[2].wait()
    for i, row in enumerate((odd, 1 - odd)):
        for part, ref, at, third in (
            (0, state_ref, 2 * i, 8 + i),
            (2, rhs_ref, (4, 10)[i], None),
        ):
            value = ref[row]
            block = part + i
            if block == 3:
                far_ref[...] = value.astype(BF)
            else:
                own_ref[block * cols : (block + 1) * cols, :] = value.astype(BF)
            low, high = value[0:2], value[cols - 2 : cols]
            build_ref[0, at : at + 2, :] = jnp.where(even, high, low)
            build_ref[1, at : at + 2, :] = jnp.where(even, low, high)
            if third is not None:
                low, high = value[2:3], value[cols - 3 : cols - 2]
                build_ref[0, third : third + 1, :] = jnp.where(even, high, low)
                build_ref[1, third : third + 1, :] = jnp.where(even, low, high)
    near_ref[...] = state_ref[1 - odd].astype(BF)
    copies[3].wait()
    copies[4].wait()
    for c in range(3):
        top = halves(disp_ref[c, 0:2, :])
        bottom = halves(disp_ref[c, 14:16, :])
        at = EDGE + 2 * c
        build_ref[0, at : at + 2, :] = jnp.where(even, bottom, top)
        build_ref[1, at : at + 2, :] = jnp.where(even, top, bottom)
    one_ref[...] = build_ref[0].astype(BF)
    three_ref[...] = build_ref[1].astype(BF)


def sweep_kernel(
    state_ref,
    rhs_ref,
    scale_ref,
    near_ref,
    inner_ref,
    outer_ref,
    rest_ref,
    one_ref,
    three_ref,
    relay_ref,
    matrix_ref,
    x_ref,
    y_ref,
    inverse_ref,
    tmap_ref,
    elem_hbm,
    point_hbm,
    count_hbm,
    out_ref,
    message_hbm,
    v_ref,
    r_ref,
    s_ref,
    i_ref,
    line_ref,
    elem_ref,
    point_ref,
    count_ref,
    rows_ref,
    message_ref,
    sems,
):
    copies = [
        pltpu.make_async_copy(a, b, sems.at[i])
        for i, (a, b) in enumerate(
            ((elem_hbm, elem_ref), (point_hbm, point_ref), (count_hbm, count_ref))
        )
    ]
    for copy in copies:
        copy.start()
    slab, patch = lax.axis_index("slab"), lax.axis_index("patch")
    last_slab, last_patch = lax.axis_size("slab") - 1, lax.axis_size("patch") - 1
    odd = slab % 2
    even = patch % 2 == 0
    cols, width = state_ref.shape[1], state_ref.shape[2]
    wide = cols + 16
    inside = (slab > 0) & (slab < last_slab)
    col = iota((wide, width), 0)
    valid = (col >= 8) & (col < 8 + cols)
    valid = valid | ((col < 8) & (patch > 0)) | ((col >= 8 + cols) & (patch < last_patch))
    edge = valid.astype(F32)
    keep = edge * inside.astype(F32)
    v_ref[:, 0:8, :] = jnp.zeros((8, 8, width), F32)
    v_ref[:, 8 + cols :, :] = jnp.zeros((8, 8, width), F32)
    r_ref[:, 0:8, :] = jnp.zeros((6, 8, width), F32)
    r_ref[:, 8 + cols :, :] = jnp.zeros((6, 8, width), F32)
    tail = 3 * cols + 8
    strips = {
        0: (one_ref[0:EDGE], three_ref[0:EDGE]),
        1: (inner_ref[tail : tail + EDGE], inner_ref[tail + EDGE : tail + 2 * EDGE]),
        2: (rest_ref[cols : cols + THIN], rest_ref[cols + THIN : cols + 2 * THIN]),
    }
    sides = {}
    for kind, pair in strips.items():
        one, three = (x.astype(F32) for x in pair)
        sides[kind] = (jnp.where(even, three, one), jnp.where(even, one, three))
    lane = iota((1, 128), 1)
    line_ref[...] = jnp.zeros_like(line_ref)
    line_ref[0:2, 0:cols] = scale_ref[...]
    exact = pltpu.roll(line_ref[...], 8, 1)
    table = ((2, 1), (2, 0), (0, 0), (0, 1), (1, 1), (1, 0))
    for r, (kind, i) in enumerate(table):
        if kind == 0:
            row = odd if i == 0 else 1 - odd
            v_ref[r + 1, 8 : 8 + cols, :] = state_ref[row]
            r_ref[r, 8 : 8 + cols, :] = rhs_ref[row]
            line = jnp.where(row == 1, exact[1:2], exact[0:1])
        else:
            if kind == 1:
                value = near_ref[...] if i == 1 else inner_ref[0:cols]
                rhs = inner_ref[2 * cols + 8 : 3 * cols + 8] if i == 1 else inner_ref[cols : 2 * cols]
                ref, below = inner_ref, 2 * cols
            else:
                value = outer_ref[i * cols : (i + 1) * cols]
                rhs = rest_ref[cols + 2 * THIN :] if i == 1 else outer_ref[2 * cols : 3 * cols]
                ref, below = outer_ref, 3 * cols
            v_ref[r + 1, 8 : 8 + cols, :] = value.astype(F32)
            r_ref[r, 8 : 8 + cols, :] = rhs.astype(F32)
            both = ref[below : below + 8, :].astype(F32)[i : i + 1]
            line = both[:, :128] + both[:, 128:]
        for side, start, far in zip(sides[kind], (6, 8 + cols), (5, 10 + cols)):
            v_ref[r + 1, start : start + 2, :] = side[2 * i : 2 * i + 2]
            if i == 0:
                r_ref[r, start : start + 2, :] = side[4:6]
            elif kind < 2:
                r_ref[r, start : start + 2, :] = side[10:12]
            if kind == 0:
                v_ref[r + 1, far : far + 1, :] = side[8 + i : 9 + i]
            both = side[6 + i : 7 + i]
            far = pltpu.roll(both[:, :128] + both[:, 128:], 64, 1)
            here = (lane >= start) & (lane < start + 2)
            line = jnp.where(here, far, line)
        line_ref[r : r + 1, :] = jnp.where(line > 0.0, line, 1.0)
    line_ref[6:8, :] = jnp.ones((2, 128), F32)
    v_ref[0, 8 : 8 + cols, :] = rest_ref[0:cols, :].astype(F32)
    beyond = (slab != 1) & (slab != last_slab - 1)
    v_ref[7, 8 : 8 + cols, :] = relay_ref[...].astype(F32) * beyond.astype(F32)
    for r in range(8):
        v_ref[r] = v_ref[r] * (keep if r < 3 else edge)
    lines = line_ref[...]
    columns = jnp.transpose(lines)
    inverses = jnp.transpose(1.0 / lines)
    for r in range(6):
        s_ref[r] = jnp.broadcast_to(columns[:wide, r : r + 1], (wide, width))
        i_ref[r] = jnp.broadcast_to(inverses[:wide, r : r + 1], (wide, width))
    for sweep in range(SWEEPS):
        a, b = 1 + sweep, 7 - sweep
        value = relaxed(
            v_ref[a:b],
            v_ref[a - 1 : b - 1],
            v_ref[a + 1 : b + 1],
            r_ref[a - 1 : b - 1],
            s_ref[a - 1 : b - 1],
            i_ref[a - 1 : b - 1],
            (matrix_ref, x_ref, y_ref, inverse_ref),
        )
        for j in range(b - a):
            v_ref[a + j] = value[j] * (keep if a + j < 3 else edge)
    out_ref[odd] = v_ref[3, 8 : 8 + cols, :]
    out_ref[1 - odd] = v_ref[4, 8 : 8 + cols, :]
    final = out_ref[...].astype(BF).reshape(2 * cols, width)
    for copy in copies:
        copy.wait()
    elem = elem_ref[0]
    owners = rows_ref.shape[0]
    live, code = slot_codes(point_ref[0], count_ref.at[0], owners)
    chosen = jnp.where(live, elem, -1).astype(F32).astype(BF)
    place = iota((2 * cols, elem.shape[1]), 0).astype(F32).astype(BF)
    hot = jnp.where(place == chosen, jnp.ones(place.shape, BF), jnp.zeros(place.shape, BF))
    pull = jnp.dot(nt(tmap_ref[...], final).astype(BF), hot, preferred_element_type=F32)
    for k in range(owners):
        for j in range(4):
            source = code if j == 3 else pull[j : j + 1]
            for h in range(2):
                start = k * 256 + h * 128
                rows_ref[k, 2 * j + h : 2 * j + h + 1, :] = source[:, start : start + 128]
    message_ref[...] = jnp.broadcast_to(rows_ref[...].astype(BF)[None], message_ref.shape)
    part = message_ref.shape[0]
    copies = [
        pltpu.make_async_copy(message_ref, message_hbm.at[i * part : (i + 1) * part], sems.at[3 + i])
        for i in range(message_hbm.shape[0] // part)
    ]
    for copy in copies:
        copy.start()
    for copy in copies:
        copy.wait()


def relaxed(center, up, down, rhs, scale, inverse_scale, matrices):
    matrix_ref, x_ref, y_ref, inverse_ref = matrices
    n, wide, width = center.shape
    flat = (n * wide, width)
    up, mid, down = (x.astype(BF).astype(F32) for x in (up, center, down))
    nx = (up + down).astype(BF)
    ny = (pltpu.roll(mid, 1, 1) + pltpu.roll(mid, wide - 1, 1)).astype(BF)
    own = jnp.dot(mid.astype(BF).reshape(flat), matrix_ref[...], preferred_element_type=F32)
    both = jnp.concatenate([nx.reshape(flat), ny.reshape(flat)], axis=1)
    couple = jnp.concatenate([x_ref[...], y_ref[...]], axis=0)
    side = jnp.dot(both, couple, preferred_element_type=F32)
    residue = (rhs.reshape(flat) - (scale.reshape(flat) * own - side)).astype(BF)
    update = jnp.dot(residue, inverse_ref[...], preferred_element_type=F32)
    update = update * inverse_scale.reshape(flat)
    return center + update.reshape(center.shape)


def call(kernel, name, out_shape, operands, scratch=(), in_specs=None, out_specs=None):
    return pl.pallas_call(
        kernel,
        out_shape=out_shape,
        in_specs=in_specs or vmem(len(operands)),
        out_specs=out_specs or jax.tree.map(lambda _: vmem(1)[0], out_shape),
        scratch_shapes=list(scratch),
        compiler_params=params(),
        name=name,
    )(*operands)


def shards(
    fluid_state,
    fluid_rhs,
    element_scale,
    element_matrix,
    couple_x,
    couple_y,
    block_inverse,
    traction_map,
    slot_elem,
    slot_point,
    slot_count,
    displacement,
    stiffness,
):
    cols, width = fluid_state.shape[1:]
    slots = slot_elem.shape[2]
    slabs, owners = lax.axis_size("slab"), lax.axis_size("patch")
    shape = jax.ShapeDtypeStruct
    inner_pairs = [(s, s ^ 1) for s in range(slabs)]
    outer_pairs = [(s, (s + 1) % slabs) for s in range(1, slabs, 2)]
    outer_pairs = outer_pairs + [(b, a) for a, b in outer_pairs]
    strip = shape((EDGE + 8, width), BF)
    row = shape((cols, width), BF)
    near, own, far, to_one, to_three = call(
        near_kernel,
        "near",
        (row, shape((3 * cols + 8, width), BF), row, strip, strip),
        tuple(
            pltpu.with_memory_space_constraint(x, pltpu.HBM)
            for x in (fluid_state, fluid_rhs, element_scale, displacement)
        ),
        [
            pltpu.VMEM(fluid_state.shape, F32),
            pltpu.VMEM(fluid_rhs.shape, F32),
            pltpu.VMEM(element_scale.shape, F32),
            pltpu.VMEM((displacement.shape[0], 16, displacement.shape[2]), F32),
            pltpu.VMEM((8, 128), F32),
            pltpu.VMEM((2, EDGE + 8, width), F32),
            pltpu.SemaphoreType.DMA((5,)),
        ],
        in_specs=hbm(4),
    )
    outer = lax.ppermute(own, "slab", outer_pairs)
    inner_near = lax.ppermute(near, "slab", inner_pairs)
    from_three = lax.ppermute(to_three, "patch", patch_pairs(3))
    from_one = lax.ppermute(to_one, "patch", patch_pairs(1))
    strips = [from_one[:EDGE], from_three[:EDGE]]
    thin = [from_one[:THIN], from_three[:THIN]]
    rest = lax.ppermute(jnp.concatenate([inner_near] + thin + [far]), "slab", outer_pairs)
    others = jnp.concatenate([own[:cols], own[2 * cols :], far] + strips)
    others, _ = lax.optimization_barrier((others, inner_near))
    inner = lax.ppermute(others, "slab", inner_pairs)
    relay = lax.ppermute(outer[:cols], "slab", inner_pairs)
    wide = cols + 16
    state, message = call(
        sweep_kernel,
        "sweep",
        (shape(fluid_state.shape, F32), shape((slabs, owners, 8, 128), BF)),
        (
            fluid_state,
            fluid_rhs,
            element_scale,
            inner_near,
            inner,
            outer,
            rest,
            from_one,
            from_three,
            relay,
            element_matrix,
            couple_x,
            couple_y,
            block_inverse,
            traction_map,
            slot_elem,
            slot_point,
            slot_count,
        ),
        [
            pltpu.VMEM((8, wide, width), F32),
            pltpu.VMEM((6, wide, width), F32),
            pltpu.VMEM((6, wide, width), F32),
            pltpu.VMEM((6, wide, width), F32),
            pltpu.VMEM((8, 128), F32),
            pltpu.VMEM((1, 1, slots), I32),
            pltpu.VMEM((1, 1, slots), I32),
            pltpu.VMEM((1, 1, owners), I32),
            pltpu.VMEM((owners, 8, 128), F32),
            pltpu.VMEM((slabs // 4, owners, 8, 128), BF),
            pltpu.SemaphoreType.DMA((7,)),
        ],
        in_specs=vmem(15) + hbm(3),
        out_specs=tuple(vmem(1) + hbm(1)),
    )
    kd, final = call(
        shell_kernel,
        "shell",
        (shape(displacement.shape, F32), shape(state.shape, F32)),
        (from_one[EDGE:], from_three[EDGE:], displacement, stiffness, state),
        [pltpu.VMEM((3, displacement.shape[1] + 16, 128), F32)] * 2 + [pltpu.SemaphoreType.DMA],
        out_specs=tuple(vmem(1) + hbm(1)),
    )
    new, wall = exchange_and_relax(message, displacement, stiffness, kd)
    return final, new, wall


def solution(mesh):
    return jax.shard_map(
        shards,
        mesh=mesh,
        in_specs=(
            P("slab", "patch", None),
            P("slab", "patch", None),
            P("slab", "patch"),
            P(),
            P(),
            P(),
            P(),
            P(),
            P("slab", "patch", None),
            P("slab", "patch", None),
            P("slab", "patch", None),
            P(None, "patch", None),
            P("patch", None),
        ),
        out_specs=(
            P("slab", "patch", None),
            P(None, "patch", None),
            P(None, "slab", "patch", None),
        ),
        check_vma=False,
    )
```
